32 devices in a mesh: seq: 8 (over z, y), head: 4 (over x, core).
Axes of the slice: x: 2, y: 2, z: 4, core: 2. Of those that a mesh axis runs over, the one named last changes fastest.
Arguments:
- queries: bfloat16 [4096, 4096], P('seq', 'head'), may hold values from -6 to 6
- keys: bfloat16 [4096, 4096], P('seq', 'head'), may hold values from -6 to 6
- values: bfloat16 [4096, 4096], P('seq', 'head'), may hold values from -6 to 6
- level_weights: float32 [5, 32, 4096], P(None, 'head', 'seq'), may hold values from 0.1 to 3, as said below
- norm_gain: float32 [4096], P('head'), may hold values from 0.25 to 1.75
Outputs:
- mixed: bfloat16 [4096, 4096], P('seq', 'head')
The draws below stay inside these ranges and needn't reach their ends.
Inputs may be any that keep to these rules, and one draw needn't show every extreme that they name: `level_weights`: positive level weights.
All inputs are finite; a program needn't handle non-finite values.
Results may differ from the reference program's by a relative error of at most 0.0049.
Values may be sent and summed in bfloat16 or wider, within the bound.
No kernel may reach another device: no remote copies, remote signals or barrier semaphores. Data moves between devices by JAX's collectives and lax.ppermute only.
A program may use at most 64 MiB of HBM per device.

```python
import math
import jax
import jax.numpy as jnp
from jax import lax

HEADS = 32
HEAD_DIM = 128
STRETCH = 256
D = 4096
TOKENS = 4096
LOCAL_BITS = 1
SEQ_BITS = 3
LEVELS = 5


def draw_level_weights(key, part):
    head_place = jnp.arange(HEADS, dtype=jnp.float32)[None, :, None]
    head_ramp = head_place / (HEADS - 1)
    base_draw = jnp.exp(jax.random.uniform(key, (LEVELS, HEADS, TOKENS), jnp.float32, math.log(0.1), 0.0))
    factor = 1.0 + 2.0 * head_ramp
    return base_draw * factor


def shard_levels(rng, dims, cuts, least, largest):
    factor_of, own = 1.0, jax.random.fold_in(rng, 6)
    for position, parts in cuts:
        heights = jnp.exp(jax.random.uniform(jax.random.fold_in(own, position), (parts,), jnp.float32, least / len(cuts), largest / len(cuts)))
        factor_of = factor_of * jnp.repeat(heights, dims[position] // parts).reshape([-1 if axis == position else 1 for axis in range(len(dims))])
    return factor_of


def gaussian(rng, dims, spread, limit, cuts=(), kind=jnp.bfloat16):
    result = spread * jax.random.normal(rng, dims, jnp.float32)
    if cuts:
        result = result * shard_levels(rng, dims, cuts, -0.22, 0.18)
    return jnp.clip(result, -limit, limit).astype(kind)


def setup_inputs(seed: int = 0) -> dict:
    seeds = jax.random.split(jax.random.key(seed), 6)
    return {
        "queries": gaussian(seeds[0], (TOKENS, D), 1.0, 6.0, ((0, 8), (1, 4))),
        "keys": gaussian(seeds[1], (TOKENS, D), 1.0, 6.0, ((0, 8), (1, 4))),
        "values": gaussian(seeds[2], (TOKENS, D), 1.0, 6.0, ((0, 8), (1, 4))),
        "level_weights": draw_level_weights(jax.random.fold_in(seeds[5], 71), 0),
        "norm_gain": jnp.clip(1.0 + 0.15 * jax.random.normal(seeds[4], (D,), jnp.float32), 0.25, 1.75),
    }


EPSILON = 1e-06
PRECISION_TOP = lax.Precision.HIGHEST

def one_head(pieces):
    query_h, key_h, value_h, weight_h = pieces
    groups_total = TOKENS // STRETCH
    query_block_list = query_h.astype(jnp.float32).reshape(groups_total, STRETCH, HEAD_DIM)
    key_blocks = key_h.astype(jnp.float32).reshape(groups_total, STRETCH, HEAD_DIM)
    value_blocks = value_h.astype(jnp.float32).reshape(groups_total, STRETCH, HEAD_DIM)
    states = jnp.einsum('ctk,ctv->ckv', key_blocks, value_blocks, precision=PRECISION_TOP)
    scores = jnp.einsum('ctk,csk->cts', query_block_list, key_blocks, precision=PRECISION_TOP)
    causal = lax.broadcasted_iota(jnp.int32, (STRETCH, STRETCH), 0) >= lax.broadcasted_iota(jnp.int32, (STRETCH, STRETCH), 1)
    attn_probs = jnp.where(causal[None], scores, jnp.zeros_like(scores)).astype(jnp.bfloat16)
    attn_probs = lax.optimization_barrier(attn_probs).astype(jnp.float32)
    intra_out = jnp.einsum('cts,csv->ctv', attn_probs, value_blocks, precision=PRECISION_TOP)
    combined = weight_h[0].reshape(groups_total, STRETCH)[:, :, None] * intra_out
    running = states
    for level_bit in range(LOCAL_BITS + SEQ_BITS):
        groups = running.shape[0] // 2
        block_span = 2 ** level_bit
        halves = running.reshape(groups, 2, HEAD_DIM, HEAD_DIM)
        leftward_sum = lax.optimization_barrier(halves[:, 0].astype(jnp.bfloat16)).astype(jnp.float32)
        rightward_queries = query_block_list.reshape(groups, 2, block_span * STRETCH, HEAD_DIM)[:, 1]
        state_readout = jnp.einsum('yag,ygq->yaq', rightward_queries, leftward_sum, precision=PRECISION_TOP)
        level_weight = weight_h[1 + level_bit].reshape(groups, 2, block_span * STRETCH)[:, 1]
        contrib = level_weight[:, :, None] * state_readout
        padded = jnp.stack([jnp.zeros_like(contrib), contrib], axis=1)
        combined = combined + padded.reshape(groups_total, STRETCH, HEAD_DIM)
        running = halves[:, 0] + halves[:, 1]
    return combined.reshape(TOKENS, HEAD_DIM)

def reference(queries, keys, values, level_weights, norm_gain):
    query_heads = queries.reshape(TOKENS, HEADS, HEAD_DIM).transpose(1, 0, 2)
    key_heads = keys.reshape(TOKENS, HEADS, HEAD_DIM).transpose(1, 0, 2)
    value_heads = values.reshape(TOKENS, HEADS, HEAD_DIM).transpose(1, 0, 2)
    weight_heads = level_weights.transpose(1, 0, 2)
    per_head = lax.map(one_head, (query_heads, key_heads, value_heads, weight_heads))
    attended = per_head.transpose(1, 0, 2).reshape(TOKENS, D)
    mean_square = lax.optimization_barrier(jnp.mean(attended * attended, axis=1, keepdims=True))
    mixed = attended * lax.rsqrt(mean_square + EPSILON) * norm_gain.astype(jnp.float32)[None, :]
    return mixed.astype(jnp.bfloat16)
```

```python
import functools

import jax
import jax.numpy as jnp
from jax import lax
from jax.experimental import pallas as pl
from jax.experimental.pallas import tpu as pltpu
from jax.sharding import PartitionSpec as P

HEAD_DIM = 128
STRETCH = 256
EPSILON = 1e-06
QUAD = 4
F32 = jnp.float32
BF16 = jnp.bfloat16
VMEM = pl.BlockSpec(memory_space=pltpu.VMEM)
SMEM = pl.BlockSpec(memory_space=pltpu.SMEM)
ANY = pl.BlockSpec(memory_space=pl.ANY)
GRANT = 24 << 20


def params():
    return pltpu.CompilerParams(vmem_limit_bytes=GRANT)


def cost(flops, moved):
    return pl.CostEstimate(flops=flops, bytes_accessed=moved, transcendentals=0)


def exchanged(block, axis, mask):
    count = lax.axis_size(axis)
    return lax.ppermute(block, axis, [(i, i ^ mask) for i in range(count)])


def nn(a, b):
    return jnp.dot(a, b, preferred_element_type=F32)


def nt(a, b):
    return lax.dot_general(a, b, (((1,), (1,)), ((), ())), preferred_element_type=F32)


def tn(a, b):
    return lax.dot_general(a, b, (((0,), (0,)), ((), ())), preferred_element_type=F32)


def column(head):
    return pl.ds(head * HEAD_DIM, HEAD_DIM)


def states_kernel(group, place_ref, k_hbm, v_hbm, own_ref, one_ref, two_ref, three_ref, rest_ref, k_buf, v_buf, sems):
    width = group * HEAD_DIM
    place = place_ref[0]
    order = (1, 3, 2, 0)
    copies = []
    for slot, r in enumerate(order):
        cols = pl.ds(pl.multiple_of((place ^ r) * width, width), width)
        pair = (
            pltpu.make_async_copy(k_hbm.at[:, cols], k_buf.at[slot], sems.at[0, slot]),
            pltpu.make_async_copy(v_hbm.at[:, cols], v_buf.at[slot], sems.at[1, slot]),
        )
        for copy in pair:
            copy.start()
        copies.append(pair)
    sent = {1: one_ref, 2: two_ref, 3: three_ref}
    spot = {0: 0, 3: 1, 2: 2}
    for slot, r in enumerate(order):
        for copy in copies[slot]:
            copy.wait()
        for j in range(group):
            state = tn(k_buf[slot, :, column(j)], v_buf[slot, :, column(j)])
            if r == 0:
                own_ref[j] = state
            else:
                sent[r][j] = state.astype(BF16)
            if r in spot:
                rest_ref[spot[r] * group + j] = state.astype(BF16)


def intra_kernel(group, q_ref, k_ref, v_ref, w_ref, out_ref):
    rows = q_ref.shape[0]
    heads = QUAD * group
    base = pl.program_id(0) * group
    causal = lax.broadcasted_iota(jnp.int32, (STRETCH, STRETCH), 0) >= lax.broadcasted_iota(
        jnp.int32, (STRETCH, STRETCH), 1
    )
    local_bits = (rows // STRETCH).bit_length() - 1
    weights = [jnp.transpose(w_ref[level, 0], (1, 0)) for level in range(1 + local_bits)]
    for j in range(group):
        states = []
        for c in range(rows // STRETCH):
            here = pl.ds(c * STRETCH, STRETCH)
            q, k, v = (ref[here, column(j)] for ref in (q_ref, k_ref, v_ref))
            probs = jnp.where(causal, nt(q, k), 0.0).astype(BF16)
            total = weights[0][c * STRETCH : (c + 1) * STRETCH, j : j + 1] * nn(probs, v)
            for bit in range(local_bits):
                if c >> bit & 1:
                    low = (c >> bit + 1) << bit + 1
                    left = functools.reduce(jnp.add, states[low : low + (1 << bit)])
                    scale = weights[1 + bit][c * STRETCH : (c + 1) * STRETCH, j : j + 1]
                    total += scale * nn(q, left.astype(BF16))
            out_ref[here, column(j)] = total
            if c + 1 < rows // STRETCH:
                states.append(tn(k, v))
    del heads, base


def readout(group, place, q_ref, w_list, total_ref, r, blocks):
    width = group * HEAD_DIM
    start = pl.multiple_of((place ^ r) * width, width)
    first = (place ^ r) * group
    return width, start, first


def far_kernel(group, bits, place_ref, q_ref, w_ref, *refs):
    n = len(bits)
    state_refs, total_ref, out_ref = refs[: QUAD * n], refs[QUAD * n], refs[QUAD * n + 1]
    place = place_ref[0]
    for r in range(QUAD):
        for j in range(group):
            head = (place & (QUAD - 1) ^ r) * group + j
            cols = pl.ds(pl.multiple_of(head * HEAD_DIM, HEAD_DIM), HEAD_DIM)
            q = q_ref[:, cols]
            total = total_ref[:, cols]
            for i, bit in enumerate(bits):
                row = w_ref[i, pl.ds(head, 1), :]
                row = jnp.where(place >> bit & 1 == 1, row, 0.0)
                scale = jnp.transpose(jnp.broadcast_to(row, (8, row.shape[1])), (1, 0))[:, :1]
                total += scale * nn(q, state_refs[QUAD * i + r][j])
            out_ref[:, cols] = total


def last_kernel(group, bits, place_ref, q_ref, w_ref, *refs):
    n = len(bits)
    state_refs = refs[:QUAD]
    total_ref, out_ref, sq_ref = refs[QUAD:]
    place = place_ref[0]
    squares = jnp.zeros((q_ref.shape[0], HEAD_DIM), F32)
    for r in range(QUAD):
        for j in range(group):
            head = (place & (QUAD - 1) ^ r) * group + j
            cols = pl.ds(pl.multiple_of(head * HEAD_DIM, HEAD_DIM), HEAD_DIM)
            q = q_ref[:, cols]
            total = total_ref[:, cols]
            for i, bit in enumerate(bits):
                row = w_ref[i, pl.ds(head, 1), :]
                row = jnp.where(place >> bit & 1 == 1, row, 0.0)
                scale = jnp.transpose(jnp.broadcast_to(row, (8, row.shape[1])), (1, 0))[:, :1]
                total += scale * nn(q, state_refs[r][i * group + j])
            out_ref[:, cols] = total
            squares += total * total
    sq_ref[...] = jnp.sum(jnp.transpose(squares, (1, 0)), axis=0, keepdims=True)


def norm_kernel(width, x_ref, sq_ref, gain_ref, out_hbm, buf, sems):
    rows = x_ref.shape[0]
    step = rows // sems.shape[0]
    inverse = lax.rsqrt(sq_ref[...] / width + EPSILON)
    scale = jnp.transpose(jnp.broadcast_to(inverse, (8, rows)), (1, 0))[:, :1]
    gain = gain_ref[...]
    copies = []
    for i in range(rows // step):
        here = pl.ds(i * step, step)
        buf[here, :] = (x_ref[here, :] * scale[i * step : (i + 1) * step] * gain).astype(BF16)
        copies.append(pltpu.make_async_copy(buf.at[here, :], out_hbm.at[here, :], sems.at[i]))
        copies[-1].start()
    for copy in copies:
        copy.wait()


def local(queries, keys, values, level_weights, norm_gain):
    rows, width = queries.shape
    heads = width // HEAD_DIM
    group = heads // QUAD
    levels = level_weights.shape[0]
    local_bits = (rows // STRETCH).bit_length() - 1
    seq_bits = lax.axis_size("seq").bit_length() - 1
    full_width = width * lax.axis_size("head")
    position = lax.axis_index("seq").astype(jnp.int32)
    place = (position & (QUAD - 1)).reshape(1)
    whole = position.reshape(1)
    block = (group, HEAD_DIM, HEAD_DIM)
    sds = jax.ShapeDtypeStruct

    own, one, two, three, rest = pl.pallas_call(
        functools.partial(states_kernel, group),
        out_shape=(sds(block, F32), sds(block, BF16), sds(block, BF16), sds(block, BF16), sds((3 * group,) + block[1:], BF16)),
        in_specs=[SMEM, ANY, ANY],
        out_specs=(VMEM,) * 5,
        scratch_shapes=[
            pltpu.VMEM((QUAD, rows, group * HEAD_DIM), BF16),
            pltpu.VMEM((QUAD, rows, group * HEAD_DIM), BF16),
            pltpu.SemaphoreType.DMA((2, QUAD)),
        ],
        compiler_params=params(),
        cost_estimate=cost(2 * rows * width * HEAD_DIM, 4 * rows * width),
        name="states",
    )(place, keys, values)

    got1, got2, got3 = exchanged(one, "seq", 1), exchanged(two, "seq", 2), exchanged(three, "seq", 3)

    weights4 = level_weights.reshape(levels, QUAD, group, rows)
    total = pl.pallas_call(
        functools.partial(intra_kernel, group),
        grid=(QUAD,),
        out_shape=sds((rows, width), F32),
        in_specs=[pl.BlockSpec((rows, group * HEAD_DIM), lambda i: (0, i))] * 3
        + [pl.BlockSpec((1 + local_bits, 1, group, rows), lambda i: (0, i, 0, 0))],
        out_specs=pl.BlockSpec((rows, group * HEAD_DIM), lambda i: (0, i)),
        compiler_params=params(),
        cost_estimate=cost(6 * rows * STRETCH * width, 10 * rows * width),
        name="intra",
    )(queries, keys, values, weights4)

    pair = own + got1.astype(F32)
    other = got2.astype(F32) + got3.astype(F32)
    running = pair + other
    left_pair = jnp.where(position >> 1 & 1 == 1, other, pair).astype(BF16)
    upper = []
    for bit in range(2, seq_bits):
        came = exchanged(running.astype(BF16), "seq", 1 << bit)
        upper.append(came)
        running = running + came.astype(F32)
    rest_got = exchanged(rest, "seq", 1)
    near = [got1] + [rest_got[i * group : (i + 1) * group] for i in range(3)]
    middle = [left_pair] + [exchanged(left_pair, "seq", r) for r in range(1, QUAD)]
    top = jnp.concatenate(upper, axis=0) if len(upper) > 1 else upper[0]
    tops = [top] + [exchanged(top, "seq", r) for r in range(1, QUAD)]

    first = 1 + local_bits
    total = pl.pallas_call(
        functools.partial(far_kernel, group, (0, 1)),
        out_shape=sds((rows, width), F32),
        in_specs=[SMEM] + [VMEM] * (2 + 2 * QUAD + 1),
        out_specs=VMEM,
        input_output_aliases={3 + 2 * QUAD: 0},
        compiler_params=params(),
        cost_estimate=cost(4 * rows * width * HEAD_DIM, 8 * rows * width),
        name="far",
    )(whole, queries, level_weights[first : first + 2], *near, *middle, total)

    total, squares = pl.pallas_call(
        functools.partial(last_kernel, group, tuple(range(2, seq_bits))),
        out_shape=(sds((rows, width), F32), sds((1, rows), F32)),
        in_specs=[SMEM] + [VMEM] * (2 + QUAD + 1),
        out_specs=(VMEM, VMEM),
        input_output_aliases={3 + QUAD: 0},
        compiler_params=params(),
        cost_estimate=cost(2 * (seq_bits - 2) * rows * width * HEAD_DIM, 8 * rows * width),
        name="last",
    )(whole, queries, level_weights[first + 2 :], *tops, total)

    mask = 1
    while mask < lax.axis_size("head"):
        squares = squares + exchanged(squares, "head", mask)
        mask *= 2

    return pl.pallas_call(
        functools.partial(norm_kernel, full_width),
        out_shape=sds((rows, width), BF16),
        in_specs=[VMEM] * 3,
        out_specs=ANY,
        scratch_shapes=[pltpu.VMEM((rows, width), BF16), pltpu.SemaphoreType.DMA((4,))],
        compiler_params=params(),
        cost_estimate=cost(2 * rows * width, 2 * rows * width),
        name="norm",
    )(total, squares, norm_gain.reshape(1, width))


def solution(mesh):
    return jax.shard_map(
        local,
        mesh=mesh,
        in_specs=(P("seq", "head"), P("seq", "head"), P("seq", "head"), P(None, "head", "seq"), P("head")),
        out_specs=P("seq", "head"),
        check_vma=False,
    )
```

```python
import functools

import jax
import jax.numpy as jnp
from jax import lax
from jax.experimental import pallas as pl
from jax.experimental.pallas import tpu as pltpu
from jax.sharding import PartitionSpec as P


HEAD_DIM = 128
STRETCH = 256
EPSILON = 1e-06
QUAD = 4
F32 = jnp.float32
BF16 = jnp.bfloat16
VMEM = pl.BlockSpec(memory_space=pltpu.VMEM)
SMEM = pl.BlockSpec(memory_space=pltpu.SMEM)
ANY = pl.BlockSpec(memory_space=pl.ANY)
HBM = pl.BlockSpec(memory_space=pltpu.HBM)
GRANT = 24 << 20
STATES_GRANT = 51968 << 10


def params(grant=GRANT):
    return pltpu.CompilerParams(vmem_limit_bytes=grant)


def cost(flops, moved):
    return pl.CostEstimate(flops=flops, bytes_accessed=moved, transcendentals=0)


def exchanged(block, axis, mask):
    count = lax.axis_size(axis)
    return lax.ppermute(block, axis, [(i, i ^ mask) for i in range(count)])


def nt(a, b):
    return lax.dot_general(a, b, (((1,), (1,)), ((), ())), preferred_element_type=F32)


def tn(a, b):
    return lax.dot_general(a, b, (((0,), (0,)), ((), ())), preferred_element_type=F32)


def column(head):
    return pl.ds(head * HEAD_DIM, HEAD_DIM)


def states_kernel(group, place_ref, k_hbm, v_hbm, k_ref, v_ref, own_ref, one_ref, two_ref, three_ref, rest_ref, sems):
    width = group * HEAD_DIM
    place = place_ref[0] & (QUAD - 1)
    order = (3, 1, 2, 0)
    copies = {}
    for r in order:
        cols = pl.ds(pl.multiple_of((place ^ r) * width, width), width)
        copies[r] = (
            pltpu.make_async_copy(k_hbm.at[:, cols], k_ref.at[r], sems.at[0, r]),
            pltpu.make_async_copy(v_hbm.at[:, cols], v_ref.at[r], sems.at[1, r]),
        )
        for copy in copies[r]:
            copy.start()
    sent = {1: one_ref, 2: two_ref, 3: three_ref}
    spot = {0: 0, 3: 1, 2: 2}
    for r in order:
        for copy in copies[r]:
            copy.wait()
        for j in range(group):
            state = tn(v_ref[r, :, column(j)], k_ref[r, :, column(j)])
            if r == 0:
                own_ref[j] = state
            else:
                sent[r][j] = state.astype(BF16)
            if r in spot:
                rest_ref[spot[r] * group + j] = state.astype(BF16)


def intra_kernel(group, groups, place_ref, q_ref, k_ref, v_ref, w_ref, out_ref):
    count = q_ref.shape[0] // STRETCH
    local_bits = count.bit_length() - 1
    place = place_ref[0] & (QUAD - 1)
    causal = lax.broadcasted_iota(jnp.int32, (STRETCH, STRETCH), 0) <= lax.broadcasted_iota(
        jnp.int32, (STRETCH, STRETCH), 1
    )
    for at, r in enumerate(groups):
        for j in range(group):
            head = (place ^ r) * group + j
            cols = pl.ds(pl.multiple_of(head * HEAD_DIM, HEAD_DIM), HEAD_DIM)
            states = []
            for c in range(count):
                here = slice(c * STRETCH, (c + 1) * STRETCH)
                q, k, v = q_ref[here, cols], k_ref[r, here, column(j)], v_ref[r, here, column(j)]
                probs = jnp.where(causal, nt(k, q), 0.0).astype(BF16)
                total = w_ref[0, pl.ds(head, 1), here] * tn(v, probs)
                for bit in range(local_bits):
                    if c >> bit & 1:
                        low = (c >> bit + 1) << bit + 1
                        left = functools.reduce(jnp.add, states[low : low + (1 << bit)])
                        total += w_ref[1 + bit, pl.ds(head, 1), here] * nt(left.astype(BF16), q)
                out_ref[at, column(j), here] = total
                if c + 1 < count:
                    states.append(tn(v, k))


def weight_of(w_ref, level, head, place, bit):
    return jnp.where(place >> bit & 1 == 1, w_ref[level, pl.ds(head, 1), :], 0.0)


def far_kernel(group, first, bits, place_ref, q_ref, w_ref, *refs):
    n = len(bits)
    state_refs, total_refs, out_refs = refs[: 2 * n], refs[2 * n : 2 * n + 2], refs[2 * n + 2 :]
    place = place_ref[0]
    for r in range(QUAD):
        for j in range(group):
            head = (place & (QUAD - 1) ^ r) * group + j
            q = q_ref[:, pl.ds(pl.multiple_of(head * HEAD_DIM, HEAD_DIM), HEAD_DIM)]
            total = total_refs[r // 2][r % 2, column(j), :]
            for i, bit in enumerate(bits):
                state = state_refs[2 * i][j] if r == 0 else state_refs[2 * i + 1][(r - 1) * group + j]
                total += weight_of(w_ref, first + bit, head, place, bit) * nt(state, q)
            out_refs[r // 2][r % 2, column(j), :] = total


def last_kernel(group, first, bits, place_ref, q_ref, w_ref, *refs):
    state_refs, total_refs, out_refs, sq_ref = refs[:QUAD], refs[QUAD : QUAD + 2], refs[QUAD + 2 : QUAD + 4], refs[QUAD + 4]
    place = place_ref[0]
    squares = jnp.zeros(sq_ref.shape, F32)
    for r in range(QUAD):
        for j in range(group):
            head = (place & (QUAD - 1) ^ r) * group + j
            q = q_ref[:, pl.ds(pl.multiple_of(head * HEAD_DIM, HEAD_DIM), HEAD_DIM)]
            total = total_refs[r // 2][r % 2, column(j), :]
            for i, bit in enumerate(bits):
                total += weight_of(w_ref, first + bit, head, place, bit) * nt(state_refs[r][i * group + j], q)
            out_refs[r // 2][r % 2, column(j), :] = total
            squares += jnp.sum(total * total, axis=0, keepdims=True)
    sq_ref[...] = squares


def norm_kernel(group, full_width, place_ref, a_ref, b_ref, sq_ref, gain_ref, out_hbm, buf, sems):
    width = group * HEAD_DIM
    place = place_ref[0] & (QUAD - 1)
    scale = lax.rsqrt(sq_ref[...] / full_width + EPSILON)
    copies = []
    for r in range(QUAD):
        cols = pl.ds(pl.multiple_of((place ^ r) * width, width), width)
        x = jnp.transpose((a_ref, b_ref)[r // 2][r % 2] * scale, (1, 0))
        buf[r] = (x * gain_ref[:, cols]).astype(BF16)
        copies.append(pltpu.make_async_copy(buf.at[r], out_hbm.at[:, cols], sems.at[r]))
        copies[-1].start()
    for copy in copies:
        copy.wait()


def local(queries, keys, values, level_weights, norm_gain):
    rows, width = queries.shape
    group = width // HEAD_DIM // QUAD
    local_bits = (rows // STRETCH).bit_length() - 1
    seq_bits = lax.axis_size("seq").bit_length() - 1
    full_width = width * lax.axis_size("head")
    position = lax.axis_index("seq").astype(jnp.int32)
    place = position.reshape(1)
    block = (group, HEAD_DIM, HEAD_DIM)
    others = (3 * group, HEAD_DIM, HEAD_DIM)
    panel = (QUAD, rows, group * HEAD_DIM)
    half = jax.ShapeDtypeStruct((2, group * HEAD_DIM, rows), F32)
    sds = jax.ShapeDtypeStruct

    k_here, v_here, own, one, two, three, rest = pl.pallas_call(
        functools.partial(states_kernel, group),
        out_shape=(sds(panel, BF16), sds(panel, BF16), sds(block, F32), sds(block, BF16), sds(block, BF16), sds(block, BF16), sds(others, BF16)),
        in_specs=[SMEM, HBM, HBM],
        out_specs=(VMEM,) * 7,
        scratch_shapes=[pltpu.SemaphoreType.DMA((2, QUAD))],
        compiler_params=params(STATES_GRANT),
        cost_estimate=cost(2 * rows * width * HEAD_DIM, 4 * rows * width),
        name="states",
    )(place, keys, values)

    got3 = exchanged(three, "seq", 3)
    got1 = exchanged(one, "seq", 1)
    got2 = exchanged(two, "seq", 2)
    near = exchanged(rest, "seq", 1)

    totals = []
    for groups in ((0, 1), (2, 3)):
        totals.append(
            pl.pallas_call(
                functools.partial(intra_kernel, group, groups),
                out_shape=half,
                in_specs=[SMEM] + [VMEM] * 4,
                out_specs=VMEM,
                compiler_params=params(),
                cost_estimate=cost(3 * rows * STRETCH * width, 2 * rows * width),
                name="intra",
            )(place, queries, k_here, v_here, level_weights)
        )

    pair = own + got1.astype(F32)
    other = got2.astype(F32) + got3.astype(F32)
    running = pair + other
    upper = []
    for bit in range(2, seq_bits):
        came = exchanged(running.astype(BF16), "seq", 1 << bit)
        upper.append(came)
        running = running + came.astype(F32)
    top = jnp.concatenate(upper, axis=0) if len(upper) > 1 else upper[0]
    gathered = {r: exchanged(top, "seq", r) for r in (3, 1, 2)}
    tops = [top] + [gathered[r] for r in (1, 2, 3)]

    sums = [
        three.astype(F32) + near[2 * group :].astype(F32),
        pair,
        one.astype(F32) + near[:group].astype(F32),
    ]
    middle = exchanged(jnp.concatenate(sums, axis=0).astype(BF16), "seq", 2)

    first = 1 + local_bits
    totals = pl.pallas_call(
        functools.partial(far_kernel, group, first, (0, 1)),
        out_shape=(half, half),
        in_specs=[SMEM] + [VMEM] * 8,
        out_specs=(VMEM, VMEM),
        input_output_aliases={7: 0, 8: 1},
        compiler_params=params(),
        cost_estimate=cost(4 * rows * width * HEAD_DIM, 8 * rows * width),
        name="far",
    )(place, queries, level_weights, got1, near, other.astype(BF16), middle, *totals)

    *totals, squares = pl.pallas_call(
        functools.partial(last_kernel, group, first, tuple(range(2, seq_bits))),
        out_shape=(half, half, sds((1, rows), F32)),
        in_specs=[SMEM] + [VMEM] * (2 + QUAD + 2),
        out_specs=(VMEM, VMEM, VMEM),
        input_output_aliases={3 + QUAD: 0, 4 + QUAD: 1},
        compiler_params=params(),
        cost_estimate=cost(2 * (seq_bits - 2) * rows * width * HEAD_DIM, 8 * rows * width),
        name="last",
    )(place, queries, level_weights, *tops, *totals)

    mask = 1
    while mask < lax.axis_size("head"):
        squares = squares + exchanged(squares, "head", mask)
        mask *= 2

    return pl.pallas_call(
        functools.partial(norm_kernel, group, full_width),
        out_shape=sds((rows, width), BF16),
        in_specs=[SMEM] + [VMEM] * 4,
        out_specs=ANY,
        scratch_shapes=[pltpu.VMEM(panel, BF16), pltpu.SemaphoreType.DMA((QUAD,))],
        compiler_params=params(),
        cost_estimate=cost(2 * rows * width, 2 * rows * width),
        name="norm",
    )(place, *totals, squares, norm_gain.reshape(1, width))


def solution(mesh):
    return jax.shard_map(
        local,
        mesh=mesh,
        in_specs=(P("seq", "head"), P("seq", "head"), P("seq", "head"), P(None, "head", "seq"), P("head")),
        out_specs=P("seq", "head"),
        check_vma=False,
    )
```

```python
import functools

import jax
import jax.numpy as jnp
from jax import lax
from jax.experimental import pallas as pl
from jax.experimental.pallas import tpu as pltpu
from jax.sharding import PartitionSpec as P


HEAD_DIM = 128
STRETCH = 256
EPSILON = 1e-06
QUAD = 4
F32 = jnp.float32
BF16 = jnp.bfloat16
VMEM = pl.BlockSpec(memory_space=pltpu.VMEM)
SMEM = pl.BlockSpec(memory_space=pltpu.SMEM)
ANY = pl.BlockSpec(memory_space=pl.ANY)
HBM = pl.BlockSpec(memory_space=pltpu.HBM)
GRANT = 24 << 20
TILE = 256
STATES_GRANT = 52992 << 10
OWN_GRANT = 53248 << 10


def params(grant=GRANT):
    return pltpu.CompilerParams(vmem_limit_bytes=grant)


def cost(flops, moved):
    return pl.CostEstimate(flops=flops, bytes_accessed=moved, transcendentals=0)


def exchanged(block, axis, mask):
    count = lax.axis_size(axis)
    return lax.ppermute(block, axis, [(i, i ^ mask) for i in range(count)])


def nt(a, b):
    return lax.dot_general(a, b, (((1,), (1,)), ((), ())), preferred_element_type=F32)


def tn(a, b):
    return lax.dot_general(a, b, (((0,), (0,)), ((), ())), preferred_element_type=F32)


def column(head):
    return pl.ds(head * HEAD_DIM, HEAD_DIM)


def states_of(group, groups, place, k_hbm, v_hbm, k_ref, v_ref, sems, use):
    width = group * HEAD_DIM
    copies = []
    for at, r in enumerate(groups):
        cols = pl.ds(pl.multiple_of((place ^ r) * width, width), width)
        copies.append(
            (
                pltpu.make_async_copy(k_hbm.at[:, cols], k_ref.at[at], sems.at[0, at]),
                pltpu.make_async_copy(v_hbm.at[:, cols], v_ref.at[at], sems.at[1, at]),
            )
        )
        for copy in copies[-1]:
            copy.start()
    for at, r in enumerate(groups):
        for copy in copies[at]:
            copy.wait()
        for j in range(group):
            use(r, j, tn(v_ref[at, :, column(j)], k_ref[at, :, column(j)]))


def sent_kernel(group, groups, place_ref, k_hbm, v_hbm, k_ref, v_ref, *refs):
    sent = dict(zip(groups, refs))

    def use(r, j, state):
        sent[r][j] = state.astype(BF16)

    states_of(group, groups, place_ref[0] & (QUAD - 1), k_hbm, v_hbm, k_ref, v_ref, refs[-1], use)


def own_kernel(group, place_ref, k_hbm, v_hbm, gain_hbm, three_ref, two_ref, k_ref, v_ref, gain_ref, own_ref, rest_ref, sems, gain_sem):
    gain = pltpu.make_async_copy(gain_hbm, gain_ref, gain_sem)
    gain.start()
    rest_ref[group : 2 * group] = three_ref[...]
    rest_ref[2 * group :] = two_ref[...]

    def use(r, j, state):
        own_ref[j] = state
        rest_ref[j] = state.astype(BF16)

    states_of(group, (0,), place_ref[0] & (QUAD - 1), k_hbm, v_hbm, k_ref, v_ref, sems, use)
    gain.wait()


def intra_kernel(group, work, place_ref, q_ref, w_ref, *refs):
    n = len(work)
    sources, out_refs = refs[:-n], refs[-n:]
    count = q_ref.shape[0] // STRETCH
    local_bits = count.bit_length() - 1
    place = place_ref[0] & (QUAD - 1)
    causal = lax.broadcasted_iota(jnp.int32, (STRETCH, STRETCH), 0) <= lax.broadcasted_iota(
        jnp.int32, (STRETCH, STRETCH), 1
    )
    for (r, source, slot), out_ref in zip(work, out_refs):
        k_ref, v_ref = sources[2 * source : 2 * source + 2]
        for j in range(group):
            head = (place ^ r) * group + j
            cols = pl.ds(pl.multiple_of(head * HEAD_DIM, HEAD_DIM), HEAD_DIM)
            states = []
            for c in range(count):
                here = slice(c * STRETCH, (c + 1) * STRETCH)
                q, k, v = q_ref[here, cols], k_ref[slot, here, column(j)], v_ref[slot, here, column(j)]
                probs = jnp.where(causal, nt(k, q), 0.0).astype(BF16)
                total = w_ref[0, pl.ds(head, 1), here] * tn(v, probs)
                for bit in range(local_bits):
                    if c >> bit & 1:
                        low = (c >> bit + 1) << bit + 1
                        left = functools.reduce(jnp.add, states[low : low + (1 << bit)])
                        total += w_ref[1 + bit, pl.ds(head, 1), here] * nt(left.astype(BF16), q)
                out_ref[column(j), here] = total
                if c + 1 < count:
                    states.append(tn(v, k))


def readout_kernel(group, first, work, n_states, carry, finish, place_ref, q_ref, w_ref, *refs):
    n = len(work)
    state_refs, total_refs, refs = refs[:n_states], refs[n_states : n_states + n], refs[n_states + n :]
    carried_ref = refs[0] if carry else None
    out_refs, squares_ref = refs[carry : carry + n], refs[carry + n]
    rows = q_ref.shape[0]
    place = place_ref[0]
    for t in range(0, rows, TILE):
        here = slice(t, t + TILE)
        squares = carried_ref[:, here] if carry else jnp.zeros((8, TILE), F32)
        for (r, complete, reads), total_ref, out_ref in zip(work, total_refs, out_refs):
            for j in range(group):
                head = (place & (QUAD - 1) ^ r) * group + j
                q = q_ref[here, pl.ds(pl.multiple_of(head * HEAD_DIM, HEAD_DIM), HEAD_DIM)]
                total = total_ref[column(j), here]
                for bit, ref, slot in reads:
                    row = w_ref[first + bit, pl.ds(head, 1), here]
                    row = jnp.where(place >> bit & 1 == 1, row, 0.0)
                    total += row * nt(state_refs[ref][slot + j], q)
                out_ref[column(j), here] = total
                if complete:
                    squares += jnp.sum((total * total).reshape(HEAD_DIM // 8, 8, TILE), axis=0)
        squares_ref[:, here] = jnp.sum(squares, axis=0, keepdims=True) if finish else squares


def norm_kernel(group, full_width, place_ref, *refs):
    total_refs, (sq_ref, gain_ref, out_hbm, buf, sems) = refs[:QUAD], refs[QUAD:]
    width = group * HEAD_DIM
    place = place_ref[0] & (QUAD - 1)
    scale = lax.rsqrt(sq_ref[...] / full_width + EPSILON)
    copies = []
    for r in range(QUAD):
        cols = pl.ds(pl.multiple_of((place ^ r) * width, width), width)
        x = jnp.transpose(total_refs[r][...] * scale, (1, 0))
        buf[r] = (x * gain_ref[:, cols]).astype(BF16)
        copies.append(pltpu.make_async_copy(buf.at[r], out_hbm.at[:, cols], sems.at[r]))
        copies[-1].start()
    for copy in copies:
        copy.wait()


def local(queries, keys, values, level_weights, norm_gain):
    rows, width = queries.shape
    group = width // HEAD_DIM // QUAD
    local_bits = (rows // STRETCH).bit_length() - 1
    seq_bits = lax.axis_size("seq").bit_length() - 1
    full_width = width * lax.axis_size("head")
    position = lax.axis_index("seq").astype(jnp.int32)
    place = position.reshape(1)
    sds = jax.ShapeDtypeStruct
    block = (group, HEAD_DIM, HEAD_DIM)
    others = (3 * group, HEAD_DIM, HEAD_DIM)
    panel = (rows, group * HEAD_DIM)
    part = sds((group * HEAD_DIM, rows), F32)

    groups = (3, 1, 2)
    k_sent, v_sent, three, one, two = pl.pallas_call(
        functools.partial(sent_kernel, group, groups),
        out_shape=(sds((3,) + panel, BF16),) * 2 + (sds(block, BF16),) * 3,
        in_specs=[SMEM, HBM, HBM],
        out_specs=(VMEM,) * 5,
        scratch_shapes=[pltpu.SemaphoreType.DMA((2, 3))],
        compiler_params=params(STATES_GRANT),
        cost_estimate=cost(3 * rows * width * HEAD_DIM // 2, 3 * rows * width),
        name="sent",
    )(place, keys, values)

    got3 = exchanged(three, "seq", 3)
    got1 = exchanged(one, "seq", 1)
    got2 = exchanged(two, "seq", 2)

    k_own, v_own, gain, own, rest = pl.pallas_call(
        functools.partial(own_kernel, group),
        out_shape=(sds((1,) + panel, BF16),) * 2 + (sds((1, width), F32), sds(block, F32), sds(others, BF16)),
        in_specs=[SMEM, HBM, HBM, HBM, VMEM, VMEM],
        out_specs=(VMEM,) * 5,
        scratch_shapes=[pltpu.SemaphoreType.DMA((2, 1)), pltpu.SemaphoreType.DMA],
        compiler_params=params(OWN_GRANT),
        cost_estimate=cost(rows * width * HEAD_DIM // 2, rows * width),
        name="own",
    )(place, keys, values, norm_gain.reshape(1, width), three, two)
    near = exchanged(rest, "seq", 1)

    totals = {}
    for work, sources in (
        (((3, 0, 0), (1, 0, 1)), (k_sent, v_sent)),
        (((2, 0, 2), (0, 1, 0)), (k_sent, v_sent, k_own, v_own)),
    ):
        outs = pl.pallas_call(
            functools.partial(intra_kernel, group, work),
            out_shape=(part,) * len(work),
            in_specs=[SMEM] + [VMEM] * (2 + len(sources)),
            out_specs=(VMEM,) * len(work),
            compiler_params=params(),
            cost_estimate=cost(3 * rows * STRETCH * width, 2 * rows * width),
            name="intra",
        )(place, queries, level_weights, *sources)
        totals |= {r: out for (r, _, _), out in zip(work, outs)}

    pair = own + got1.astype(F32)
    other = got2.astype(F32) + got3.astype(F32)
    running = pair + other
    upper = []
    for bit in range(2, seq_bits):
        came = exchanged(running.astype(BF16), "seq", 1 << bit)
        upper.append(came)
        running = running + came.astype(F32)
    top = jnp.concatenate(upper, axis=0) if len(upper) > 1 else upper[0]
    tops = {0: top} | {r: exchanged(top, "seq", r) for r in (3, 1, 2)}

    sums = [
        three.astype(F32) + near[2 * group :].astype(F32),
        pair,
        one.astype(F32) + near[:group].astype(F32),
    ]
    middle = exchanged(jnp.concatenate(sums, axis=0).astype(BF16), "seq", 2)

    def top_reads(ref):
        return tuple((bit, ref, (bit - 2) * group) for bit in range(2, seq_bits))

    def readout(work, states, squares, finish=False):
        n, carry = len(work), squares is not None
        kernel = functools.partial(readout_kernel, group, 1 + local_bits, work, len(states), carry, finish)
        ins = [place, queries, level_weights, *states, *(totals[r] for r, _, _ in work)] + [squares] * carry
        shapes = [part] * n + [sds((1 if finish else 8, rows), F32)]
        outs = pl.pallas_call(
            kernel,
            out_shape=tuple(shapes),
            in_specs=[SMEM] + [VMEM] * (len(ins) - 1),
            out_specs=(VMEM,) * len(shapes),
            compiler_params=params(),
            cost_estimate=cost(n * rows * width * HEAD_DIM, 2 * n * rows * width),
        )(*ins)
        totals.update({r: out for (r, _, _), out in zip(work, outs)})
        return outs[n]

    below = {0: ((0, 0, 0), (1, 2, 0))} | {r: ((0, 1, (r - 1) * group), (1, 3, (r - 1) * group)) for r in (1, 2, 3)}
    work = tuple((r, r == 0, below[r] + (top_reads(4) if r == 0 else ())) for r in (3, 1, 2, 0))
    squares = readout(work, (got1, near, other.astype(BF16), middle, top), None)
    squares = readout(((3, True, top_reads(0)), (1, True, top_reads(1))), (tops[3], tops[1]), squares)
    squares = readout(((2, True, top_reads(0)),), (tops[2],), squares, finish=True)

    mask = 1
    while mask < lax.axis_size("head"):
        squares = squares + exchanged(squares, "head", mask)
        mask *= 2

    return pl.pallas_call(
        functools.partial(norm_kernel, group, full_width),
        out_shape=sds((rows, width), BF16),
        in_specs=[SMEM] + [VMEM] * (QUAD + 2),
        out_specs=ANY,
        scratch_shapes=[pltpu.VMEM((QUAD,) + panel, BF16), pltpu.SemaphoreType.DMA((QUAD,))],
        compiler_params=params(),
        cost_estimate=cost(2 * rows * width, 2 * rows * width),
        name="norm",
    )(place, *(totals[r] for r in range(QUAD)), squares, gain)


def solution(mesh):
    return jax.shard_map(
        local,
        mesh=mesh,
        in_specs=(P("seq", "head"), P("seq", "head"), P("seq", "head"), P(None, "head", "seq"), P("head")),
        out_specs=P("seq", "head"),
        check_vma=False,
    )
```

```python
import functools

import jax
import jax.numpy as jnp
from jax import lax
from jax.experimental import pallas as pl
from jax.experimental.pallas import tpu as pltpu
from jax.sharding import PartitionSpec as P


HEAD_DIM = 128
STRETCH = 256
EPSILON = 1e-06
QUAD = 4
F32 = jnp.float32
BF16 = jnp.bfloat16
VMEM = pl.BlockSpec(memory_space=pltpu.VMEM)
SMEM = pl.BlockSpec(memory_space=pltpu.SMEM)
ANY = pl.BlockSpec(memory_space=pl.ANY)
HBM = pl.BlockSpec(memory_space=pltpu.HBM)
GRANT = 24 << 20
TILE = 256
STATES_GRANT = 52992 << 10
OWN_GRANT = 53248 << 10


def params(grant=GRANT):
    return pltpu.CompilerParams(vmem_limit_bytes=grant)


def cost(flops, moved):
    return pl.CostEstimate(flops=flops, bytes_accessed=moved, transcendentals=0)


def exchanged(block, axis, mask, lowest=0):
    count = lax.axis_size(axis)
    return lax.ppermute(block, axis, [(i, i ^ mask) for i in range(lowest, count)])


def nt(a, b):
    return lax.dot_general(a, b, (((1,), (1,)), ((), ())), preferred_element_type=F32)


def tn(a, b):
    return lax.dot_general(a, b, (((0,), (0,)), ((), ())), preferred_element_type=F32)


def column(head):
    return pl.ds(head * HEAD_DIM, HEAD_DIM)


def states_of(group, groups, place, k_hbm, v_hbm, k_ref, v_ref, sems, use):
    width = group * HEAD_DIM
    copies = []
    for at, r in enumerate(groups):
        cols = pl.ds(pl.multiple_of((place ^ r) * width, width), width)
        copies.append(
            (
                pltpu.make_async_copy(k_hbm.at[:, cols], k_ref.at[at], sems.at[0, at]),
                pltpu.make_async_copy(v_hbm.at[:, cols], v_ref.at[at], sems.at[1, at]),
            )
        )
        for copy in copies[-1]:
            copy.start()
    for at, r in enumerate(groups):
        for copy in copies[at]:
            copy.wait()
        for j in range(group):
            use(r, j, tn(v_ref[at, :, column(j)], k_ref[at, :, column(j)]))


def sent_kernel(group, groups, place_ref, k_hbm, v_hbm, k_ref, v_ref, *refs):
    sent = dict(zip(groups, refs))

    def use(r, j, state):
        sent[r][j] = state.astype(BF16)

    states_of(group, groups, place_ref[0] & (QUAD - 1), k_hbm, v_hbm, k_ref, v_ref, refs[-1], use)


def own_kernel(group, place_ref, k_hbm, v_hbm, gain_hbm, three_ref, two_ref, k_ref, v_ref, gain_ref, own_ref, rest_ref, sems, gain_sem):
    gain = pltpu.make_async_copy(gain_hbm, gain_ref, gain_sem)
    gain.start()
    rest_ref[group : 2 * group] = three_ref[...]
    rest_ref[2 * group :] = two_ref[...]

    def use(r, j, state):
        own_ref[j] = state
        rest_ref[j] = state.astype(BF16)

    states_of(group, (0,), place_ref[0] & (QUAD - 1), k_hbm, v_hbm, k_ref, v_ref, sems, use)
    gain.wait()


def intra_kernel(group, work, place_ref, q_ref, w_ref, *refs):
    n = len(work)
    sources, out_refs = refs[:-n], refs[-n:]
    count = q_ref.shape[0] // STRETCH
    local_bits = count.bit_length() - 1
    place = place_ref[0] & (QUAD - 1)
    causal = lax.broadcasted_iota(jnp.int32, (STRETCH, STRETCH), 0) <= lax.broadcasted_iota(
        jnp.int32, (STRETCH, STRETCH), 1
    )
    for (r, source, slot), out_ref in zip(work, out_refs):
        k_ref, v_ref = sources[2 * source : 2 * source + 2]
        for j in range(group):
            head = (place ^ r) * group + j
            cols = pl.ds(pl.multiple_of(head * HEAD_DIM, HEAD_DIM), HEAD_DIM)
            states = []
            for c in range(count):
                here = slice(c * STRETCH, (c + 1) * STRETCH)
                q, k, v = q_ref[here, cols], k_ref[slot, here, column(j)], v_ref[slot, here, column(j)]
                probs = jnp.where(causal, nt(k, q), 0.0).astype(BF16)
                total = w_ref[0, pl.ds(head, 1), here] * tn(v, probs)
                for bit in range(local_bits):
                    if c >> bit & 1:
                        low = (c >> bit + 1) << bit + 1
                        left = functools.reduce(jnp.add, states[low : low + (1 << bit)])
                        total += w_ref[1 + bit, pl.ds(head, 1), here] * nt(left.astype(BF16), q)
                out_ref[column(j), here] = total
                if c + 1 < count:
                    states.append(tn(v, k))


def readout_kernel(group, first, work, n_states, carry, finish, place_ref, q_ref, w_ref, *refs):
    n = len(work)
    state_refs, total_refs, refs = refs[:n_states], refs[n_states : n_states + n], refs[n_states + n :]
    carried_ref = refs[0] if carry else None
    out_refs, squares_ref = refs[carry : carry + n], refs[carry + n]
    rows = q_ref.shape[0]
    place = place_ref[0]
    for t in range(0, rows, TILE):
        here = slice(t, t + TILE)
        squares = carried_ref[:, here] if carry else jnp.zeros((8, TILE), F32)
        for (r, complete, reads), total_ref, out_ref in zip(work, total_refs, out_refs):
            for j in range(group):
                head = (place & (QUAD - 1) ^ r) * group + j
                q = q_ref[here, pl.ds(pl.multiple_of(head * HEAD_DIM, HEAD_DIM), HEAD_DIM)]
                total = total_ref[column(j), here]
                for bit, ref, slot in reads:
                    row = w_ref[first + bit, pl.ds(head, 1), here]
                    row = jnp.where(place >> bit & 1 == 1, row, 0.0)
                    total += row * nt(state_refs[ref][slot + j], q)
                out_ref[column(j), here] = total
                if complete:
                    squares += jnp.sum((total * total).reshape(HEAD_DIM // 8, 8, TILE), axis=0)
        squares_ref[:, here] = jnp.sum(squares, axis=0, keepdims=True) if finish else squares


def norm_kernel(group, full_width, place_ref, *refs):
    total_refs, (sq_ref, gain_ref, out_hbm, buf, sems) = refs[:QUAD], refs[QUAD:]
    width = group * HEAD_DIM
    place = place_ref[0] & (QUAD - 1)
    scale = lax.rsqrt(sq_ref[...] / full_width + EPSILON)
    copies = []
    for r in range(QUAD):
        cols = pl.ds(pl.multiple_of((place ^ r) * width, width), width)
        x = jnp.transpose(total_refs[r][...] * scale, (1, 0))
        buf[r] = (x * gain_ref[:, cols]).astype(BF16)
        copies.append(pltpu.make_async_copy(buf.at[r], out_hbm.at[:, cols], sems.at[r]))
        copies[-1].start()
    for copy in copies:
        copy.wait()


def local(queries, keys, values, level_weights, norm_gain):
    rows, width = queries.shape
    group = width // HEAD_DIM // QUAD
    local_bits = (rows // STRETCH).bit_length() - 1
    seq_bits = lax.axis_size("seq").bit_length() - 1
    full_width = width * lax.axis_size("head")
    position = lax.axis_index("seq").astype(jnp.int32)
    place = position.reshape(1)
    sds = jax.ShapeDtypeStruct
    block = (group, HEAD_DIM, HEAD_DIM)
    others = (3 * group, HEAD_DIM, HEAD_DIM)
    panel = (rows, group * HEAD_DIM)
    part = sds((group * HEAD_DIM, rows), F32)

    groups = (3, 1, 2)
    k_sent, v_sent, three, one, two = pl.pallas_call(
        functools.partial(sent_kernel, group, groups),
        out_shape=(sds((3,) + panel, BF16),) * 2 + (sds(block, BF16),) * 3,
        in_specs=[SMEM, HBM, HBM],
        out_specs=(VMEM,) * 5,
        scratch_shapes=[pltpu.SemaphoreType.DMA((2, 3))],
        compiler_params=params(STATES_GRANT),
        cost_estimate=cost(3 * rows * width * HEAD_DIM // 2, 3 * rows * width),
        name="sent",
    )(place, keys, values)

    got3 = exchanged(three, "seq", 3)
    got1 = exchanged(one, "seq", 1)
    got2 = exchanged(two, "seq", 2)

    k_own, v_own, gain, own, rest = pl.pallas_call(
        functools.partial(own_kernel, group),
        out_shape=(sds((1,) + panel, BF16),) * 2 + (sds((1, width), F32), sds(block, F32), sds(others, BF16)),
        in_specs=[SMEM, HBM, HBM, HBM, VMEM, VMEM],
        out_specs=(VMEM,) * 5,
        scratch_shapes=[pltpu.SemaphoreType.DMA((2, 1)), pltpu.SemaphoreType.DMA],
        compiler_params=params(OWN_GRANT),
        cost_estimate=cost(rows * width * HEAD_DIM // 2, rows * width),
        name="own",
    )(place, keys, values, norm_gain.reshape(1, width), three, two)
    near = exchanged(rest, "seq", 1)

    totals = {}
    for work, sources in (
        (((3, 0, 0), (1, 0, 1)), (k_sent, v_sent)),
        (((2, 0, 2), (0, 1, 0)), (k_sent, v_sent, k_own, v_own)),
    ):
        outs = pl.pallas_call(
            functools.partial(intra_kernel, group, work),
            out_shape=(part,) * len(work),
            in_specs=[SMEM] + [VMEM] * (2 + len(sources)),
            out_specs=(VMEM,) * len(work),
            compiler_params=params(),
            cost_estimate=cost(3 * rows * STRETCH * width, 2 * rows * width),
            name="intra",
        )(place, queries, level_weights, *sources)
        totals |= {r: out for (r, _, _), out in zip(work, outs)}

    pair = own + got1.astype(F32)
    other = got2.astype(F32) + got3.astype(F32)
    running = pair + other
    upper = []
    for bit in range(2, seq_bits):
        came = exchanged(running.astype(BF16), "seq", 1 << bit)
        upper.append(came)
        running = running + came.astype(F32)
    top = jnp.concatenate(upper, axis=0) if len(upper) > 1 else upper[0]
    tops = {0: top} | {r: exchanged(top, "seq", r, QUAD) for r in (3, 1, 2)}

    left_pair = jnp.where(position >> 1 & 1 == 1, other, pair).astype(BF16)
    middle = {0: left_pair} | {r: exchanged(left_pair, "seq", r) for r in (3, 1, 2)}

    def top_reads(ref):
        return tuple((bit, ref, (bit - 2) * group) for bit in range(2, seq_bits))

    def readout(work, states, squares, finish=False):
        n, carry = len(work), squares is not None
        kernel = functools.partial(readout_kernel, group, 1 + local_bits, work, len(states), carry, finish)
        ins = [place, queries, level_weights, *states, *(totals[r] for r, _, _ in work)] + [squares] * carry
        shapes = [part] * n + [sds((1 if finish else 8, rows), F32)]
        outs = pl.pallas_call(
            kernel,
            out_shape=tuple(shapes),
            in_specs=[SMEM] + [VMEM] * (len(ins) - 1),
            out_specs=(VMEM,) * len(shapes),
            compiler_params=params(),
            cost_estimate=cost(n * rows * width * HEAD_DIM, 2 * n * rows * width),
        )(*ins)
        totals.update({r: out for (r, _, _), out in zip(work, outs)})
        return outs[n]

    below = {0: ((0, 0, 0), (1, 2, 0))} | {r: ((0, 1, (r - 1) * group), (1, 2 + r, 0)) for r in (1, 2, 3)}
    work = tuple((r, r == 0, below[r] + (top_reads(6) if r == 0 else ())) for r in (3, 1, 2, 0))
    squares = readout(work, (got1, near, *(middle[r] for r in range(QUAD)), top), None)
    squares = readout(((3, True, top_reads(0)), (1, True, top_reads(1))), (tops[3], tops[1]), squares)
    squares = readout(((2, True, top_reads(0)),), (tops[2],), squares, finish=True)

    mask = 1
    while mask < lax.axis_size("head"):
        squares = squares + exchanged(squares, "head", mask)
        mask *= 2

    return pl.pallas_call(
        functools.partial(norm_kernel, group, full_width),
        out_shape=sds((rows, width), BF16),
        in_specs=[SMEM] + [VMEM] * (QUAD + 2),
        out_specs=ANY,
        scratch_shapes=[pltpu.VMEM((QUAD,) + panel, BF16), pltpu.SemaphoreType.DMA((QUAD,))],
        compiler_params=params(),
        cost_estimate=cost(2 * rows * width, 2 * rows * width),
        name="norm",
    )(place, *(totals[r] for r in range(QUAD)), squares, gain)


def solution(mesh):
    return jax.shard_map(
        local,
        mesh=mesh,
        in_specs=(P("seq", "head"), P("seq", "head"), P("seq", "head"), P(None, "head", "seq"), P("head")),
        out_specs=P("seq", "head"),
        check_vma=False,
    )
```

```python
import functools

import jax
import jax.numpy as jnp
from jax import lax
from jax.experimental import pallas as pl
from jax.experimental.pallas import tpu as pltpu
from jax.sharding import PartitionSpec as P


HEAD_DIM = 128
STRETCH = 256
EPSILON = 1e-06
QUAD = 4
F32 = jnp.float32
BF16 = jnp.bfloat16
VMEM = pl.BlockSpec(memory_space=pltpu.VMEM)
SMEM = pl.BlockSpec(memory_space=pltpu.SMEM)
ANY = pl.BlockSpec(memory_space=pl.ANY)
HBM = pl.BlockSpec(memory_space=pltpu.HBM)
GRANT = 24 << 20
TILE = 256
STATES_GRANT = 52992 << 10
OWN_GRANT = 53248 << 10


def params(grant=GRANT):
    return pltpu.CompilerParams(vmem_limit_bytes=grant)


def cost(flops, moved):
    return pl.CostEstimate(flops=flops, bytes_accessed=moved, transcendentals=0)


def exchanged(block, axis, mask):
    count = lax.axis_size(axis)
    return lax.ppermute(block, axis, [(i, i ^ mask) for i in range(count)])


def exchanged_above(block, mask):
    seq, head = lax.axis_size("seq"), lax.axis_size("head")
    route = []
    for s in range(seq):
        for h in range(head):
            to = (s ^ mask, h) if s >= QUAD else (s, h ^ 1)
            route.append((s * head + h, to[0] * head + to[1]))
    return lax.ppermute(block, ("seq", "head"), route)


def nt(a, b):
    return lax.dot_general(a, b, (((1,), (1,)), ((), ())), preferred_element_type=F32)


def tn(a, b):
    return lax.dot_general(a, b, (((0,), (0,)), ((), ())), preferred_element_type=F32)


def column(head):
    return pl.ds(head * HEAD_DIM, HEAD_DIM)


def states_of(group, groups, place, k_hbm, v_hbm, k_ref, v_ref, sems, use):
    width = group * HEAD_DIM
    copies = []
    for at, r in enumerate(groups):
        cols = pl.ds(pl.multiple_of((place ^ r) * width, width), width)
        copies.append(
            (
                pltpu.make_async_copy(k_hbm.at[:, cols], k_ref.at[at], sems.at[0, at]),
                pltpu.make_async_copy(v_hbm.at[:, cols], v_ref.at[at], sems.at[1, at]),
            )
        )
        for copy in copies[-1]:
            copy.start()
    for at, r in enumerate(groups):
        for copy in copies[at]:
            copy.wait()
        for j in range(group):
            use(r, j, tn(v_ref[at, :, column(j)], k_ref[at, :, column(j)]))


def sent_kernel(group, groups, place_ref, k_hbm, v_hbm, k_ref, v_ref, *refs):
    sent = dict(zip(groups, refs))

    def use(r, j, state):
        sent[r][j] = state.astype(BF16)

    states_of(group, groups, place_ref[0] & (QUAD - 1), k_hbm, v_hbm, k_ref, v_ref, refs[-1], use)


def own_kernel(group, place_ref, k_hbm, v_hbm, gain_hbm, three_ref, two_ref, k_ref, v_ref, gain_ref, own_ref, rest_ref, sems, gain_sem):
    gain = pltpu.make_async_copy(gain_hbm, gain_ref, gain_sem)
    gain.start()
    rest_ref[group : 2 * group] = three_ref[...]
    rest_ref[2 * group :] = two_ref[...]

    def use(r, j, state):
        own_ref[j] = state
        rest_ref[j] = state.astype(BF16)

    states_of(group, (0,), place_ref[0] & (QUAD - 1), k_hbm, v_hbm, k_ref, v_ref, sems, use)
    gain.wait()


def sums_kernel(place_ref, own_ref, one_ref, two_ref, three_ref, sent_ref, left_ref, *total_refs):
    pair = own_ref[...] + one_ref[...].astype(F32)
    other = two_ref[...].astype(F32) + three_ref[...].astype(F32)
    total = pair + other
    for total_ref in total_refs:
        total_ref[...] = total
    sent_ref[...] = total.astype(BF16)
    left_ref[...] = jnp.where(place_ref[0] >> 1 & 1 == 1, other, pair).astype(BF16)


def intra_kernel(group, work, place_ref, q_ref, w_ref, *refs):
    n = len(work)
    sources, out_refs = refs[:-n], refs[-n:]
    count = q_ref.shape[0] // STRETCH
    local_bits = count.bit_length() - 1
    place = place_ref[0] & (QUAD - 1)
    causal = lax.broadcasted_iota(jnp.int32, (STRETCH, STRETCH), 0) <= lax.broadcasted_iota(
        jnp.int32, (STRETCH, STRETCH), 1
    )
    for (r, source, slot), out_ref in zip(work, out_refs):
        k_ref, v_ref = sources[2 * source : 2 * source + 2]
        for j in range(group):
            head = (place ^ r) * group + j
            cols = pl.ds(pl.multiple_of(head * HEAD_DIM, HEAD_DIM), HEAD_DIM)
            states = []
            for c in range(count):
                here = slice(c * STRETCH, (c + 1) * STRETCH)
                q, k, v = q_ref[here, cols], k_ref[slot, here, column(j)], v_ref[slot, here, column(j)]
                probs = jnp.where(causal, nt(k, q), 0.0).astype(BF16)
                total = w_ref[0, pl.ds(head, 1), here] * tn(v, probs)
                for bit in range(local_bits):
                    if c >> bit & 1:
                        low = (c >> bit + 1) << bit + 1
                        left = functools.reduce(jnp.add, states[low : low + (1 << bit)])
                        total += w_ref[1 + bit, pl.ds(head, 1), here] * nt(left.astype(BF16), q)
                out_ref[column(j), here] = total
                if c + 1 < count:
                    states.append(tn(v, k))


def readout_kernel(group, first, work, n_states, carry, finish, place_ref, q_ref, w_ref, *refs):
    n = len(work)
    state_refs, total_refs, refs = refs[:n_states], refs[n_states : n_states + n], refs[n_states + n :]
    carried_ref = refs[0] if carry else None
    out_refs, squares_ref = refs[carry : carry + n], refs[carry + n]
    rows = q_ref.shape[0]
    place = place_ref[0]
    for t in range(0, rows, TILE):
        here = slice(t, t + TILE)
        squares = carried_ref[:, here] if carry else jnp.zeros((8, TILE), F32)
        for (r, complete, reads), total_ref, out_ref in zip(work, total_refs, out_refs):
            for j in range(group):
                head = (place & (QUAD - 1) ^ r) * group + j
                q = q_ref[here, pl.ds(pl.multiple_of(head * HEAD_DIM, HEAD_DIM), HEAD_DIM)]
                total = total_ref[column(j), here]
                for bit, ref, slot in reads:
                    row = w_ref[first + bit, pl.ds(head, 1), here]
                    row = jnp.where(place >> bit & 1 == 1, row, 0.0)
                    total += row * nt(state_refs[ref][slot + j], q)
                out_ref[column(j), here] = total
                if complete:
                    squares += jnp.sum((total * total).reshape(HEAD_DIM // 8, 8, TILE), axis=0)
        squares_ref[:, here] = jnp.sum(squares, axis=0, keepdims=True) if finish else squares


def norm_kernel(group, full_width, place_ref, *refs):
    total_refs, (sq_ref, gain_ref, out_hbm, buf, sems) = refs[:QUAD], refs[QUAD:]
    width = group * HEAD_DIM
    place = place_ref[0] & (QUAD - 1)
    scale = lax.rsqrt(sq_ref[...] / full_width + EPSILON)
    copies = []
    for r in range(QUAD):
        cols = pl.ds(pl.multiple_of((place ^ r) * width, width), width)
        x = jnp.transpose(total_refs[r][...] * scale, (1, 0))
        buf[r] = (x * gain_ref[:, cols]).astype(BF16)
        copies.append(pltpu.make_async_copy(buf.at[r], out_hbm.at[:, cols], sems.at[r]))
        copies[-1].start()
    for copy in copies:
        copy.wait()


def local(queries, keys, values, level_weights, norm_gain):
    rows, width = queries.shape
    group = width // HEAD_DIM // QUAD
    local_bits = (rows // STRETCH).bit_length() - 1
    seq_bits = lax.axis_size("seq").bit_length() - 1
    full_width = width * lax.axis_size("head")
    position = lax.axis_index("seq").astype(jnp.int32)
    place = position.reshape(1)
    sds = jax.ShapeDtypeStruct
    block = (group, HEAD_DIM, HEAD_DIM)
    others = (3 * group, HEAD_DIM, HEAD_DIM)
    panel = (rows, group * HEAD_DIM)
    part = sds((group * HEAD_DIM, rows), F32)

    groups = (3, 1, 2)
    k_sent, v_sent, three, one, two = pl.pallas_call(
        functools.partial(sent_kernel, group, groups),
        out_shape=(sds((3,) + panel, BF16),) * 2 + (sds(block, BF16),) * 3,
        in_specs=[SMEM, HBM, HBM],
        out_specs=(VMEM,) * 5,
        scratch_shapes=[pltpu.SemaphoreType.DMA((2, 3))],
        compiler_params=params(STATES_GRANT),
        cost_estimate=cost(3 * rows * width * HEAD_DIM // 2, 3 * rows * width),
        name="sent",
    )(place, keys, values)

    got3 = exchanged(three, "seq", 3)
    got1 = exchanged(one, "seq", 1)
    got2 = exchanged(two, "seq", 2)

    k_own, v_own, gain, own, rest = pl.pallas_call(
        functools.partial(own_kernel, group),
        out_shape=(sds((1,) + panel, BF16),) * 2 + (sds((1, width), F32), sds(block, F32), sds(others, BF16)),
        in_specs=[SMEM, HBM, HBM, HBM, VMEM, VMEM],
        out_specs=(VMEM,) * 5,
        scratch_shapes=[pltpu.SemaphoreType.DMA((2, 1)), pltpu.SemaphoreType.DMA],
        compiler_params=params(OWN_GRANT),
        cost_estimate=cost(rows * width * HEAD_DIM // 2, rows * width),
        name="own",
    )(place, keys, values, norm_gain.reshape(1, width), three, two)
    near = exchanged(rest, "seq", 1)

    totals = {}
    for work, sources in (
        (((3, 0, 0), (1, 0, 1)), (k_sent, v_sent)),
        (((2, 0, 2), (0, 1, 0)), (k_sent, v_sent, k_own, v_own)),
    ):
        outs = pl.pallas_call(
            functools.partial(intra_kernel, group, work),
            out_shape=(part,) * len(work),
            in_specs=[SMEM] + [VMEM] * (2 + len(sources)),
            out_specs=(VMEM,) * len(work),
            compiler_params=params(),
            cost_estimate=cost(3 * rows * STRETCH * width, 2 * rows * width),
            name="intra",
        )(place, queries, level_weights, *sources)
        totals |= {r: out for (r, _, _), out in zip(work, outs)}

    sums, left_pair, *running = pl.pallas_call(
        sums_kernel,
        out_shape=(sds(block, BF16), sds(block, BF16)) + (sds(block, F32),) * (seq_bits > 3),
        in_specs=[SMEM] + [VMEM] * 4,
        out_specs=(VMEM,) * (2 + (seq_bits > 3)),
        compiler_params=params(),
        cost_estimate=cost(4 * group * HEAD_DIM**2, 16 * group * HEAD_DIM**2),
        name="sums",
    )(place, own, got1, got2, got3)
    upper = []
    for bit in range(2, seq_bits):
        if bit > 2:
            running = [running[0] + upper[-1].astype(F32)]
            sums = running[0].astype(BF16)
        upper.append(exchanged(sums, "seq", 1 << bit))
    top = jnp.concatenate(upper, axis=0) if len(upper) > 1 else upper[0]
    tops = {0: top} | {r: exchanged_above(top, r) for r in (3, 1, 2)}

    middle = {0: left_pair} | {r: exchanged(left_pair, "seq", r) for r in (3, 1, 2)}

    def top_reads(ref):
        return tuple((bit, ref, (bit - 2) * group) for bit in range(2, seq_bits))

    def readout(work, states, squares, finish=False):
        n, carry = len(work), squares is not None
        kernel = functools.partial(readout_kernel, group, 1 + local_bits, work, len(states), carry, finish)
        ins = [place, queries, level_weights, *states, *(totals[r] for r, _, _ in work)] + [squares] * carry
        shapes = [part] * n + [sds((1 if finish else 8, rows), F32)]
        outs = pl.pallas_call(
            kernel,
            out_shape=tuple(shapes),
            in_specs=[SMEM] + [VMEM] * (len(ins) - 1),
            out_specs=(VMEM,) * len(shapes),
            compiler_params=params(),
            cost_estimate=cost(n * rows * width * HEAD_DIM, 2 * n * rows * width),
        )(*ins)
        totals.update({r: out for (r, _, _), out in zip(work, outs)})
        return outs[n]

    below = {0: ((0, 0, 0), (1, 2, 0))} | {r: ((0, 1, (r - 1) * group), (1, 2 + r, 0)) for r in (1, 2, 3)}
    work = tuple((r, r == 0, below[r] + (top_reads(6) if r == 0 else ())) for r in (3, 1, 2, 0))
    squares = readout(work, (got1, near, *(middle[r] for r in range(QUAD)), top), None)
    squares = readout(((3, True, top_reads(0)), (1, True, top_reads(1))), (tops[3], tops[1]), squares)
    squares = readout(((2, True, top_reads(0)),), (tops[2],), squares, finish=True)

    mask = 1
    while mask < lax.axis_size("head"):
        squares = squares + exchanged(squares, "head", mask)
        mask *= 2

    return pl.pallas_call(
        functools.partial(norm_kernel, group, full_width),
        out_shape=sds((rows, width), BF16),
        in_specs=[SMEM] + [VMEM] * (QUAD + 2),
        out_specs=ANY,
        scratch_shapes=[pltpu.VMEM((QUAD,) + panel, BF16), pltpu.SemaphoreType.DMA((QUAD,))],
        compiler_params=params(),
        cost_estimate=cost(2 * rows * width, 2 * rows * width),
        name="norm",
    )(place, *(totals[r] for r in range(QUAD)), squares, gain)


def solution(mesh):
    return jax.shard_map(
        local,
        mesh=mesh,
        in_specs=(P("seq", "head"), P("seq", "head"), P("seq", "head"), P(None, "head", "seq"), P("head")),
        out_specs=P("seq", "head"),
        check_vma=False,
    )
```

```python
import functools

import jax
import jax.numpy as jnp
from jax import lax
from jax.experimental import pallas as pl
from jax.experimental.pallas import tpu as pltpu
from jax.sharding import PartitionSpec as P


HEAD_DIM = 128
STRETCH = 256
EPSILON = 1e-06
QUAD = 4
F32 = jnp.float32
BF16 = jnp.bfloat16
VMEM = pl.BlockSpec(memory_space=pltpu.VMEM)
SMEM = pl.BlockSpec(memory_space=pltpu.SMEM)
ANY = pl.BlockSpec(memory_space=pl.ANY)
HBM = pl.BlockSpec(memory_space=pltpu.HBM)
GRANT = 24 << 20
TILE = 256
STATES_GRANT = 51968 << 10


def params(grant=GRANT):
    return pltpu.CompilerParams(vmem_limit_bytes=grant)


def cost(flops, moved):
    return pl.CostEstimate(flops=flops, bytes_accessed=moved, transcendentals=0)


def exchanged(block, axis, mask):
    count = lax.axis_size(axis)
    return lax.ppermute(block, axis, [(i, i ^ mask) for i in range(count)])


def exchanged_in(block, mask, real):
    seq, head = lax.axis_size("seq"), lax.axis_size("head")
    route = []
    for s in range(seq):
        for h in range(head):
            to = (s ^ mask, h) if real(s // QUAD, seq // QUAD) else (s, h ^ 1)
            route.append((s * head + h, to[0] * head + to[1]))
    return lax.ppermute(block, ("seq", "head"), route)


def nt(a, b):
    return lax.dot_general(a, b, (((1,), (1,)), ((), ())), preferred_element_type=F32)


def tn(a, b):
    return lax.dot_general(a, b, (((0,), (0,)), ((), ())), preferred_element_type=F32)


def column(head):
    return pl.ds(head * HEAD_DIM, HEAD_DIM)


def states_kernel(group, place_ref, k_hbm, v_hbm, k_ref, v_ref, own_ref, one_ref, two_ref, three_ref, rest_ref, sems):
    width = group * HEAD_DIM
    place = place_ref[0] & (QUAD - 1)
    order = (3, 1, 2, 0)
    copies = {}
    for r in order:
        cols = pl.ds(pl.multiple_of((place ^ r) * width, width), width)
        copies[r] = (
            pltpu.make_async_copy(k_hbm.at[:, cols], k_ref.at[r], sems.at[0, r]),
            pltpu.make_async_copy(v_hbm.at[:, cols], v_ref.at[r], sems.at[1, r]),
        )
        for copy in copies[r]:
            copy.start()
    sent = {1: one_ref, 2: two_ref, 3: three_ref}
    spot = {0: 0, 3: 1, 2: 2}
    for r in order:
        for copy in copies[r]:
            copy.wait()
        for j in range(group):
            state = tn(v_ref[r, :, column(j)], k_ref[r, :, column(j)])
            if r == 0:
                own_ref[j] = state
            else:
                sent[r][j] = state.astype(BF16)
            if r in spot:
                rest_ref[spot[r] * group + j] = state.astype(BF16)


def sums_kernel(own_ref, one_ref, two_ref, three_ref, sent_ref, *total_refs):
    total = own_ref[...] + one_ref[...].astype(F32) + two_ref[...].astype(F32) + three_ref[...].astype(F32)
    for total_ref in total_refs:
        total_ref[...] = total
    sent_ref[...] = total.astype(BF16)


def left_kernel(seq, place_ref, own_ref, *refs):
    left_ref, neighbour_ref = refs[6:]
    last_quad = place_ref[0] >= seq - QUAD
    one, two, three = (jnp.where(last_quad, refs[3 + i][...], refs[i][...]) for i in range(3))
    pair = own_ref[...] + one.astype(F32)
    other = two.astype(F32) + three.astype(F32)
    left_ref[...] = jnp.where(place_ref[0] >> 1 & 1 == 1, other, pair).astype(BF16)
    neighbour_ref[...] = one


def intra_kernel(group, groups, place_ref, q_ref, w_ref, k_all, v_all, *refs):
    out_refs = refs[-len(groups) :]
    if len(refs) > len(groups):
        gain_ref, kept_ref = refs[:2]
        kept_ref[...] = gain_ref[...]
    count = q_ref.shape[0] // STRETCH
    local_bits = count.bit_length() - 1
    place = place_ref[0] & (QUAD - 1)
    causal = lax.broadcasted_iota(jnp.int32, (STRETCH, STRETCH), 0) <= lax.broadcasted_iota(
        jnp.int32, (STRETCH, STRETCH), 1
    )
    for r, out_ref in zip(groups, out_refs):
        for j in range(group):
            head = (place ^ r) * group + j
            cols = pl.ds(pl.multiple_of(head * HEAD_DIM, HEAD_DIM), HEAD_DIM)
            states = []
            for c in range(count):
                here = slice(c * STRETCH, (c + 1) * STRETCH)
                q, k, v = q_ref[here, cols], k_all[r, here, column(j)], v_all[r, here, column(j)]
                probs = jnp.where(causal, nt(k, q), 0.0).astype(BF16)
                total = w_ref[0, pl.ds(head, 1), here] * tn(v, probs)
                for bit in range(local_bits):
                    if c >> bit & 1:
                        low = (c >> bit + 1) << bit + 1
                        left = functools.reduce(jnp.add, states[low : low + (1 << bit)])
                        total += w_ref[1 + bit, pl.ds(head, 1), here] * nt(left.astype(BF16), q)
                out_ref[column(j), here] = total
                if c + 1 < count:
                    states.append(tn(v, k))


def readout_kernel(group, first, work, n_states, carry, finish, place_ref, q_ref, w_ref, *refs):
    n = len(work)
    state_refs, total_refs, refs = refs[:n_states], refs[n_states : n_states + n], refs[n_states + n :]
    carried_ref = refs[0] if carry else None
    out_refs, squares_ref = refs[carry : carry + n], refs[carry + n]
    rows = q_ref.shape[0]
    place = place_ref[0]
    for t in range(0, rows, TILE):
        here = slice(t, t + TILE)
        squares = carried_ref[:, here] if carry else jnp.zeros((8, TILE), F32)
        for (r, complete, reads), total_ref, out_ref in zip(work, total_refs, out_refs):
            for j in range(group):
                head = (place & (QUAD - 1) ^ r) * group + j
                q = q_ref[here, pl.ds(pl.multiple_of(head * HEAD_DIM, HEAD_DIM), HEAD_DIM)]
                total = total_ref[column(j), here]
                for bit, ref, slot in reads:
                    row = w_ref[first + bit, pl.ds(head, 1), here]
                    row = jnp.where(place >> bit & 1 == 1, row, 0.0)
                    total += row * nt(state_refs[ref][slot + j], q)
                out_ref[column(j), here] = total
                if complete:
                    squares += jnp.sum((total * total).reshape(HEAD_DIM // 8, 8, TILE), axis=0)
        squares_ref[:, here] = jnp.sum(squares, axis=0, keepdims=True) if finish else squares


def norm_kernel(group, full_width, place_ref, *refs):
    total_refs, (sq_ref, gain_ref, out_hbm, buf, sems) = refs[:QUAD], refs[QUAD:]
    width = group * HEAD_DIM
    place = place_ref[0] & (QUAD - 1)
    scale = lax.rsqrt(sq_ref[...] / full_width + EPSILON)
    copies = []
    for r in range(QUAD):
        cols = pl.ds(pl.multiple_of((place ^ r) * width, width), width)
        x = jnp.transpose(total_refs[r][...] * scale, (1, 0))
        buf[r] = (x * gain_ref[:, cols]).astype(BF16)
        copies.append(pltpu.make_async_copy(buf.at[r], out_hbm.at[:, cols], sems.at[r]))
        copies[-1].start()
    for copy in copies:
        copy.wait()


def local(queries, keys, values, level_weights, norm_gain):
    rows, width = queries.shape
    group = width // HEAD_DIM // QUAD
    local_bits = (rows // STRETCH).bit_length() - 1
    seq_bits = lax.axis_size("seq").bit_length() - 1
    full_width = width * lax.axis_size("head")
    position = lax.axis_index("seq").astype(jnp.int32)
    place = position.reshape(1)
    sds = jax.ShapeDtypeStruct
    block = (group, HEAD_DIM, HEAD_DIM)
    others = (3 * group, HEAD_DIM, HEAD_DIM)
    panel = (rows, group * HEAD_DIM)
    part_shape = sds((group * HEAD_DIM, rows), F32)

    k_all, v_all, own, one, two, three, rest = pl.pallas_call(
        functools.partial(states_kernel, group),
        out_shape=(sds((QUAD,) + panel, BF16),) * 2 + (sds(block, F32),) + (sds(block, BF16),) * 3 + (sds(others, BF16),),
        in_specs=[SMEM, HBM, HBM],
        out_specs=(VMEM,) * 7,
        scratch_shapes=[pltpu.SemaphoreType.DMA((2, QUAD))],
        compiler_params=params(STATES_GRANT),
        cost_estimate=cost(2 * rows * width * HEAD_DIM, 4 * rows * width),
        name="states",
    )(place, keys, values)

    parts = ((3, three), (1, one), (2, two))
    early = {r: exchanged_in(part, r, lambda quad, quads: quad < quads - 1) for r, part in parts}
    late = {r: exchanged_in(part, r, lambda quad, quads: quad == quads - 1) for r, part in parts}
    near = exchanged(rest, "seq", 1)

    totals = {}
    for number, groups in enumerate(((3, 1), (2, 0))):
        extra = [norm_gain.reshape(1, width)] if number == 0 else []
        outs = pl.pallas_call(
            functools.partial(intra_kernel, group, groups),
            out_shape=(sds((1, width), F32),) * len(extra) + (part_shape,) * len(groups),
            in_specs=[SMEM] + [VMEM] * (4 + len(extra)),
            out_specs=(VMEM,) * (len(extra) + len(groups)),
            compiler_params=params(),
            cost_estimate=cost(3 * rows * STRETCH * width, 2 * rows * width),
            name="intra",
        )(place, queries, level_weights, k_all, v_all, *extra)
        if extra:
            gain, *outs = outs
        totals |= dict(zip(groups, outs))

    sums, *running = pl.pallas_call(
        sums_kernel,
        out_shape=(sds(block, BF16),) + (sds(block, F32),) * (seq_bits > 3),
        in_specs=[VMEM] * 4,
        out_specs=(VMEM,) * (1 + (seq_bits > 3)),
        compiler_params=params(),
        cost_estimate=cost(4 * group * HEAD_DIM**2, 16 * group * HEAD_DIM**2),
        name="sums",
    )(own, early[1], early[2], early[3])
    upper = []
    for bit in range(2, seq_bits):
        if bit > 2:
            running = [running[0] + upper[-1].astype(F32)]
            sums = running[0].astype(BF16)
        upper.append(exchanged(sums, "seq", 1 << bit))
    left_pair, neighbour = pl.pallas_call(
        functools.partial(left_kernel, lax.axis_size("seq")),
        out_shape=(sds(block, BF16), sds(block, BF16)),
        in_specs=[SMEM] + [VMEM] * 7,
        out_specs=(VMEM,) * 2,
        compiler_params=params(),
        cost_estimate=cost(4 * group * HEAD_DIM**2, 16 * group * HEAD_DIM**2),
        name="left",
    )(place, own, early[1], early[2], early[3], late[1], late[2], late[3])
    top = jnp.concatenate(upper, axis=0) if len(upper) > 1 else upper[0]
    tops = {0: top} | {r: exchanged_in(top, r, lambda quad, quads: quad > 0) for r in (3, 1, 2)}

    middle = {0: left_pair} | {r: exchanged(left_pair, "seq", r) for r in (3, 1, 2)}

    def top_reads(ref):
        return tuple((bit, ref, (bit - 2) * group) for bit in range(2, seq_bits))

    def readout(work, states, squares, finish=False):
        n, carry = len(work), squares is not None
        kernel = functools.partial(readout_kernel, group, 1 + local_bits, work, len(states), carry, finish)
        ins = [place, queries, level_weights, *states, *(totals[r] for r, _, _ in work)] + [squares] * carry
        shapes = [part_shape] * n + [sds((1 if finish else 8, rows), F32)]
        outs = pl.pallas_call(
            kernel,
            out_shape=tuple(shapes),
            in_specs=[SMEM] + [VMEM] * (len(ins) - 1),
            out_specs=(VMEM,) * len(shapes),
            compiler_params=params(),
            cost_estimate=cost(n * rows * width * HEAD_DIM, 2 * n * rows * width),
        )(*ins)
        totals.update({r: out for (r, _, _), out in zip(work, outs)})
        return outs[n]

    below = {0: ((0, 0, 0), (1, 2, 0))} | {r: ((0, 1, (r - 1) * group), (1, 2 + r, 0)) for r in (1, 2, 3)}
    work = tuple((r, r == 0, below[r] + (top_reads(6) if r == 0 else ())) for r in (3, 1, 2, 0))
    squares = readout(work, (neighbour, near, *(middle[r] for r in range(QUAD)), top), None)
    squares = readout(((3, True, top_reads(0)), (1, True, top_reads(1))), (tops[3], tops[1]), squares)
    squares = readout(((2, True, top_reads(0)),), (tops[2],), squares, finish=True)

    mask = 1
    while mask < lax.axis_size("head"):
        squares = squares + exchanged(squares, "head", mask)
        mask *= 2

    return pl.pallas_call(
        functools.partial(norm_kernel, group, full_width),
        out_shape=sds((rows, width), BF16),
        in_specs=[SMEM] + [VMEM] * (QUAD + 2),
        out_specs=ANY,
        scratch_shapes=[pltpu.VMEM((QUAD,) + panel, BF16), pltpu.SemaphoreType.DMA((QUAD,))],
        compiler_params=params(),
        cost_estimate=cost(2 * rows * width, 2 * rows * width),
        name="norm",
    )(place, *(totals[r] for r in range(QUAD)), squares, gain)


def solution(mesh):
    return jax.shard_map(
        local,
        mesh=mesh,
        in_specs=(P("seq", "head"), P("seq", "head"), P("seq", "head"), P(None, "head", "seq"), P("head")),
        out_specs=P("seq", "head"),
        check_vma=False,
    )
```

```python
import functools

import jax
import jax.numpy as jnp
from jax import lax
from jax.experimental import pallas as pl
from jax.experimental.pallas import tpu as pltpu
from jax.sharding import PartitionSpec as P


HEAD_DIM = 128
STRETCH = 256
EPSILON = 1e-06
QUAD = 4
F32 = jnp.float32
BF16 = jnp.bfloat16
VMEM = pl.BlockSpec(memory_space=pltpu.VMEM)
SMEM = pl.BlockSpec(memory_space=pltpu.SMEM)
ANY = pl.BlockSpec(memory_space=pl.ANY)
HBM = pl.BlockSpec(memory_space=pltpu.HBM)
GRANT = 24 << 20
TILE = 256
STATES_GRANT = 51968 << 10


def params(grant=GRANT):
    return pltpu.CompilerParams(vmem_limit_bytes=grant)


def cost(flops, moved):
    return pl.CostEstimate(flops=flops, bytes_accessed=moved, transcendentals=0)


def exchanged(block, axis, mask):
    count = lax.axis_size(axis)
    return lax.ppermute(block, axis, [(i, i ^ mask) for i in range(count)])


def exchanged_in(block, mask, real):
    seq, head = lax.axis_size("seq"), lax.axis_size("head")
    route = []
    for s in range(seq):
        for h in range(head):
            to = (s ^ mask, h) if real(s // QUAD, seq // QUAD) else (s, h ^ 1)
            route.append((s * head + h, to[0] * head + to[1]))
    return lax.ppermute(block, ("seq", "head"), route)


def nt(a, b):
    return lax.dot_general(a, b, (((1,), (1,)), ((), ())), preferred_element_type=F32)


def tn(a, b):
    return lax.dot_general(a, b, (((0,), (0,)), ((), ())), preferred_element_type=F32)


def column(head):
    return pl.ds(head * HEAD_DIM, HEAD_DIM)


def states_kernel(group, place_ref, k_hbm, v_hbm, k_ref, v_ref, own_ref, one_ref, two_ref, three_ref, rest_ref, sems):
    width = group * HEAD_DIM
    place = place_ref[0] & (QUAD - 1)
    order = (3, 1, 2, 0)
    copies = {}
    for r in order:
        cols = pl.ds(pl.multiple_of((place ^ r) * width, width), width)
        copies[r] = (
            pltpu.make_async_copy(k_hbm.at[:, cols], k_ref.at[r], sems.at[0, r]),
            pltpu.make_async_copy(v_hbm.at[:, cols], v_ref.at[r], sems.at[1, r]),
        )
        for copy in copies[r]:
            copy.start()
    sent = {1: one_ref, 2: two_ref, 3: three_ref}
    spot = {0: 0, 3: 1, 2: 2}
    for r in order:
        for copy in copies[r]:
            copy.wait()
        for j in range(group):
            state = tn(v_ref[r, :, column(j)], k_ref[r, :, column(j)])
            if r == 0:
                own_ref[j] = state
            else:
                sent[r][j] = state.astype(BF16)
            if r in spot:
                rest_ref[spot[r] * group + j] = state.astype(BF16)


def sums_kernel(own_ref, one_ref, two_ref, three_ref, sent_ref, *total_refs):
    total = own_ref[...] + one_ref[...].astype(F32) + two_ref[...].astype(F32) + three_ref[...].astype(F32)
    for total_ref in total_refs:
        total_ref[...] = total
    sent_ref[...] = total.astype(BF16)


def left_kernel(seq, place_ref, own_ref, *refs):
    left_ref, neighbour_ref = refs[6:]
    last_quad = place_ref[0] >= seq - QUAD
    one, two, three = (jnp.where(last_quad, refs[3 + i][...], refs[i][...]) for i in range(3))
    pair = own_ref[...] + one.astype(F32)
    other = two.astype(F32) + three.astype(F32)
    left_ref[...] = jnp.where(place_ref[0] >> 1 & 1 == 1, other, pair).astype(BF16)
    neighbour_ref[...] = one


def intra_kernel(group, groups, place_ref, q_ref, w_ref, k_all, v_all, *refs):
    out_refs = refs[-len(groups) :]
    if len(refs) > len(groups):
        gain_ref, kept_ref = refs[:2]
        kept_ref[...] = gain_ref[...]
    count = q_ref.shape[0] // STRETCH
    local_bits = count.bit_length() - 1
    place = place_ref[0] & (QUAD - 1)
    causal = lax.broadcasted_iota(jnp.int32, (STRETCH, STRETCH), 0) <= lax.broadcasted_iota(
        jnp.int32, (STRETCH, STRETCH), 1
    )
    for r, out_ref in zip(groups, out_refs):
        for j in range(group):
            head = (place ^ r) * group + j
            cols = pl.ds(pl.multiple_of(head * HEAD_DIM, HEAD_DIM), HEAD_DIM)
            states = []
            for c in range(count):
                here = slice(c * STRETCH, (c + 1) * STRETCH)
                q, k, v = q_ref[here, cols], k_all[r, here, column(j)], v_all[r, here, column(j)]
                probs = jnp.where(causal, nt(k, q), 0.0).astype(BF16)
                total = w_ref[0, pl.ds(head, 1), here] * tn(v, probs)
                for bit in range(local_bits):
                    if c >> bit & 1:
                        low = (c >> bit + 1) << bit + 1
                        left = functools.reduce(jnp.add, states[low : low + (1 << bit)])
                        total += w_ref[1 + bit, pl.ds(head, 1), here] * nt(left.astype(BF16), q)
                out_ref[column(j), here] = total
                if c + 1 < count:
                    states.append(tn(v, k))


def readout_kernel(group, first, work, n_states, carry, finish, place_ref, q_ref, w_ref, *refs):
    n = len(work)
    state_refs, total_refs, refs = refs[:n_states], refs[n_states : n_states + n], refs[n_states + n :]
    carried_ref = refs[0] if carry else None
    out_refs, squares_ref = refs[carry : carry + n], refs[carry + n]
    rows = q_ref.shape[0]
    place = place_ref[0]
    for t in range(0, rows, TILE):
        here = slice(t, t + TILE)
        squares = carried_ref[:, here] if carry else jnp.zeros((8, TILE), F32)
        for (r, complete, reads), total_ref, out_ref in zip(work, total_refs, out_refs):
            for j in range(group):
                head = (place & (QUAD - 1) ^ r) * group + j
                q = q_ref[here, pl.ds(pl.multiple_of(head * HEAD_DIM, HEAD_DIM), HEAD_DIM)]
                total = total_ref[column(j), here]
                for bit, ref, slot in reads:
                    row = w_ref[first + bit, pl.ds(head, 1), here]
                    row = jnp.where(place >> bit & 1 == 1, row, 0.0)
                    total += row * nt(state_refs[ref][slot + j], q)
                out_ref[column(j), here] = total
                if complete:
                    squares += jnp.sum((total * total).reshape(HEAD_DIM // 8, 8, TILE), axis=0)
        squares_ref[:, here] = jnp.sum(squares, axis=0, keepdims=True) if finish else squares


def norm_kernel(group, full_width, place_ref, *refs):
    total_refs, share_refs, (gain_ref, out_hbm, buf, sems) = refs[:QUAD], refs[QUAD:-4], refs[-4:]
    width = group * HEAD_DIM
    place = place_ref[0] & (QUAD - 1)
    scale = lax.rsqrt(functools.reduce(jnp.add, (ref[...] for ref in share_refs)) / full_width + EPSILON)
    copies = []
    for r in range(QUAD):
        cols = pl.ds(pl.multiple_of((place ^ r) * width, width), width)
        x = jnp.transpose(total_refs[r][...] * scale, (1, 0))
        buf[r] = (x * gain_ref[:, cols]).astype(BF16)
        copies.append(pltpu.make_async_copy(buf.at[r], out_hbm.at[:, cols], sems.at[r]))
        copies[-1].start()
    for copy in copies:
        copy.wait()


def local(queries, keys, values, level_weights, norm_gain):
    rows, width = queries.shape
    group = width // HEAD_DIM // QUAD
    local_bits = (rows // STRETCH).bit_length() - 1
    seq_bits = lax.axis_size("seq").bit_length() - 1
    full_width = width * lax.axis_size("head")
    position = lax.axis_index("seq").astype(jnp.int32)
    place = position.reshape(1)
    sds = jax.ShapeDtypeStruct
    block = (group, HEAD_DIM, HEAD_DIM)
    others = (3 * group, HEAD_DIM, HEAD_DIM)
    panel = (rows, group * HEAD_DIM)
    part_shape = sds((group * HEAD_DIM, rows), F32)

    k_all, v_all, own, one, two, three, rest = pl.pallas_call(
        functools.partial(states_kernel, group),
        out_shape=(sds((QUAD,) + panel, BF16),) * 2 + (sds(block, F32),) + (sds(block, BF16),) * 3 + (sds(others, BF16),),
        in_specs=[SMEM, HBM, HBM],
        out_specs=(VMEM,) * 7,
        scratch_shapes=[pltpu.SemaphoreType.DMA((2, QUAD))],
        compiler_params=params(STATES_GRANT),
        cost_estimate=cost(2 * rows * width * HEAD_DIM, 4 * rows * width),
        name="states",
    )(place, keys, values)

    parts = ((3, three), (1, one), (2, two))
    early = {r: exchanged_in(part, r, lambda quad, quads: quad < quads - 1) for r, part in parts}
    late = {r: exchanged_in(part, r, lambda quad, quads: quad == quads - 1) for r, part in parts}
    near = exchanged(rest, "seq", 1)

    totals = {}
    for number, groups in enumerate(((3, 1), (2, 0))):
        extra = [norm_gain.reshape(1, width)] if number == 0 else []
        outs = pl.pallas_call(
            functools.partial(intra_kernel, group, groups),
            out_shape=(sds((1, width), F32),) * len(extra) + (part_shape,) * len(groups),
            in_specs=[SMEM] + [VMEM] * (4 + len(extra)),
            out_specs=(VMEM,) * (len(extra) + len(groups)),
            compiler_params=params(),
            cost_estimate=cost(3 * rows * STRETCH * width, 2 * rows * width),
            name="intra",
        )(place, queries, level_weights, k_all, v_all, *extra)
        if extra:
            gain, *outs = outs
        totals |= dict(zip(groups, outs))

    sums, *running = pl.pallas_call(
        sums_kernel,
        out_shape=(sds(block, BF16),) + (sds(block, F32),) * (seq_bits > 3),
        in_specs=[VMEM] * 4,
        out_specs=(VMEM,) * (1 + (seq_bits > 3)),
        compiler_params=params(),
        cost_estimate=cost(4 * group * HEAD_DIM**2, 16 * group * HEAD_DIM**2),
        name="sums",
    )(own, early[1], early[2], early[3])
    upper = []
    for bit in range(2, seq_bits):
        if bit > 2:
            running = [running[0] + upper[-1].astype(F32)]
            sums = running[0].astype(BF16)
        upper.append(exchanged(sums, "seq", 1 << bit))
    left_pair, neighbour = pl.pallas_call(
        functools.partial(left_kernel, lax.axis_size("seq")),
        out_shape=(sds(block, BF16), sds(block, BF16)),
        in_specs=[SMEM] + [VMEM] * 7,
        out_specs=(VMEM,) * 2,
        compiler_params=params(),
        cost_estimate=cost(4 * group * HEAD_DIM**2, 16 * group * HEAD_DIM**2),
        name="left",
    )(place, own, early[1], early[2], early[3], late[1], late[2], late[3])
    top = jnp.concatenate(upper, axis=0) if len(upper) > 1 else upper[0]
    tops = {0: top} | {r: exchanged_in(top, r, lambda quad, quads: quad > 0) for r in (3, 1, 2)}

    middle = {0: left_pair} | {r: exchanged(left_pair, "seq", r) for r in (3, 1, 2)}

    def top_reads(ref):
        return tuple((bit, ref, (bit - 2) * group) for bit in range(2, seq_bits))

    def readout(work, states, squares, finish=False):
        n, carry = len(work), squares is not None
        kernel = functools.partial(readout_kernel, group, 1 + local_bits, work, len(states), carry, finish)
        ins = [place, queries, level_weights, *states, *(totals[r] for r, _, _ in work)] + [squares] * carry
        shapes = [part_shape] * n + [sds((1 if finish else 8, rows), F32)]
        outs = pl.pallas_call(
            kernel,
            out_shape=tuple(shapes),
            in_specs=[SMEM] + [VMEM] * (len(ins) - 1),
            out_specs=(VMEM,) * len(shapes),
            compiler_params=params(),
            cost_estimate=cost(n * rows * width * HEAD_DIM, 2 * n * rows * width),
        )(*ins)
        totals.update({r: out for (r, _, _), out in zip(work, outs)})
        return outs[n]

    below = {0: ((0, 0, 0), (1, 2, 0))} | {r: ((0, 1, (r - 1) * group), (1, 2 + r, 0)) for r in (1, 2, 3)}
    work = tuple((r, r == 0, below[r] + (top_reads(6) if r == 0 else ())) for r in (3, 1, 2, 0))
    squares = readout(work, (neighbour, near, *(middle[r] for r in range(QUAD)), top), None)
    squares = readout(((3, True, top_reads(0)), (1, True, top_reads(1))), (tops[3], tops[1]), squares)
    squares = readout(((2, True, top_reads(0)),), (tops[2],), squares, finish=True)

    shares = [squares] + [exchanged(squares, "head", mask) for mask in range(1, lax.axis_size("head"))]

    return pl.pallas_call(
        functools.partial(norm_kernel, group, full_width),
        out_shape=sds((rows, width), BF16),
        in_specs=[SMEM] + [VMEM] * (QUAD + len(shares) + 1),
        out_specs=ANY,
        scratch_shapes=[pltpu.VMEM((QUAD,) + panel, BF16), pltpu.SemaphoreType.DMA((QUAD,))],
        compiler_params=params(),
        cost_estimate=cost(2 * rows * width, 2 * rows * width),
        name="norm",
    )(place, *(totals[r] for r in range(QUAD)), *shares, gain)


def solution(mesh):
    return jax.shard_map(
        local,
        mesh=mesh,
        in_specs=(P("seq", "head"), P("seq", "head"), P("seq", "head"), P(None, "head", "seq"), P("head")),
        out_specs=P("seq", "head"),
        check_vma=False,
    )
```

```python
import functools

import jax
import jax.numpy as jnp
from jax import lax
from jax.experimental import pallas as pl
from jax.experimental.pallas import tpu as pltpu
from jax.sharding import PartitionSpec as P


HEAD_DIM = 128
STRETCH = 256
EPSILON = 1e-06
QUAD = 4
F32 = jnp.float32
BF16 = jnp.bfloat16
VMEM = pl.BlockSpec(memory_space=pltpu.VMEM)
SMEM = pl.BlockSpec(memory_space=pltpu.SMEM)
ANY = pl.BlockSpec(memory_space=pl.ANY)
HBM = pl.BlockSpec(memory_space=pltpu.HBM)
GRANT = 24 << 20
TILE = 256
STATES_GRANT = 51968 << 10


def params(grant=GRANT):
    return pltpu.CompilerParams(vmem_limit_bytes=grant)


def cost(flops, moved):
    return pl.CostEstimate(flops=flops, bytes_accessed=moved, transcendentals=0)


def exchanged(block, axis, mask):
    count = lax.axis_size(axis)
    return lax.ppermute(block, axis, [(i, i ^ mask) for i in range(count)])


def exchanged_in(block, mask, real):
    seq, head = lax.axis_size("seq"), lax.axis_size("head")
    route = []
    for s in range(seq):
        for h in range(head):
            to = (s ^ mask, h) if real(s // QUAD, seq // QUAD) else (s, h ^ 1)
            route.append((s * head + h, to[0] * head + to[1]))
    return lax.ppermute(block, ("seq", "head"), route)


def nt(a, b):
    return lax.dot_general(a, b, (((1,), (1,)), ((), ())), preferred_element_type=F32)


def tn(a, b):
    return lax.dot_general(a, b, (((0,), (0,)), ((), ())), preferred_element_type=F32)


def column(head):
    return pl.ds(head * HEAD_DIM, HEAD_DIM)


def states_kernel(group, place_ref, k_hbm, v_hbm, k_ref, v_ref, even_ref, one_ref, two_ref, three_ref, odd_sent_ref, even_sent_ref, sems):
    width = group * HEAD_DIM
    place = place_ref[0] & (QUAD - 1)
    order = (3, 1, 2, 0)
    copies = {}
    for r in order:
        cols = pl.ds(pl.multiple_of((place ^ r) * width, width), width)
        copies[r] = (
            pltpu.make_async_copy(k_hbm.at[:, cols], k_ref.at[r], sems.at[0, r]),
            pltpu.make_async_copy(v_hbm.at[:, cols], v_ref.at[r], sems.at[1, r]),
        )
        for copy in copies[r]:
            copy.start()
    sent = {1: one_ref, 2: two_ref, 3: three_ref}
    for r in order:
        for copy in copies[r]:
            copy.wait()
        for j in range(group):
            state = tn(v_ref[r, :, column(j)], k_ref[r, :, column(j)])
            spot = r // 2 * group + j
            if r % 2 == 0:
                even_ref[spot] = state
            (odd_sent_ref if r % 2 else even_sent_ref)[spot] = state.astype(BF16)
            if r in sent:
                sent[r][j] = state.astype(BF16)


def sums_kernel(group, even_ref, one_ref, two_ref, three_ref, sent_ref, *total_refs):
    total = even_ref[:group] + one_ref[...].astype(F32) + two_ref[...].astype(F32) + three_ref[...].astype(F32)
    for total_ref in total_refs:
        total_ref[...] = total
    sent_ref[...] = total.astype(BF16)


def pair_kernel(even_ref, near_ref, pair_ref):
    pair_ref[...] = (even_ref[...] + near_ref[...].astype(F32)).astype(BF16)


def intra_kernel(group, groups, place_ref, q_ref, w_ref, k_all, v_all, *refs):
    out_refs = refs[-len(groups) :]
    if len(refs) > len(groups):
        gain_ref, kept_ref = refs[:2]
        kept_ref[...] = gain_ref[...]
    count = q_ref.shape[0] // STRETCH
    local_bits = count.bit_length() - 1
    place = place_ref[0] & (QUAD - 1)
    causal = lax.broadcasted_iota(jnp.int32, (STRETCH, STRETCH), 0) <= lax.broadcasted_iota(
        jnp.int32, (STRETCH, STRETCH), 1
    )
    for r, out_ref in zip(groups, out_refs):
        for j in range(group):
            head = (place ^ r) * group + j
            cols = pl.ds(pl.multiple_of(head * HEAD_DIM, HEAD_DIM), HEAD_DIM)
            states = []
            for c in range(count):
                here = slice(c * STRETCH, (c + 1) * STRETCH)
                q, k, v = q_ref[here, cols], k_all[r, here, column(j)], v_all[r, here, column(j)]
                probs = jnp.where(causal, nt(k, q), 0.0).astype(BF16)
                total = w_ref[0, pl.ds(head, 1), here] * tn(v, probs)
                for bit in range(local_bits):
                    if c >> bit & 1:
                        low = (c >> bit + 1) << bit + 1
                        left = functools.reduce(jnp.add, states[low : low + (1 << bit)])
                        total += w_ref[1 + bit, pl.ds(head, 1), here] * nt(left.astype(BF16), q)
                out_ref[column(j), here] = total
                if c + 1 < count:
                    states.append(tn(v, k))


def readout_kernel(group, first, work, n_states, carry, finish, place_ref, q_ref, w_ref, *refs):
    n = len(work)
    state_refs, total_refs, refs = refs[:n_states], refs[n_states : n_states + n], refs[n_states + n :]
    carried_ref = refs[0] if carry else None
    out_refs, squares_ref = refs[carry : carry + n], refs[carry + n]
    rows = q_ref.shape[0]
    place = place_ref[0]
    for t in range(0, rows, TILE):
        here = slice(t, t + TILE)
        squares = carried_ref[:, here] if carry else jnp.zeros((8, TILE), F32)
        for (r, complete, reads), total_ref, out_ref in zip(work, total_refs, out_refs):
            for j in range(group):
                head = (place & (QUAD - 1) ^ r) * group + j
                q = q_ref[here, pl.ds(pl.multiple_of(head * HEAD_DIM, HEAD_DIM), HEAD_DIM)]
                total = total_ref[column(j), here]
                for bit, ref, slot in reads:
                    row = w_ref[first + bit, pl.ds(head, 1), here]
                    row = jnp.where(place >> bit & 1 == 1, row, 0.0)
                    total += row * nt(state_refs[ref][slot + j], q)
                out_ref[column(j), here] = total
                if complete:
                    squares += jnp.sum((total * total).reshape(HEAD_DIM // 8, 8, TILE), axis=0)
        squares_ref[:, here] = jnp.sum(squares, axis=0, keepdims=True) if finish else squares


def norm_kernel(group, full_width, place_ref, *refs):
    total_refs, share_refs, (gain_ref, out_hbm, buf, sems) = refs[:QUAD], refs[QUAD:-4], refs[-4:]
    width = group * HEAD_DIM
    place = place_ref[0] & (QUAD - 1)
    scale = lax.rsqrt(functools.reduce(jnp.add, (ref[...] for ref in share_refs)) / full_width + EPSILON)
    copies = []
    for r in range(QUAD):
        cols = pl.ds(pl.multiple_of((place ^ r) * width, width), width)
        x = jnp.transpose(total_refs[r][...] * scale, (1, 0))
        buf[r] = (x * gain_ref[:, cols]).astype(BF16)
        copies.append(pltpu.make_async_copy(buf.at[r], out_hbm.at[:, cols], sems.at[r]))
        copies[-1].start()
    for copy in copies:
        copy.wait()


def local(queries, keys, values, level_weights, norm_gain):
    rows, width = queries.shape
    group = width // HEAD_DIM // QUAD
    local_bits = (rows // STRETCH).bit_length() - 1
    seq_bits = lax.axis_size("seq").bit_length() - 1
    full_width = width * lax.axis_size("head")
    position = lax.axis_index("seq").astype(jnp.int32)
    place = position.reshape(1)
    sds = jax.ShapeDtypeStruct
    block = (group, HEAD_DIM, HEAD_DIM)
    half = (2 * group, HEAD_DIM, HEAD_DIM)
    panel = (rows, group * HEAD_DIM)
    part_shape = sds((group * HEAD_DIM, rows), F32)

    k_all, v_all, even, one, two, three, odd_sent, even_sent = pl.pallas_call(
        functools.partial(states_kernel, group),
        out_shape=(sds((QUAD,) + panel, BF16),) * 2 + (sds(half, F32),) + (sds(block, BF16),) * 3 + (sds(half, BF16),) * 2,
        in_specs=[SMEM, HBM, HBM],
        out_specs=(VMEM,) * 8,
        scratch_shapes=[pltpu.SemaphoreType.DMA((2, QUAD))],
        compiler_params=params(STATES_GRANT),
        cost_estimate=cost(2 * rows * width * HEAD_DIM, 4 * rows * width),
        name="states",
    )(place, keys, values)

    parts = ((3, three), (1, one), (2, two))
    taken = {r: exchanged_in(part, r, lambda quad, quads: quad < quads - 1) for r, part in parts}
    near = exchanged(odd_sent, "seq", 1), exchanged(even_sent, "seq", 1)

    totals = {}
    for number, groups in enumerate(((3, 1), (2, 0))):
        extra = [norm_gain.reshape(1, width)] if number == 0 else []
        outs = pl.pallas_call(
            functools.partial(intra_kernel, group, groups),
            out_shape=(sds((1, width), F32),) * len(extra) + (part_shape,) * len(groups),
            in_specs=[SMEM] + [VMEM] * (4 + len(extra)),
            out_specs=(VMEM,) * (len(extra) + len(groups)),
            compiler_params=params(),
            cost_estimate=cost(3 * rows * STRETCH * width, 2 * rows * width),
            name="intra",
        )(place, queries, level_weights, k_all, v_all, *extra)
        if extra:
            gain, *outs = outs
        totals |= dict(zip(groups, outs))

    sums, *running = pl.pallas_call(
        functools.partial(sums_kernel, group),
        out_shape=(sds(block, BF16),) + (sds(block, F32),) * (seq_bits > 3),
        in_specs=[VMEM] * 4,
        out_specs=(VMEM,) * (1 + (seq_bits > 3)),
        compiler_params=params(),
        cost_estimate=cost(4 * group * HEAD_DIM**2, 16 * group * HEAD_DIM**2),
        name="sums",
    )(even, taken[1], taken[2], taken[3])
    upper = []
    for bit in range(2, seq_bits):
        if bit > 2:
            running = [running[0] + upper[-1].astype(F32)]
            sums = running[0].astype(BF16)
        upper.append(exchanged(sums, "seq", 1 << bit))
    pair = pl.pallas_call(
        pair_kernel,
        out_shape=sds(half, BF16),
        in_specs=[VMEM] * 2,
        out_specs=VMEM,
        compiler_params=params(),
        cost_estimate=cost(2 * group * HEAD_DIM**2, 16 * group * HEAD_DIM**2),
        name="pair",
    )(even, near[0])
    middle = exchanged(pair, "seq", 2), exchanged(pair, "seq", 3)
    top = jnp.concatenate(upper, axis=0) if len(upper) > 1 else upper[0]
    tops = {0: top} | {r: exchanged_in(top, r, lambda quad, quads: quad > 0) for r in (3, 1, 2)}

    def top_reads(ref):
        return tuple((bit, ref, (bit - 2) * group) for bit in range(2, seq_bits))

    def readout(work, states, squares, finish=False):
        n, carry = len(work), squares is not None
        kernel = functools.partial(readout_kernel, group, 1 + local_bits, work, len(states), carry, finish)
        ins = [place, queries, level_weights, *states, *(totals[r] for r, _, _ in work)] + [squares] * carry
        shapes = [part_shape] * n + [sds((1 if finish else 8, rows), F32)]
        outs = pl.pallas_call(
            kernel,
            out_shape=tuple(shapes),
            in_specs=[SMEM] + [VMEM] * (len(ins) - 1),
            out_specs=(VMEM,) * len(shapes),
            compiler_params=params(),
            cost_estimate=cost(n * rows * width * HEAD_DIM, 2 * n * rows * width),
        )(*ins)
        totals.update({r: out for (r, _, _), out in zip(work, outs)})
        return outs[n]

    below = {r: ((0, r % 2, r // 2 * group), (1, 2 + r % 2, (1 - r // 2) * group)) for r in range(QUAD)}
    work = tuple((r, r == 0, below[r] + (top_reads(4) if r == 0 else ())) for r in (3, 1, 2, 0))
    squares = readout(work, (*near, *middle, top), None)
    squares = readout(((3, True, top_reads(0)), (1, True, top_reads(1))), (tops[3], tops[1]), squares)
    squares = readout(((2, True, top_reads(0)),), (tops[2],), squares, finish=True)

    shares = [squares] + [exchanged(squares, "head", mask) for mask in range(1, lax.axis_size("head"))]

    return pl.pallas_call(
        functools.partial(norm_kernel, group, full_width),
        out_shape=sds((rows, width), BF16),
        in_specs=[SMEM] + [VMEM] * (QUAD + len(shares) + 1),
        out_specs=ANY,
        scratch_shapes=[pltpu.VMEM((QUAD,) + panel, BF16), pltpu.SemaphoreType.DMA((QUAD,))],
        compiler_params=params(),
        cost_estimate=cost(2 * rows * width, 2 * rows * width),
        name="norm",
    )(place, *(totals[r] for r in range(QUAD)), *shares, gain)


def solution(mesh):
    return jax.shard_map(
        local,
        mesh=mesh,
        in_specs=(P("seq", "head"), P("seq", "head"), P("seq", "head"), P(None, "head", "seq"), P("head")),
        out_specs=P("seq", "head"),
        check_vma=False,
    )
```

```python
import functools

import jax
import jax.numpy as jnp
from jax import lax
from jax.experimental import pallas as pl
from jax.experimental.pallas import tpu as pltpu
from jax.sharding import PartitionSpec as P


HEAD_DIM = 128
STRETCH = 256
EPSILON = 1e-06
QUAD = 4
F32 = jnp.float32
BF16 = jnp.bfloat16
VMEM = pl.BlockSpec(memory_space=pltpu.VMEM)
SMEM = pl.BlockSpec(memory_space=pltpu.SMEM)
ANY = pl.BlockSpec(memory_space=pl.ANY)
HBM = pl.BlockSpec(memory_space=pltpu.HBM)
GRANT = 24 << 20
TILE = 256
STATES_GRANT = 51968 << 10


def params(grant=GRANT):
    return pltpu.CompilerParams(vmem_limit_bytes=grant)


def cost(flops, moved):
    return pl.CostEstimate(flops=flops, bytes_accessed=moved, transcendentals=0)


def exchanged(block, axis, mask):
    count = lax.axis_size(axis)
    return lax.ppermute(block, axis, [(i, i ^ mask) for i in range(count)])


def exchanged_in(block, mask, real):
    seq, head = lax.axis_size("seq"), lax.axis_size("head")
    route = []
    for s in range(seq):
        for h in range(head):
            to = (s ^ mask, h) if real(s // QUAD, seq // QUAD) else (s, h ^ 1)
            route.append((s * head + h, to[0] * head + to[1]))
    return lax.ppermute(block, ("seq", "head"), route)


def nt(a, b):
    return lax.dot_general(a, b, (((1,), (1,)), ((), ())), preferred_element_type=F32)


def tn(a, b):
    return lax.dot_general(a, b, (((0,), (0,)), ((), ())), preferred_element_type=F32)


def column(head):
    return pl.ds(head * HEAD_DIM, HEAD_DIM)


def states_kernel(group, place_ref, k_hbm, v_hbm, k_ref, v_ref, even_ref, one_ref, two_ref, three_ref, even_sent_ref, sems):
    width = group * HEAD_DIM
    place = place_ref[0] & (QUAD - 1)
    order = (3, 1, 2, 0)
    copies = {}
    for r in order:
        cols = pl.ds(pl.multiple_of((place ^ r) * width, width), width)
        copies[r] = (
            pltpu.make_async_copy(k_hbm.at[:, cols], k_ref.at[r], sems.at[0, r]),
            pltpu.make_async_copy(v_hbm.at[:, cols], v_ref.at[r], sems.at[1, r]),
        )
        for copy in copies[r]:
            copy.start()
    sent = {1: one_ref, 2: two_ref, 3: three_ref}
    for r in order:
        for copy in copies[r]:
            copy.wait()
        for j in range(group):
            state = tn(v_ref[r, :, column(j)], k_ref[r, :, column(j)])
            spot = r // 2 * group + j
            if r % 2 == 0:
                even_ref[spot] = state
                even_sent_ref[spot] = state.astype(BF16)
            if r in sent:
                sent[r][j] = state.astype(BF16)


def sums_kernel(group, even_ref, one_ref, two_ref, three_ref, sent_ref, *total_refs):
    total = even_ref[:group] + one_ref[...].astype(F32) + two_ref[...].astype(F32) + three_ref[...].astype(F32)
    for total_ref in total_refs:
        total_ref[...] = total
    sent_ref[...] = total.astype(BF16)


def pair_kernel(group, even_ref, near0_ref, near2_ref, pair_ref):
    pair_ref[:group] = (even_ref[:group] + near0_ref[...].astype(F32)).astype(BF16)
    pair_ref[group:] = (even_ref[group:] + near2_ref[...].astype(F32)).astype(BF16)


def intra_kernel(group, groups, place_ref, q_ref, w_ref, k_all, v_all, *refs):
    out_refs = refs[-len(groups) :]
    if len(refs) > len(groups):
        gain_ref, kept_ref = refs[:2]
        kept_ref[...] = gain_ref[...]
    count = q_ref.shape[0] // STRETCH
    local_bits = count.bit_length() - 1
    place = place_ref[0] & (QUAD - 1)
    causal = lax.broadcasted_iota(jnp.int32, (STRETCH, STRETCH), 0) <= lax.broadcasted_iota(
        jnp.int32, (STRETCH, STRETCH), 1
    )
    for r, out_ref in zip(groups, out_refs):
        for j in range(group):
            head = (place ^ r) * group + j
            cols = pl.ds(pl.multiple_of(head * HEAD_DIM, HEAD_DIM), HEAD_DIM)
            states = []
            for c in range(count):
                here = slice(c * STRETCH, (c + 1) * STRETCH)
                q, k, v = q_ref[here, cols], k_all[r, here, column(j)], v_all[r, here, column(j)]
                probs = jnp.where(causal, nt(k, q), 0.0).astype(BF16)
                total = w_ref[0, pl.ds(head, 1), here] * tn(v, probs)
                for bit in range(local_bits):
                    if c >> bit & 1:
                        low = (c >> bit + 1) << bit + 1
                        left = functools.reduce(jnp.add, states[low : low + (1 << bit)])
                        total += w_ref[1 + bit, pl.ds(head, 1), here] * nt(left.astype(BF16), q)
                out_ref[column(j), here] = total
                if c + 1 < count:
                    states.append(tn(v, k))


def readout_kernel(group, first, work, n_states, carry, finish, place_ref, q_ref, w_ref, *refs):
    n = len(work)
    state_refs, total_refs, refs = refs[:n_states], refs[n_states : n_states + n], refs[n_states + n :]
    carried_ref = refs[0] if carry else None
    out_refs, squares_ref = refs[carry : carry + n], refs[carry + n]
    rows = q_ref.shape[0]
    place = place_ref[0]
    for t in range(0, rows, TILE):
        here = slice(t, t + TILE)
        squares = carried_ref[:, here] if carry else jnp.zeros((8, TILE), F32)
        for (r, complete, reads), total_ref, out_ref in zip(work, total_refs, out_refs):
            for j in range(group):
                head = (place & (QUAD - 1) ^ r) * group + j
                q = q_ref[here, pl.ds(pl.multiple_of(head * HEAD_DIM, HEAD_DIM), HEAD_DIM)]
                total = total_ref[column(j), here]
                for bit, ref, slot in reads:
                    row = w_ref[first + bit, pl.ds(head, 1), here]
                    row = jnp.where(place >> bit & 1 == 1, row, 0.0)
                    total += row * nt(state_refs[ref][slot + j], q)
                out_ref[column(j), here] = total
                if complete:
                    squares += jnp.sum((total * total).reshape(HEAD_DIM // 8, 8, TILE), axis=0)
        squares_ref[:, here] = jnp.sum(squares, axis=0, keepdims=True) if finish else squares


def norm_kernel(group, full_width, place_ref, *refs):
    total_refs, share_refs, (gain_ref, out_hbm, buf, sems) = refs[:QUAD], refs[QUAD:-4], refs[-4:]
    width = group * HEAD_DIM
    place = place_ref[0] & (QUAD - 1)
    scale = lax.rsqrt(functools.reduce(jnp.add, (ref[...] for ref in share_refs)) / full_width + EPSILON)
    copies = []
    for r in range(QUAD):
        cols = pl.ds(pl.multiple_of((place ^ r) * width, width), width)
        x = jnp.transpose(total_refs[r][...] * scale, (1, 0))
        buf[r] = (x * gain_ref[:, cols]).astype(BF16)
        copies.append(pltpu.make_async_copy(buf.at[r], out_hbm.at[:, cols], sems.at[r]))
        copies[-1].start()
    for copy in copies:
        copy.wait()


def local(queries, keys, values, level_weights, norm_gain):
    rows, width = queries.shape
    group = width // HEAD_DIM // QUAD
    local_bits = (rows // STRETCH).bit_length() - 1
    seq_bits = lax.axis_size("seq").bit_length() - 1
    full_width = width * lax.axis_size("head")
    position = lax.axis_index("seq").astype(jnp.int32)
    place = position.reshape(1)
    sds = jax.ShapeDtypeStruct
    block = (group, HEAD_DIM, HEAD_DIM)
    half = (2 * group, HEAD_DIM, HEAD_DIM)
    panel = (rows, group * HEAD_DIM)
    part_shape = sds((group * HEAD_DIM, rows), F32)

    k_all, v_all, even, one, two, three, even_sent = pl.pallas_call(
        functools.partial(states_kernel, group),
        out_shape=(sds((QUAD,) + panel, BF16),) * 2 + (sds(half, F32),) + (sds(block, BF16),) * 3 + (sds(half, BF16),),
        in_specs=[SMEM, HBM, HBM],
        out_specs=(VMEM,) * 7,
        scratch_shapes=[pltpu.SemaphoreType.DMA((2, QUAD))],
        compiler_params=params(STATES_GRANT),
        cost_estimate=cost(2 * rows * width * HEAD_DIM, 4 * rows * width),
        name="states",
    )(place, keys, values)

    taken3 = exchanged_in(three, 3, lambda quad, quads: quad < quads - 1)
    taken1 = exchanged(one, "seq", 1)
    taken2 = exchanged_in(two, 2, lambda quad, quads: quad < quads - 1)
    near2, near_odd = exchanged(three, "seq", 1), exchanged(even_sent, "seq", 1)

    totals = {}
    for number, groups in enumerate(((3, 1), (2, 0))):
        extra = [norm_gain.reshape(1, width)] if number == 0 else []
        outs = pl.pallas_call(
            functools.partial(intra_kernel, group, groups),
            out_shape=(sds((1, width), F32),) * len(extra) + (part_shape,) * len(groups),
            in_specs=[SMEM] + [VMEM] * (4 + len(extra)),
            out_specs=(VMEM,) * (len(extra) + len(groups)),
            compiler_params=params(),
            cost_estimate=cost(3 * rows * STRETCH * width, 2 * rows * width),
            name="intra",
        )(place, queries, level_weights, k_all, v_all, *extra)
        if extra:
            gain, *outs = outs
        totals |= dict(zip(groups, outs))

    sums, *running = pl.pallas_call(
        functools.partial(sums_kernel, group),
        out_shape=(sds(block, BF16),) + (sds(block, F32),) * (seq_bits > 3),
        in_specs=[VMEM] * 4,
        out_specs=(VMEM,) * (1 + (seq_bits > 3)),
        compiler_params=params(),
        cost_estimate=cost(4 * group * HEAD_DIM**2, 16 * group * HEAD_DIM**2),
        name="sums",
    )(even, taken1, taken2, taken3)
    upper = []
    for bit in range(2, seq_bits):
        if bit > 2:
            running = [running[0] + upper[-1].astype(F32)]
            sums = running[0].astype(BF16)
        upper.append(exchanged(sums, "seq", 1 << bit))
    pair = pl.pallas_call(
        functools.partial(pair_kernel, group),
        out_shape=sds(half, BF16),
        in_specs=[VMEM] * 3,
        out_specs=VMEM,
        compiler_params=params(),
        cost_estimate=cost(2 * group * HEAD_DIM**2, 16 * group * HEAD_DIM**2),
        name="pair",
    )(even, taken1, near2)
    middle = exchanged(pair, "seq", 2), exchanged(pair, "seq", 3)
    top = jnp.concatenate(upper, axis=0) if len(upper) > 1 else upper[0]
    tops = {0: top} | {r: exchanged_in(top, r, lambda quad, quads: quad > 0) for r in (3, 1, 2)}

    def top_reads(ref):
        return tuple((bit, ref, (bit - 2) * group) for bit in range(2, seq_bits))

    def readout(work, states, squares, finish=False):
        n, carry = len(work), squares is not None
        kernel = functools.partial(readout_kernel, group, 1 + local_bits, work, len(states), carry, finish)
        ins = [place, queries, level_weights, *states, *(totals[r] for r, _, _ in work)] + [squares] * carry
        shapes = [part_shape] * n + [sds((1 if finish else 8, rows), F32)]
        outs = pl.pallas_call(
            kernel,
            out_shape=tuple(shapes),
            in_specs=[SMEM] + [VMEM] * (len(ins) - 1),
            out_specs=(VMEM,) * len(shapes),
            compiler_params=params(),
            cost_estimate=cost(n * rows * width * HEAD_DIM, 2 * n * rows * width),
        )(*ins)
        totals.update({r: out for (r, _, _), out in zip(work, outs)})
        return outs[n]

    bit0 = {0: (0, 0, 0), 2: (0, 1, 0), 1: (0, 2, 0), 3: (0, 2, group)}
    bit1 = {r: (1, 3 + r % 2, (1 - r // 2) * group) for r in range(QUAD)}
    work = tuple((r, r == 0, (bit0[r], bit1[r]) + (top_reads(5) if r == 0 else ())) for r in (3, 1, 2, 0))
    squares = readout(work, (taken1, near2, near_odd, *middle, top), None)
    squares = readout(((3, True, top_reads(0)), (1, True, top_reads(1))), (tops[3], tops[1]), squares)
    squares = readout(((2, True, top_reads(0)),), (tops[2],), squares, finish=True)

    shares = [squares] + [exchanged(squares, "head", mask) for mask in range(1, lax.axis_size("head"))]

    return pl.pallas_call(
        functools.partial(norm_kernel, group, full_width),
        out_shape=sds((rows, width), BF16),
        in_specs=[SMEM] + [VMEM] * (QUAD + len(shares) + 1),
        out_specs=ANY,
        scratch_shapes=[pltpu.VMEM((QUAD,) + panel, BF16), pltpu.SemaphoreType.DMA((QUAD,))],
        compiler_params=params(),
        cost_estimate=cost(2 * rows * width, 2 * rows * width),
        name="norm",
    )(place, *(totals[r] for r in range(QUAD)), *shares, gain)


def solution(mesh):
    return jax.shard_map(
        local,
        mesh=mesh,
        in_specs=(P("seq", "head"), P("seq", "head"), P("seq", "head"), P(None, "head", "seq"), P("head")),
        out_specs=P("seq", "head"),
        check_vma=False,
    )
```

```python
import functools

import jax
import jax.numpy as jnp
from jax import lax
from jax.experimental import pallas as pl
from jax.experimental.pallas import tpu as pltpu
from jax.sharding import PartitionSpec as P


HEAD_DIM = 128
STRETCH = 256
EPSILON = 1e-06
QUAD = 4
F32 = jnp.float32
BF16 = jnp.bfloat16
VMEM = pl.BlockSpec(memory_space=pltpu.VMEM)
SMEM = pl.BlockSpec(memory_space=pltpu.SMEM)
ANY = pl.BlockSpec(memory_space=pl.ANY)
HBM = pl.BlockSpec(memory_space=pltpu.HBM)
GRANT = 24 << 20
TILE = 256
STATES_GRANT = 51968 << 10


def params(grant=GRANT):
    return pltpu.CompilerParams(vmem_limit_bytes=grant)


def cost(flops, moved):
    return pl.CostEstimate(flops=flops, bytes_accessed=moved, transcendentals=0)


def exchanged(block, axis, mask):
    count = lax.axis_size(axis)
    return lax.ppermute(block, axis, [(i, i ^ mask) for i in range(count)])


def exchanged_in(block, mask, real):
    seq, head = lax.axis_size("seq"), lax.axis_size("head")
    route = []
    for s in range(seq):
        for h in range(head):
            to = (s ^ mask, h) if real(s, seq) else (s, h ^ 1)
            route.append((s * head + h, to[0] * head + to[1]))
    return lax.ppermute(block, ("seq", "head"), route)


def nt(a, b):
    return lax.dot_general(a, b, (((1,), (1,)), ((), ())), preferred_element_type=F32)


def tn(a, b):
    return lax.dot_general(a, b, (((0,), (0,)), ((), ())), preferred_element_type=F32)


def column(head):
    return pl.ds(head * HEAD_DIM, HEAD_DIM)


def states_kernel(group, place_ref, k_hbm, v_hbm, k_ref, v_ref, own_ref, one_ref, two_ref, three_ref, rest_ref, sems):
    width = group * HEAD_DIM
    place = place_ref[0] & (QUAD - 1)
    order = (3, 1, 2, 0)
    copies = {}
    for r in order:
        cols = pl.ds(pl.multiple_of((place ^ r) * width, width), width)
        copies[r] = (
            pltpu.make_async_copy(k_hbm.at[:, cols], k_ref.at[r], sems.at[0, r]),
            pltpu.make_async_copy(v_hbm.at[:, cols], v_ref.at[r], sems.at[1, r]),
        )
        for copy in copies[r]:
            copy.start()
    sent = {1: one_ref, 2: two_ref, 3: three_ref}
    spot = {0: 0, 3: 1, 2: 2}
    for r in order:
        for copy in copies[r]:
            copy.wait()
        for j in range(group):
            state = tn(v_ref[r, :, column(j)], k_ref[r, :, column(j)])
            if r == 0:
                own_ref[j] = state
            else:
                sent[r][j] = state.astype(BF16)
            if r in spot:
                rest_ref[spot[r] * group + j] = state.astype(BF16)


def sums_kernel(own_ref, one_ref, two_ref, three_ref, sent_ref, *total_refs):
    total = own_ref[...] + one_ref[...].astype(F32) + two_ref[...].astype(F32) + three_ref[...].astype(F32)
    for total_ref in total_refs:
        total_ref[...] = total
    sent_ref[...] = total.astype(BF16)


def left_kernel(seq, place_ref, own_ref, one_ref, early2_ref, early3_ref, late2_ref, late3_ref, left_ref):
    last_quad = place_ref[0] >= seq - QUAD
    two = jnp.where(last_quad, late2_ref[...], early2_ref[...])
    three = jnp.where(last_quad, late3_ref[...], early3_ref[...])
    pair = own_ref[...] + one_ref[...].astype(F32)
    other = two.astype(F32) + three.astype(F32)
    left_ref[...] = jnp.where(place_ref[0] >> 1 & 1 == 1, other, pair).astype(BF16)


def intra_kernel(group, groups, place_ref, q_ref, w_ref, k_all, v_all, *refs):
    out_refs = refs[-len(groups) :]
    if len(refs) > len(groups):
        gain_ref, kept_ref = refs[:2]
        kept_ref[...] = gain_ref[...]
    count = q_ref.shape[0] // STRETCH
    local_bits = count.bit_length() - 1
    place = place_ref[0] & (QUAD - 1)
    causal = lax.broadcasted_iota(jnp.int32, (STRETCH, STRETCH), 0) <= lax.broadcasted_iota(
        jnp.int32, (STRETCH, STRETCH), 1
    )
    for r, out_ref in zip(groups, out_refs):
        for j in range(group):
            head = (place ^ r) * group + j
            cols = pl.ds(pl.multiple_of(head * HEAD_DIM, HEAD_DIM), HEAD_DIM)
            states = []
            for c in range(count):
                here = slice(c * STRETCH, (c + 1) * STRETCH)
                q, k, v = q_ref[here, cols], k_all[r, here, column(j)], v_all[r, here, column(j)]
                probs = jnp.where(causal, nt(k, q), 0.0).astype(BF16)
                total = w_ref[0, pl.ds(head, 1), here] * tn(v, probs)
                for bit in range(local_bits):
                    if c >> bit & 1:
                        low = (c >> bit + 1) << bit + 1
                        left = functools.reduce(jnp.add, states[low : low + (1 << bit)])
                        total += w_ref[1 + bit, pl.ds(head, 1), here] * nt(left.astype(BF16), q)
                out_ref[column(j), here] = total
                if c + 1 < count:
                    states.append(tn(v, k))


def readout_kernel(group, first, work, n_states, carry, finish, place_ref, q_ref, w_ref, *refs):
    n = len(work)
    state_refs, total_refs, refs = refs[:n_states], refs[n_states : n_states + n], refs[n_states + n :]
    carried_ref = refs[0] if carry else None
    out_refs, squares_ref = refs[carry : carry + n], refs[carry + n]
    rows = q_ref.shape[0]
    place = place_ref[0]
    for t in range(0, rows, TILE):
        here = slice(t, t + TILE)
        squares = carried_ref[:, here] if carry else jnp.zeros((8, TILE), F32)
        for (r, complete, reads), total_ref, out_ref in zip(work, total_refs, out_refs):
            for j in range(group):
                head = (place & (QUAD - 1) ^ r) * group + j
                q = q_ref[here, pl.ds(pl.multiple_of(head * HEAD_DIM, HEAD_DIM), HEAD_DIM)]
                total = total_ref[column(j), here]
                for bit, ref, slot in reads:
                    row = w_ref[first + bit, pl.ds(head, 1), here]
                    row = jnp.where(place >> bit & 1 == 1, row, 0.0)
                    total += row * nt(state_refs[ref][slot + j], q)
                out_ref[column(j), here] = total
                if complete:
                    squares += jnp.sum((total * total).reshape(HEAD_DIM // 8, 8, TILE), axis=0)
        squares_ref[:, here] = jnp.sum(squares, axis=0, keepdims=True) if finish else squares


def norm_kernel(group, full_width, place_ref, *refs):
    total_refs, share_refs, (gain_ref, out_hbm, buf, sems) = refs[:QUAD], refs[QUAD:-4], refs[-4:]
    width = group * HEAD_DIM
    place = place_ref[0] & (QUAD - 1)
    scale = lax.rsqrt(functools.reduce(jnp.add, (ref[...] for ref in share_refs)) / full_width + EPSILON)
    copies = []
    for r in range(QUAD):
        cols = pl.ds(pl.multiple_of((place ^ r) * width, width), width)
        x = jnp.transpose(total_refs[r][...] * scale, (1, 0))
        buf[r] = (x * gain_ref[:, cols]).astype(BF16)
        copies.append(pltpu.make_async_copy(buf.at[r], out_hbm.at[:, cols], sems.at[r]))
        copies[-1].start()
    for copy in copies:
        copy.wait()


def local(queries, keys, values, level_weights, norm_gain):
    rows, width = queries.shape
    group = width // HEAD_DIM // QUAD
    local_bits = (rows // STRETCH).bit_length() - 1
    seq_bits = lax.axis_size("seq").bit_length() - 1
    full_width = width * lax.axis_size("head")
    position = lax.axis_index("seq").astype(jnp.int32)
    place = position.reshape(1)
    sds = jax.ShapeDtypeStruct
    block = (group, HEAD_DIM, HEAD_DIM)
    others = (3 * group, HEAD_DIM, HEAD_DIM)
    panel = (rows, group * HEAD_DIM)
    part_shape = sds((group * HEAD_DIM, rows), F32)

    k_all, v_all, own, one, two, three, rest = pl.pallas_call(
        functools.partial(states_kernel, group),
        out_shape=(sds((QUAD,) + panel, BF16),) * 2 + (sds(block, F32),) + (sds(block, BF16),) * 3 + (sds(others, BF16),),
        in_specs=[SMEM, HBM, HBM],
        out_specs=(VMEM,) * 7,
        scratch_shapes=[pltpu.SemaphoreType.DMA((2, QUAD))],
        compiler_params=params(STATES_GRANT),
        cost_estimate=cost(2 * rows * width * HEAD_DIM, 4 * rows * width),
        name="states",
    )(place, keys, values)

    early3 = exchanged_in(three, 3, lambda s, seq: s < seq - QUAD)
    taken1 = exchanged(one, "seq", 1)
    early2 = exchanged_in(two, 2, lambda s, seq: s < seq - QUAD)
    late3 = exchanged_in(three, 3, lambda s, seq: s >= seq - QUAD)
    late2 = exchanged_in(two, 2, lambda s, seq: s >= seq - QUAD)
    near = exchanged(rest, "seq", 1)

    totals = {}
    for number, groups in enumerate(((3, 1), (2, 0))):
        extra = [norm_gain.reshape(1, width)] if number == 0 else []
        outs = pl.pallas_call(
            functools.partial(intra_kernel, group, groups),
            out_shape=(sds((1, width), F32),) * len(extra) + (part_shape,) * len(groups),
            in_specs=[SMEM] + [VMEM] * (4 + len(extra)),
            out_specs=(VMEM,) * (len(extra) + len(groups)),
            compiler_params=params(),
            cost_estimate=cost(3 * rows * STRETCH * width, 2 * rows * width),
            name="intra",
        )(place, queries, level_weights, k_all, v_all, *extra)
        if extra:
            gain, *outs = outs
        totals |= dict(zip(groups, outs))

    sums, *running = pl.pallas_call(
        sums_kernel,
        out_shape=(sds(block, BF16),) + (sds(block, F32),) * (seq_bits > 3),
        in_specs=[VMEM] * 4,
        out_specs=(VMEM,) * (1 + (seq_bits > 3)),
        compiler_params=params(),
        cost_estimate=cost(4 * group * HEAD_DIM**2, 16 * group * HEAD_DIM**2),
        name="sums",
    )(own, taken1, early2, early3)
    upper = []
    for bit in range(2, seq_bits):
        if bit > 2:
            running = [running[0] + upper[-1].astype(F32)]
            sums = running[0].astype(BF16)
        upper.append(exchanged(sums, "seq", 1 << bit))
    left_pair = pl.pallas_call(
        functools.partial(left_kernel, lax.axis_size("seq")),
        out_shape=sds(block, BF16),
        in_specs=[SMEM] + [VMEM] * 6,
        out_specs=VMEM,
        compiler_params=params(),
        cost_estimate=cost(4 * group * HEAD_DIM**2, 16 * group * HEAD_DIM**2),
        name="left",
    )(place, own, taken1, early2, early3, late2, late3)
    top = jnp.concatenate(upper, axis=0) if len(upper) > 1 else upper[0]
    tops = {0: top} | {r: exchanged_in(top, r, lambda s, seq: s >= QUAD) for r in (3, 1, 2)}

    middle = {0: left_pair} | {r: exchanged(left_pair, "seq", r) for r in (3, 2)}
    middle[1] = exchanged_in(left_pair, 1, lambda s, seq: s >> 1 & 1 == 1)

    def top_reads(ref):
        return tuple((bit, ref, (bit - 2) * group) for bit in range(2, seq_bits))

    def readout(work, states, squares, finish=False):
        n, carry = len(work), squares is not None
        kernel = functools.partial(readout_kernel, group, 1 + local_bits, work, len(states), carry, finish)
        ins = [place, queries, level_weights, *states, *(totals[r] for r, _, _ in work)] + [squares] * carry
        shapes = [part_shape] * n + [sds((1 if finish else 8, rows), F32)]
        outs = pl.pallas_call(
            kernel,
            out_shape=tuple(shapes),
            in_specs=[SMEM] + [VMEM] * (len(ins) - 1),
            out_specs=(VMEM,) * len(shapes),
            compiler_params=params(),
            cost_estimate=cost(n * rows * width * HEAD_DIM, 2 * n * rows * width),
        )(*ins)
        totals.update({r: out for (r, _, _), out in zip(work, outs)})
        return outs[n]

    below = {0: ((0, 0, 0), (1, 2, 0))} | {r: ((0, 1, (r - 1) * group), (1, 2 + r, 0)) for r in (1, 2, 3)}
    work = tuple((r, r == 0, below[r] + (top_reads(6) if r == 0 else ())) for r in (3, 1, 2, 0))
    squares = readout(work, (taken1, near, *(middle[r] for r in range(QUAD)), top), None)
    squares = readout(((3, True, top_reads(0)), (1, True, top_reads(1))), (tops[3], tops[1]), squares)
    squares = readout(((2, True, top_reads(0)),), (tops[2],), squares, finish=True)

    shares = [squares] + [exchanged(squares, "head", mask) for mask in range(1, lax.axis_size("head"))]

    return pl.pallas_call(
        functools.partial(norm_kernel, group, full_width),
        out_shape=sds((rows, width), BF16),
        in_specs=[SMEM] + [VMEM] * (QUAD + len(shares) + 1),
        out_specs=ANY,
        scratch_shapes=[pltpu.VMEM((QUAD,) + panel, BF16), pltpu.SemaphoreType.DMA((QUAD,))],
        compiler_params=params(),
        cost_estimate=cost(2 * rows * width, 2 * rows * width),
        name="norm",
    )(place, *(totals[r] for r in range(QUAD)), *shares, gain)


def solution(mesh):
    return jax.shard_map(
        local,
        mesh=mesh,
        in_specs=(P("seq", "head"), P("seq", "head"), P("seq", "head"), P(None, "head", "seq"), P("head")),
        out_specs=P("seq", "head"),
        check_vma=False,
    )
```

```python
import functools

import jax
import jax.numpy as jnp
from jax import lax
from jax.experimental import pallas as pl
from jax.experimental.pallas import tpu as pltpu
from jax.sharding import PartitionSpec as P


HEAD_DIM = 128
STRETCH = 256
EPSILON = 1e-06
QUAD = 4
F32 = jnp.float32
BF16 = jnp.bfloat16
VMEM = pl.BlockSpec(memory_space=pltpu.VMEM)
SMEM = pl.BlockSpec(memory_space=pltpu.SMEM)
ANY = pl.BlockSpec(memory_space=pl.ANY)
HBM = pl.BlockSpec(memory_space=pltpu.HBM)
GRANT = 24 << 20
TILE = 256
STATES_GRANT = 51968 << 10


def params(grant=GRANT):
    return pltpu.CompilerParams(vmem_limit_bytes=grant)


def cost(flops, moved):
    return pl.CostEstimate(flops=flops, bytes_accessed=moved, transcendentals=0)


def exchanged(block, axis, mask):
    count = lax.axis_size(axis)
    return lax.ppermute(block, axis, [(i, i ^ mask) for i in range(count)])


def exchanged_in(block, mask, real):
    seq, head = lax.axis_size("seq"), lax.axis_size("head")
    route = []
    for s in range(seq):
        for h in range(head):
            to = (s ^ mask, h) if real(s, seq) else (s, h ^ 1)
            route.append((s * head + h, to[0] * head + to[1]))
    return lax.ppermute(block, ("seq", "head"), route)


def nt(a, b):
    return lax.dot_general(a, b, (((1,), (1,)), ((), ())), preferred_element_type=F32)


def tn(a, b):
    return lax.dot_general(a, b, (((0,), (0,)), ((), ())), preferred_element_type=F32)


def column(head):
    return pl.ds(head * HEAD_DIM, HEAD_DIM)


def states_kernel(group, place_ref, k_hbm, v_hbm, k_ref, v_ref, own_ref, one_ref, two_ref, three_ref, rest_ref, sems):
    width = group * HEAD_DIM
    place = place_ref[0] & (QUAD - 1)
    order = (3, 1, 2, 0)
    copies = {}
    for r in order:
        cols = pl.ds(pl.multiple_of((place ^ r) * width, width), width)
        copies[r] = (
            pltpu.make_async_copy(k_hbm.at[:, cols], k_ref.at[r], sems.at[0, r]),
            pltpu.make_async_copy(v_hbm.at[:, cols], v_ref.at[r], sems.at[1, r]),
        )
        for copy in copies[r]:
            copy.start()
    sent = {1: one_ref, 2: two_ref, 3: three_ref}
    spot = {0: 0, 3: 1, 2: 2}
    for r in order:
        for copy in copies[r]:
            copy.wait()
        for j in range(group):
            state = tn(v_ref[r, :, column(j)], k_ref[r, :, column(j)])
            if r == 0:
                own_ref[j] = state
            else:
                sent[r][j] = state.astype(BF16)
            if r in spot:
                rest_ref[spot[r] * group + j] = state.astype(BF16)


def sums_kernel(own_ref, one_ref, two_ref, three_ref, sent_ref, *total_refs):
    total = own_ref[...] + one_ref[...].astype(F32) + two_ref[...].astype(F32) + three_ref[...].astype(F32)
    for total_ref in total_refs:
        total_ref[...] = total
    sent_ref[...] = total.astype(BF16)


def left_kernel(seq, place_ref, own_ref, one_ref, early2_ref, early3_ref, late2_ref, late3_ref, left_ref):
    last_quad = place_ref[0] >= seq - QUAD
    two = jnp.where(last_quad, late2_ref[...], early2_ref[...])
    three = jnp.where(last_quad, late3_ref[...], early3_ref[...])
    pair = own_ref[...] + one_ref[...].astype(F32)
    other = two.astype(F32) + three.astype(F32)
    left_ref[...] = jnp.where(place_ref[0] >> 1 & 1 == 1, other, pair).astype(BF16)


def intra_kernel(group, groups, place_ref, q_ref, w_ref, k_all, v_all, *refs):
    out_refs = refs[-len(groups) :]
    if len(refs) > len(groups):
        gain_ref, column_ref = refs[:2]
        heads = gain_ref.shape[1] // HEAD_DIM
        for head in range(heads):
            rows = jnp.broadcast_to(gain_ref[:, column(head)], (HEAD_DIM, HEAD_DIM))
            column_ref[column(head), :] = jnp.transpose(rows, (1, 0))
    count = q_ref.shape[0] // STRETCH
    local_bits = count.bit_length() - 1
    place = place_ref[0] & (QUAD - 1)
    causal = lax.broadcasted_iota(jnp.int32, (STRETCH, STRETCH), 0) <= lax.broadcasted_iota(
        jnp.int32, (STRETCH, STRETCH), 1
    )
    for r, out_ref in zip(groups, out_refs):
        for j in range(group):
            head = (place ^ r) * group + j
            cols = pl.ds(pl.multiple_of(head * HEAD_DIM, HEAD_DIM), HEAD_DIM)
            states = []
            for c in range(count):
                here = slice(c * STRETCH, (c + 1) * STRETCH)
                q, k, v = q_ref[here, cols], k_all[r, here, column(j)], v_all[r, here, column(j)]
                probs = jnp.where(causal, nt(k, q), 0.0).astype(BF16)
                total = w_ref[0, pl.ds(head, 1), here] * tn(v, probs)
                for bit in range(local_bits):
                    if c >> bit & 1:
                        low = (c >> bit + 1) << bit + 1
                        left = functools.reduce(jnp.add, states[low : low + (1 << bit)])
                        total += w_ref[1 + bit, pl.ds(head, 1), here] * nt(left.astype(BF16), q)
                out_ref[column(j), here] = total
                if c + 1 < count:
                    states.append(tn(v, k))


def readout_kernel(group, first, work, n_states, carry, finish, place_ref, q_ref, w_ref, *refs):
    n = len(work)
    state_refs, total_refs, refs = refs[:n_states], refs[n_states : n_states + n], refs[n_states + n :]
    carried_ref = refs[0] if carry else None
    out_refs, squares_ref = refs[carry : carry + n], refs[carry + n]
    rows = q_ref.shape[0]
    place = place_ref[0]
    for t in range(0, rows, TILE):
        here = slice(t, t + TILE)
        squares = carried_ref[:, here] if carry else jnp.zeros((8, TILE), F32)
        for (r, complete, reads), total_ref, out_ref in zip(work, total_refs, out_refs):
            for j in range(group):
                head = (place & (QUAD - 1) ^ r) * group + j
                q = q_ref[here, pl.ds(pl.multiple_of(head * HEAD_DIM, HEAD_DIM), HEAD_DIM)]
                total = total_ref[column(j), here]
                for bit, ref, slot in reads:
                    row = w_ref[first + bit, pl.ds(head, 1), here]
                    row = jnp.where(place >> bit & 1 == 1, row, 0.0)
                    total += row * nt(state_refs[ref][slot + j], q)
                out_ref[column(j), here] = total
                if complete:
                    squares += jnp.sum((total * total).reshape(HEAD_DIM // 8, 8, TILE), axis=0)
        squares_ref[:, here] = jnp.sum(squares, axis=0, keepdims=True) if finish else squares


def norm_kernel(group, full_width, place_ref, *refs):
    total_refs, share_refs, (gain_ref, out_hbm, buf, sems) = refs[:QUAD], refs[QUAD:-4], refs[-4:]
    place = place_ref[0] & (QUAD - 1)
    rows = buf.shape[0]
    scale = lax.rsqrt(functools.reduce(jnp.add, (ref[...] for ref in share_refs)) / full_width + EPSILON)
    copies = []
    for r in range(QUAD):
        for j in range(group):
            start = pl.multiple_of(((place ^ r) * group + j) * HEAD_DIM, HEAD_DIM)
            here = pl.ds(start, HEAD_DIM)
            gain = jnp.concatenate([gain_ref[here, :]] * (rows // HEAD_DIM), axis=1)
            x = (total_refs[r][column(j), :] * scale * gain).astype(BF16)
            spot = column(r * group + j)
            buf[:, spot] = jnp.transpose(x, (1, 0))
            copies.append(pltpu.make_async_copy(buf.at[:, spot], out_hbm.at[:, here], sems.at[r * group + j]))
            copies[-1].start()
    for copy in copies:
        copy.wait()


def local(queries, keys, values, level_weights, norm_gain):
    rows, width = queries.shape
    group = width // HEAD_DIM // QUAD
    local_bits = (rows // STRETCH).bit_length() - 1
    seq_bits = lax.axis_size("seq").bit_length() - 1
    full_width = width * lax.axis_size("head")
    position = lax.axis_index("seq").astype(jnp.int32)
    place = position.reshape(1)
    sds = jax.ShapeDtypeStruct
    block = (group, HEAD_DIM, HEAD_DIM)
    others = (3 * group, HEAD_DIM, HEAD_DIM)
    panel = (rows, group * HEAD_DIM)
    part_shape = sds((group * HEAD_DIM, rows), F32)

    k_all, v_all, own, one, two, three, rest = pl.pallas_call(
        functools.partial(states_kernel, group),
        out_shape=(sds((QUAD,) + panel, BF16),) * 2 + (sds(block, F32),) + (sds(block, BF16),) * 3 + (sds(others, BF16),),
        in_specs=[SMEM, HBM, HBM],
        out_specs=(VMEM,) * 7,
        scratch_shapes=[pltpu.SemaphoreType.DMA((2, QUAD))],
        compiler_params=params(STATES_GRANT),
        cost_estimate=cost(2 * rows * width * HEAD_DIM, 4 * rows * width),
        name="states",
    )(place, keys, values)

    early3 = exchanged_in(three, 3, lambda s, seq: s < seq - QUAD)
    taken1 = exchanged(one, "seq", 1)
    early2 = exchanged_in(two, 2, lambda s, seq: s < seq - QUAD)
    late3 = exchanged_in(three, 3, lambda s, seq: s >= seq - QUAD)
    late2 = exchanged_in(two, 2, lambda s, seq: s >= seq - QUAD)
    near = exchanged(rest, "seq", 1)

    totals = {}
    for number, groups in enumerate(((3,), (1, 2, 0))):
        extra = [norm_gain.reshape(1, width)] if number == 1 else []
        outs = pl.pallas_call(
            functools.partial(intra_kernel, group, groups),
            out_shape=(sds((width, HEAD_DIM), F32),) * len(extra) + (part_shape,) * len(groups),
            in_specs=[SMEM] + [VMEM] * (4 + len(extra)),
            out_specs=(VMEM,) * (len(extra) + len(groups)),
            compiler_params=params(),
            cost_estimate=cost(3 * rows * STRETCH * width, 2 * rows * width),
            name="intra",
        )(place, queries, level_weights, k_all, v_all, *extra)
        if extra:
            gain, *outs = outs
        totals |= dict(zip(groups, outs))

    sums, *running = pl.pallas_call(
        sums_kernel,
        out_shape=(sds(block, BF16),) + (sds(block, F32),) * (seq_bits > 3),
        in_specs=[VMEM] * 4,
        out_specs=(VMEM,) * (1 + (seq_bits > 3)),
        compiler_params=params(),
        cost_estimate=cost(4 * group * HEAD_DIM**2, 16 * group * HEAD_DIM**2),
        name="sums",
    )(own, taken1, early2, early3)
    upper = []
    for bit in range(2, seq_bits):
        if bit > 2:
            running = [running[0] + upper[-1].astype(F32)]
            sums = running[0].astype(BF16)
        upper.append(exchanged(sums, "seq", 1 << bit))
    left_pair = pl.pallas_call(
        functools.partial(left_kernel, lax.axis_size("seq")),
        out_shape=sds(block, BF16),
        in_specs=[SMEM] + [VMEM] * 6,
        out_specs=VMEM,
        compiler_params=params(),
        cost_estimate=cost(4 * group * HEAD_DIM**2, 16 * group * HEAD_DIM**2),
        name="left",
    )(place, own, taken1, early2, early3, late2, late3)
    top = jnp.concatenate(upper, axis=0) if len(upper) > 1 else upper[0]
    tops = {0: top} | {r: exchanged_in(top, r, lambda s, seq: s >= QUAD) for r in (3, 1, 2)}

    middle = {0: left_pair} | {r: exchanged(left_pair, "seq", r) for r in (3, 2)}
    middle[1] = exchanged_in(left_pair, 1, lambda s, seq: s >> 1 & 1 == 1)

    def top_reads(ref):
        return tuple((bit, ref, (bit - 2) * group) for bit in range(2, seq_bits))

    def readout(work, states, squares, finish=False):
        n, carry = len(work), squares is not None
        kernel = functools.partial(readout_kernel, group, 1 + local_bits, work, len(states), carry, finish)
        ins = [place, queries, level_weights, *states, *(totals[r] for r, _, _ in work)] + [squares] * carry
        shapes = [part_shape] * n + [sds((1 if finish else 8, rows), F32)]
        outs = pl.pallas_call(
            kernel,
            out_shape=tuple(shapes),
            in_specs=[SMEM] + [VMEM] * (len(ins) - 1),
            out_specs=(VMEM,) * len(shapes),
            compiler_params=params(),
            cost_estimate=cost(n * rows * width * HEAD_DIM, 2 * n * rows * width),
        )(*ins)
        totals.update({r: out for (r, _, _), out in zip(work, outs)})
        return outs[n]

    below = {0: ((0, 0, 0), (1, 2, 0))} | {r: ((0, 1, (r - 1) * group), (1, 2 + r, 0)) for r in (1, 2, 3)}
    work = tuple((r, r == 0, below[r] + (top_reads(6) if r == 0 else ())) for r in (3, 1, 2, 0))
    squares = readout(work, (taken1, near, *(middle[r] for r in range(QUAD)), top), None)
    squares = readout(((3, True, top_reads(0)), (1, True, top_reads(1))), (tops[3], tops[1]), squares)
    squares = readout(((2, True, top_reads(0)),), (tops[2],), squares, finish=True)

    shares = [squares] + [exchanged(squares, "head", mask) for mask in range(1, lax.axis_size("head"))]

    return pl.pallas_call(
        functools.partial(norm_kernel, group, full_width),
        out_shape=sds((rows, width), BF16),
        in_specs=[SMEM] + [VMEM] * (QUAD + len(shares) + 1),
        out_specs=ANY,
        scratch_shapes=[pltpu.VMEM((rows, width), BF16), pltpu.SemaphoreType.DMA((QUAD * group,))],
        compiler_params=params(),
        cost_estimate=cost(2 * rows * width, 2 * rows * width),
        name="norm",
    )(place, *(totals[r] for r in range(QUAD)), *shares, gain)


def solution(mesh):
    return jax.shard_map(
        local,
        mesh=mesh,
        in_specs=(P("seq", "head"), P("seq", "head"), P("seq", "head"), P(None, "head", "seq"), P("head")),
        out_specs=P("seq", "head"),
        check_vma=False,
    )
```

```python
import functools

import jax
import jax.numpy as jnp
from jax import lax
from jax.experimental import pallas as pl
from jax.experimental.pallas import tpu as pltpu
from jax.sharding import PartitionSpec as P


HEAD_DIM = 128
STRETCH = 256
EPSILON = 1e-06
QUAD = 4
F32 = jnp.float32
BF16 = jnp.bfloat16
VMEM = pl.BlockSpec(memory_space=pltpu.VMEM)
SMEM = pl.BlockSpec(memory_space=pltpu.SMEM)
ANY = pl.BlockSpec(memory_space=pl.ANY)
HBM = pl.BlockSpec(memory_space=pltpu.HBM)
GRANT = 24 << 20
TILE = 256
STATES_GRANT = 51968 << 10


def params(grant=GRANT):
    return pltpu.CompilerParams(vmem_limit_bytes=grant)


def cost(flops, moved):
    return pl.CostEstimate(flops=flops, bytes_accessed=moved, transcendentals=0)


def exchanged(block, axis, mask):
    count = lax.axis_size(axis)
    return lax.ppermute(block, axis, [(i, i ^ mask) for i in range(count)])


def exchanged_in(block, mask, real):
    seq, head = lax.axis_size("seq"), lax.axis_size("head")
    route = []
    for s in range(seq):
        for h in range(head):
            to = (s ^ mask, h) if real(s, seq) else (s, h ^ 1)
            route.append((s * head + h, to[0] * head + to[1]))
    return lax.ppermute(block, ("seq", "head"), route)


def nt(a, b):
    return lax.dot_general(a, b, (((1,), (1,)), ((), ())), preferred_element_type=F32)


def tn(a, b):
    return lax.dot_general(a, b, (((0,), (0,)), ((), ())), preferred_element_type=F32)


def column(head):
    return pl.ds(head * HEAD_DIM, HEAD_DIM)


def states_kernel(group, place_ref, k_hbm, v_hbm, k_ref, v_ref, own_ref, one_ref, two_ref, three_ref, rest_ref, sems):
    width = group * HEAD_DIM
    place = place_ref[0] & (QUAD - 1)
    order = (3, 1, 2, 0)
    copies = {}
    for r in order:
        cols = pl.ds(pl.multiple_of((place ^ r) * width, width), width)
        copies[r] = (
            pltpu.make_async_copy(k_hbm.at[:, cols], k_ref.at[r], sems.at[0, r]),
            pltpu.make_async_copy(v_hbm.at[:, cols], v_ref.at[r], sems.at[1, r]),
        )
        for copy in copies[r]:
            copy.start()
    sent = {1: one_ref, 2: two_ref, 3: three_ref}
    spot = {0: 0, 3: 1, 2: 2}
    for r in order:
        for copy in copies[r]:
            copy.wait()
        for j in range(group):
            state = tn(v_ref[r, :, column(j)], k_ref[r, :, column(j)])
            if r == 0:
                own_ref[j] = state
            else:
                sent[r][j] = state.astype(BF16)
            if r in spot:
                rest_ref[spot[r] * group + j] = state.astype(BF16)


def sums_kernel(own_ref, one_ref, two_ref, three_ref, sent_ref, *total_refs):
    total = own_ref[...] + one_ref[...].astype(F32) + two_ref[...].astype(F32) + three_ref[...].astype(F32)
    for total_ref in total_refs:
        total_ref[...] = total
    sent_ref[...] = total.astype(BF16)


def left_kernel(seq, place_ref, own_ref, one_ref, early2_ref, early3_ref, late2_ref, late3_ref, gain_ref, left_ref, kept_ref):
    kept_ref[...] = gain_ref[...]
    last_quad = place_ref[0] >= seq - QUAD
    two = jnp.where(last_quad, late2_ref[...], early2_ref[...])
    three = jnp.where(last_quad, late3_ref[...], early3_ref[...])
    pair = own_ref[...] + one_ref[...].astype(F32)
    other = two.astype(F32) + three.astype(F32)
    left_ref[...] = jnp.where(place_ref[0] >> 1 & 1 == 1, other, pair).astype(BF16)


def intra_of(group, place, q_ref, w_ref, k_all, v_all, out_refs):
    count = q_ref.shape[0] // STRETCH
    local_bits = count.bit_length() - 1
    causal = lax.broadcasted_iota(jnp.int32, (STRETCH, STRETCH), 0) <= lax.broadcasted_iota(
        jnp.int32, (STRETCH, STRETCH), 1
    )
    for r, out_ref in enumerate(out_refs):
        for j in range(group):
            head = (place & (QUAD - 1) ^ r) * group + j
            cols = pl.ds(pl.multiple_of(head * HEAD_DIM, HEAD_DIM), HEAD_DIM)
            states = []
            for c in range(count):
                here = slice(c * STRETCH, (c + 1) * STRETCH)
                q, k, v = q_ref[here, cols], k_all[r, here, column(j)], v_all[r, here, column(j)]
                probs = jnp.where(causal, nt(k, q), 0.0).astype(BF16)
                total = w_ref[0, pl.ds(head, 1), here] * tn(v, probs)
                for bit in range(local_bits):
                    if c >> bit & 1:
                        low = (c >> bit + 1) << bit + 1
                        left = functools.reduce(jnp.add, states[low : low + (1 << bit)])
                        total += w_ref[1 + bit, pl.ds(head, 1), here] * nt(left.astype(BF16), q)
                out_ref[column(j), here] = total
                if c + 1 < count:
                    states.append(tn(v, k))


def intra_early_kernel(group, place_ref, *refs):
    @pl.when(place_ref[0] < QUAD)
    def _():
        intra_of(group, place_ref[0], *refs[:4], refs[4:])


def intra_late_kernel(group, place_ref, q_ref, w_ref, k_all, v_all, gain_ref, *refs):
    done_refs, column_ref, out_refs = refs[:QUAD], refs[QUAD], refs[QUAD + 1 :]
    for head in range(QUAD * group):
        rows = jnp.broadcast_to(gain_ref[:, column(head)], (HEAD_DIM, HEAD_DIM))
        column_ref[column(head), :] = jnp.transpose(rows, (1, 0))

    @pl.when(place_ref[0] < QUAD)
    def _():
        for done_ref, out_ref in zip(done_refs, out_refs):
            out_ref[...] = done_ref[...]

    @pl.when(place_ref[0] >= QUAD)
    def _():
        intra_of(group, place_ref[0], q_ref, w_ref, k_all, v_all, out_refs)


def readout_of(group, first, work, n_states, carry, finish, place_ref, q_ref, w_ref, *refs):
    n = len(work)
    state_refs, total_refs, refs = refs[:n_states], refs[n_states : n_states + n], refs[n_states + n :]
    carried_ref = refs[0] if carry else None
    out_refs, squares_ref = refs[carry : carry + n], refs[carry + n]
    rows = q_ref.shape[0]
    place = place_ref[0]
    for t in range(0, rows, TILE):
        here = slice(t, t + TILE)
        squares = carried_ref[:, here] if carry else jnp.zeros((8, TILE), F32)
        for (r, complete, reads), total_ref, out_ref in zip(work, total_refs, out_refs):
            for j in range(group):
                head = (place & (QUAD - 1) ^ r) * group + j
                q = q_ref[here, pl.ds(pl.multiple_of(head * HEAD_DIM, HEAD_DIM), HEAD_DIM)]
                total = total_ref[column(j), here]
                for bit, ref, slot in reads:
                    row = w_ref[first + bit, pl.ds(head, 1), here]
                    row = jnp.where(place >> bit & 1 == 1, row, 0.0)
                    total += row * nt(state_refs[ref][slot + j], q)
                out_ref[column(j), here] = total
                if complete:
                    squares += jnp.sum((total * total).reshape(HEAD_DIM // 8, 8, TILE), axis=0)
        squares_ref[:, here] = jnp.sum(squares, axis=0, keepdims=True) if finish else squares


def readout_kernel(group, first, work, lacks, *args):
    low = any(bit < 2 for _, _, reads in work for bit, _, _ in reads)
    fewer = tuple((r, complete, tuple(read for read in reads if low and read[0] >= 2)) for r, complete, reads in work)
    place = args[3][0]
    for present, some in ((True, work), (False, fewer)):
        pl.when(lacks(place) != present)(functools.partial(readout_of, group, first, some, *args))


def norm_kernel(group, full_width, place_ref, *refs):
    total_refs, share_refs, (gain_ref, out_hbm, buf, sems) = refs[:QUAD], refs[QUAD:-4], refs[-4:]
    place = place_ref[0] & (QUAD - 1)
    rows = buf.shape[0]
    scale = lax.rsqrt(functools.reduce(jnp.add, (ref[...] for ref in share_refs)) / full_width + EPSILON)
    copies = []
    for r in range(QUAD):
        for j in range(group):
            start = pl.multiple_of(((place ^ r) * group + j) * HEAD_DIM, HEAD_DIM)
            here = pl.ds(start, HEAD_DIM)
            gain = jnp.concatenate([gain_ref[here, :]] * (rows // HEAD_DIM), axis=1)
            x = (total_refs[r][column(j), :] * scale * gain).astype(BF16)
            spot = column(r * group + j)
            buf[:, spot] = jnp.transpose(x, (1, 0))
            copies.append(pltpu.make_async_copy(buf.at[:, spot], out_hbm.at[:, here], sems.at[r * group + j]))
            copies[-1].start()
    for copy in copies:
        copy.wait()


def local(queries, keys, values, level_weights, norm_gain):
    rows, width = queries.shape
    group = width // HEAD_DIM // QUAD
    local_bits = (rows // STRETCH).bit_length() - 1
    seq_bits = lax.axis_size("seq").bit_length() - 1
    full_width = width * lax.axis_size("head")
    position = lax.axis_index("seq").astype(jnp.int32)
    place = position.reshape(1)
    sds = jax.ShapeDtypeStruct
    block = (group, HEAD_DIM, HEAD_DIM)
    others = (3 * group, HEAD_DIM, HEAD_DIM)
    panel = (rows, group * HEAD_DIM)
    part_shape = sds((group * HEAD_DIM, rows), F32)

    k_all, v_all, own, one, two, three, rest = pl.pallas_call(
        functools.partial(states_kernel, group),
        out_shape=(sds((QUAD,) + panel, BF16),) * 2 + (sds(block, F32),) + (sds(block, BF16),) * 3 + (sds(others, BF16),),
        in_specs=[SMEM, HBM, HBM],
        out_specs=(VMEM,) * 7,
        scratch_shapes=[pltpu.SemaphoreType.DMA((2, QUAD))],
        compiler_params=params(STATES_GRANT),
        cost_estimate=cost(2 * rows * width * HEAD_DIM, 4 * rows * width),
        name="states",
    )(place, keys, values)

    early3 = exchanged_in(three, 3, lambda s, seq: s < seq - QUAD)
    taken1 = exchanged(one, "seq", 1)
    early2 = exchanged_in(two, 2, lambda s, seq: s < seq - QUAD)
    late3 = exchanged_in(three, 3, lambda s, seq: s >= seq - QUAD)
    late2 = exchanged_in(two, 2, lambda s, seq: s >= seq - QUAD)
    near = exchanged(rest, "seq", 1)

    args = (place, queries, level_weights, k_all, v_all)
    work_cost = cost(6 * rows * STRETCH * width, 4 * rows * width)
    outs = pl.pallas_call(
        functools.partial(intra_early_kernel, group),
        out_shape=(part_shape,) * QUAD,
        in_specs=[SMEM] + [VMEM] * 4,
        out_specs=(VMEM,) * QUAD,
        compiler_params=params(),
        cost_estimate=work_cost,
        name="intra_early",
    )(*args)
    sums, *running = pl.pallas_call(
        sums_kernel,
        out_shape=(sds(block, BF16),) + (sds(block, F32),) * (seq_bits > 3),
        in_specs=[VMEM] * 4,
        out_specs=(VMEM,) * (1 + (seq_bits > 3)),
        compiler_params=params(),
        cost_estimate=cost(4 * group * HEAD_DIM**2, 16 * group * HEAD_DIM**2),
        name="sums",
    )(own, taken1, early2, early3)
    upper = []
    for bit in range(2, seq_bits):
        if bit > 2:
            running = [running[0] + upper[-1].astype(F32)]
            sums = running[0].astype(BF16)
        upper.append(exchanged(sums, "seq", 1 << bit))
    left_pair, gain = pl.pallas_call(
        functools.partial(left_kernel, lax.axis_size("seq")),
        out_shape=(sds(block, BF16), sds((1, width), F32)),
        in_specs=[SMEM] + [VMEM] * 7,
        out_specs=(VMEM,) * 2,
        compiler_params=params(),
        cost_estimate=cost(4 * group * HEAD_DIM**2, 16 * group * HEAD_DIM**2),
        name="left",
    )(place, own, taken1, early2, early3, late2, late3, norm_gain.reshape(1, width))
    top = jnp.concatenate(upper, axis=0) if len(upper) > 1 else upper[0]
    tops = {0: top} | {r: exchanged_in(top, r, lambda s, seq: s >= QUAD) for r in (3, 1, 2)}

    gain, *outs = pl.pallas_call(
        functools.partial(intra_late_kernel, group),
        out_shape=(sds((width, HEAD_DIM), F32),) + (part_shape,) * QUAD,
        in_specs=[SMEM] + [VMEM] * (5 + QUAD),
        out_specs=(VMEM,) * (1 + QUAD),
        compiler_params=params(),
        cost_estimate=work_cost,
        name="intra_late",
    )(*args, gain, *outs)
    totals = dict(enumerate(outs))

    middle = {0: left_pair} | {r: exchanged(left_pair, "seq", r) for r in (3, 2)}
    middle[1] = exchanged_in(left_pair, 1, lambda s, seq: s >> 1 & 1 == 1)

    def top_reads(ref):
        return tuple((bit, ref, (bit - 2) * group) for bit in range(2, seq_bits))

    def readout(label, work, states, squares, finish=False):
        n, carry = len(work), squares is not None

        def lacks(place):
            return place & (QUAD - 1) == 0 if label == "far" else place < QUAD

        kernel = functools.partial(readout_kernel, group, 1 + local_bits, work, lacks, len(states), carry, finish)
        ins = [place, queries, level_weights, *states, *(totals[r] for r, _, _ in work)] + [squares] * carry
        shapes = [part_shape] * n + [sds((1 if finish else 8, rows), F32)]
        outs = pl.pallas_call(
            kernel,
            out_shape=tuple(shapes),
            in_specs=[SMEM] + [VMEM] * (len(ins) - 1),
            out_specs=(VMEM,) * len(shapes),
            compiler_params=params(),
            cost_estimate=cost(n * rows * width * HEAD_DIM, 2 * n * rows * width),
        )(*ins)
        totals.update({r: out for (r, _, _), out in zip(work, outs)})
        return outs[n]

    below = {0: ((0, 0, 0), (1, 2, 0))} | {r: ((0, 1, (r - 1) * group), (1, 2 + r, 0)) for r in (1, 2, 3)}
    work = tuple((r, r == 0, below[r] + (top_reads(6) if r == 0 else ())) for r in (3, 1, 2, 0))
    squares = readout("far", work, (taken1, near, *(middle[r] for r in range(QUAD)), top), None)
    squares = readout("mid", ((3, True, top_reads(0)), (1, True, top_reads(1))), (tops[3], tops[1]), squares)
    squares = readout("last", ((2, True, top_reads(0)),), (tops[2],), squares, finish=True)

    shares = [squares] + [exchanged(squares, "head", mask) for mask in range(1, lax.axis_size("head"))]

    return pl.pallas_call(
        functools.partial(norm_kernel, group, full_width),
        out_shape=sds((rows, width), BF16),
        in_specs=[SMEM] + [VMEM] * (QUAD + len(shares) + 1),
        out_specs=ANY,
        scratch_shapes=[pltpu.VMEM((rows, width), BF16), pltpu.SemaphoreType.DMA((QUAD * group,))],
        compiler_params=params(),
        cost_estimate=cost(2 * rows * width, 2 * rows * width),
        name="norm",
    )(place, *(totals[r] for r in range(QUAD)), *shares, gain)


def solution(mesh):
    return jax.shard_map(
        local,
        mesh=mesh,
        in_specs=(P("seq", "head"), P("seq", "head"), P("seq", "head"), P(None, "head", "seq"), P("head")),
        out_specs=P("seq", "head"),
        check_vma=False,
    )
```

```python
import functools

import jax
import jax.numpy as jnp
from jax import lax
from jax.experimental import pallas as pl
from jax.experimental.pallas import tpu as pltpu
from jax.sharding import PartitionSpec as P


HEAD_DIM = 128
STRETCH = 256
EPSILON = 1e-06
QUAD = 4
F32 = jnp.float32
BF16 = jnp.bfloat16
VMEM = pl.BlockSpec(memory_space=pltpu.VMEM)
SMEM = pl.BlockSpec(memory_space=pltpu.SMEM)
ANY = pl.BlockSpec(memory_space=pl.ANY)
HBM = pl.BlockSpec(memory_space=pltpu.HBM)
GRANT = 24 << 20
TILE = 256
STATES_GRANT = 51968 << 10


def params(grant=GRANT):
    return pltpu.CompilerParams(vmem_limit_bytes=grant)


def cost(flops, moved):
    return pl.CostEstimate(flops=flops, bytes_accessed=moved, transcendentals=0)


def exchanged(block, axis, mask):
    count = lax.axis_size(axis)
    return lax.ppermute(block, axis, [(i, i ^ mask) for i in range(count)])


def exchanged_in(block, mask, real):
    seq, head = lax.axis_size("seq"), lax.axis_size("head")
    route = []
    for s in range(seq):
        for h in range(head):
            to = (s ^ mask, h) if real(s, seq) else (s, h ^ 1)
            route.append((s * head + h, to[0] * head + to[1]))
    return lax.ppermute(block, ("seq", "head"), route)


def nt(a, b):
    return lax.dot_general(a, b, (((1,), (1,)), ((), ())), preferred_element_type=F32)


def tn(a, b):
    return lax.dot_general(a, b, (((0,), (0,)), ((), ())), preferred_element_type=F32)


def column(head):
    return pl.ds(head * HEAD_DIM, HEAD_DIM)


def states_kernel(group, place_ref, k_hbm, v_hbm, k_ref, v_ref, own_ref, one_ref, two_ref, three_ref, rest_ref, sems):
    width = group * HEAD_DIM
    place = place_ref[0] & (QUAD - 1)
    order = (3, 1, 2, 0)
    copies = {}
    for r in order:
        cols = pl.ds(pl.multiple_of((place ^ r) * width, width), width)
        copies[r] = (
            pltpu.make_async_copy(k_hbm.at[:, cols], k_ref.at[r], sems.at[0, r]),
            pltpu.make_async_copy(v_hbm.at[:, cols], v_ref.at[r], sems.at[1, r]),
        )
        for copy in copies[r]:
            copy.start()
    sent = {1: one_ref, 2: two_ref, 3: three_ref}
    spot = {0: 0, 3: 1, 2: 2}
    for r in order:
        for copy in copies[r]:
            copy.wait()
        for j in range(group):
            state = tn(v_ref[r, :, column(j)], k_ref[r, :, column(j)])
            if r == 0:
                own_ref[j] = state
            else:
                sent[r][j] = state.astype(BF16)
            if r in spot:
                rest_ref[spot[r] * group + j] = state.astype(BF16)


def sums_kernel(own_ref, one_ref, two_ref, three_ref, sent_ref, *total_refs):
    total = own_ref[...] + one_ref[...].astype(F32) + two_ref[...].astype(F32) + three_ref[...].astype(F32)
    for total_ref in total_refs:
        total_ref[...] = total
    sent_ref[...] = total.astype(BF16)


def left_kernel(seq, place_ref, own_ref, one_ref, early2_ref, early3_ref, late2_ref, late3_ref, gain_ref, left_ref, kept_ref):
    kept_ref[...] = gain_ref[...]
    last_quad = place_ref[0] >= seq - QUAD
    two = jnp.where(last_quad, late2_ref[...], early2_ref[...])
    three = jnp.where(last_quad, late3_ref[...], early3_ref[...])
    pair = own_ref[...] + one_ref[...].astype(F32)
    other = two.astype(F32) + three.astype(F32)
    left_ref[...] = jnp.where(place_ref[0] >> 1 & 1 == 1, other, pair).astype(BF16)


def intra_of(group, place, q_ref, w_ref, k_all, v_all, out_refs):
    count = q_ref.shape[0] // STRETCH
    local_bits = count.bit_length() - 1
    causal = lax.broadcasted_iota(jnp.int32, (STRETCH, STRETCH), 0) <= lax.broadcasted_iota(
        jnp.int32, (STRETCH, STRETCH), 1
    )
    for r, out_ref in enumerate(out_refs):
        for j in range(group):
            head = (place & (QUAD - 1) ^ r) * group + j
            cols = pl.ds(pl.multiple_of(head * HEAD_DIM, HEAD_DIM), HEAD_DIM)
            states = []
            for c in range(count):
                here = slice(c * STRETCH, (c + 1) * STRETCH)
                q, k, v = q_ref[here, cols], k_all[r, here, column(j)], v_all[r, here, column(j)]
                probs = jnp.where(causal, nt(k, q), 0.0).astype(BF16)
                total = w_ref[0, pl.ds(head, 1), here] * tn(v, probs)
                for bit in range(local_bits):
                    if c >> bit & 1:
                        low = (c >> bit + 1) << bit + 1
                        left = functools.reduce(jnp.add, states[low : low + (1 << bit)])
                        total += w_ref[1 + bit, pl.ds(head, 1), here] * nt(left.astype(BF16), q)
                out_ref[column(j), here] = total
                if c + 1 < count:
                    states.append(tn(v, k))


def intra_early_kernel(group, place_ref, *refs):
    @pl.when(place_ref[0] < QUAD)
    def _():
        intra_of(group, place_ref[0], *refs[:4], refs[4:])


def intra_late_kernel(group, place_ref, q_ref, w_ref, k_all, v_all, gain_ref, *refs):
    done_refs, column_ref, out_refs = refs[:QUAD], refs[QUAD], refs[QUAD + 1 :]
    for head in range(QUAD * group):
        rows = jnp.broadcast_to(gain_ref[:, column(head)], (HEAD_DIM, HEAD_DIM))
        column_ref[column(head), :] = jnp.transpose(rows, (1, 0))

    @pl.when(place_ref[0] < QUAD)
    def _():
        for done_ref, out_ref in zip(done_refs, out_refs):
            out_ref[...] = done_ref[...]

    @pl.when(place_ref[0] >= QUAD)
    def _():
        intra_of(group, place_ref[0], q_ref, w_ref, k_all, v_all, out_refs)


def readout_of(group, first, work, n_states, carry, finish, place_ref, q_ref, w_ref, *refs):
    n = len(work)
    state_refs, total_refs, refs = refs[:n_states], refs[n_states : n_states + n], refs[n_states + n :]
    carried_ref = refs[0] if carry else None
    out_refs, squares_ref = refs[carry : carry + n], refs[carry + n]
    rows = q_ref.shape[0]
    place = place_ref[0]
    for t in range(0, rows, TILE):
        here = slice(t, t + TILE)
        squares = carried_ref[:, here] if carry else jnp.zeros((8, TILE), F32)
        for (r, complete, reads), total_ref, out_ref in zip(work, total_refs, out_refs):
            for j in range(group):
                head = (place & (QUAD - 1) ^ r) * group + j
                q = q_ref[here, pl.ds(pl.multiple_of(head * HEAD_DIM, HEAD_DIM), HEAD_DIM)]
                total = total_ref[column(j), here]
                for bit, ref, slot in reads:
                    row = w_ref[first + bit, pl.ds(head, 1), here]
                    row = jnp.where(place >> bit & 1 == 1, row, 0.0)
                    total += row * nt(state_refs[ref][slot + j], q)
                out_ref[column(j), here] = total
                if complete:
                    squares += jnp.sum((total * total).reshape(HEAD_DIM // 8, 8, TILE), axis=0)
        squares_ref[:, here] = jnp.sum(squares, axis=0, keepdims=True) if finish else squares


def readout_kernel(group, first, work, lacks, *args):
    low = any(bit == 0 for _, _, reads in work for bit, _, _ in reads)
    fewer = tuple((r, complete, tuple(read for read in reads if low and read[0] >= 2)) for r, complete, reads in work)
    place = args[3][0]
    for present, some in ((True, work), (False, fewer)):
        pl.when(lacks(place) != present)(functools.partial(readout_of, group, first, some, *args))


def norm_kernel(group, full_width, place_ref, *refs):
    total_refs, share_refs, (gain_ref, out_hbm, buf, sems) = refs[:QUAD], refs[QUAD:-4], refs[-4:]
    place = place_ref[0] & (QUAD - 1)
    rows = buf.shape[0]
    scale = lax.rsqrt(functools.reduce(jnp.add, (ref[...] for ref in share_refs)) / full_width + EPSILON)
    copies = []
    for r in range(QUAD):
        for j in range(group):
            start = pl.multiple_of(((place ^ r) * group + j) * HEAD_DIM, HEAD_DIM)
            here = pl.ds(start, HEAD_DIM)
            gain = jnp.concatenate([gain_ref[here, :]] * (rows // HEAD_DIM), axis=1)
            x = (total_refs[r][column(j), :] * scale * gain).astype(BF16)
            spot = column(r * group + j)
            buf[:, spot] = jnp.transpose(x, (1, 0))
            copies.append(pltpu.make_async_copy(buf.at[:, spot], out_hbm.at[:, here], sems.at[r * group + j]))
            copies[-1].start()
    for copy in copies:
        copy.wait()


def local(queries, keys, values, level_weights, norm_gain):
    rows, width = queries.shape
    group = width // HEAD_DIM // QUAD
    local_bits = (rows // STRETCH).bit_length() - 1
    seq_bits = lax.axis_size("seq").bit_length() - 1
    full_width = width * lax.axis_size("head")
    position = lax.axis_index("seq").astype(jnp.int32)
    place = position.reshape(1)
    sds = jax.ShapeDtypeStruct
    block = (group, HEAD_DIM, HEAD_DIM)
    others = (3 * group, HEAD_DIM, HEAD_DIM)
    panel = (rows, group * HEAD_DIM)
    part_shape = sds((group * HEAD_DIM, rows), F32)

    k_all, v_all, own, one, two, three, rest = pl.pallas_call(
        functools.partial(states_kernel, group),
        out_shape=(sds((QUAD,) + panel, BF16),) * 2 + (sds(block, F32),) + (sds(block, BF16),) * 3 + (sds(others, BF16),),
        in_specs=[SMEM, HBM, HBM],
        out_specs=(VMEM,) * 7,
        scratch_shapes=[pltpu.SemaphoreType.DMA((2, QUAD))],
        compiler_params=params(STATES_GRANT),
        cost_estimate=cost(2 * rows * width * HEAD_DIM, 4 * rows * width),
        name="states",
    )(place, keys, values)

    early3 = exchanged_in(three, 3, lambda s, seq: s < seq - QUAD)
    taken1 = exchanged(one, "seq", 1)
    early2 = exchanged_in(two, 2, lambda s, seq: s < seq - QUAD)
    late3 = exchanged_in(three, 3, lambda s, seq: s >= seq - QUAD)
    late2 = exchanged_in(two, 2, lambda s, seq: s >= seq - QUAD)
    near = exchanged(rest, "seq", 1)

    args = (place, queries, level_weights, k_all, v_all)
    work_cost = cost(6 * rows * STRETCH * width, 4 * rows * width)
    outs = pl.pallas_call(
        functools.partial(intra_early_kernel, group),
        out_shape=(part_shape,) * QUAD,
        in_specs=[SMEM] + [VMEM] * 4,
        out_specs=(VMEM,) * QUAD,
        compiler_params=params(),
        cost_estimate=work_cost,
        name="intra_early",
    )(*args)
    sums, *running = pl.pallas_call(
        sums_kernel,
        out_shape=(sds(block, BF16),) + (sds(block, F32),) * (seq_bits > 3),
        in_specs=[VMEM] * 4,
        out_specs=(VMEM,) * (1 + (seq_bits > 3)),
        compiler_params=params(),
        cost_estimate=cost(4 * group * HEAD_DIM**2, 16 * group * HEAD_DIM**2),
        name="sums",
    )(own, taken1, early2, early3)
    upper = []
    for bit in range(2, seq_bits):
        if bit > 2:
            running = [running[0] + upper[-1].astype(F32)]
            sums = running[0].astype(BF16)
        upper.append(exchanged(sums, "seq", 1 << bit))
    left_pair, gain = pl.pallas_call(
        functools.partial(left_kernel, lax.axis_size("seq")),
        out_shape=(sds(block, BF16), sds((1, width), F32)),
        in_specs=[SMEM] + [VMEM] * 7,
        out_specs=(VMEM,) * 2,
        compiler_params=params(),
        cost_estimate=cost(4 * group * HEAD_DIM**2, 16 * group * HEAD_DIM**2),
        name="left",
    )(place, own, taken1, early2, early3, late2, late3, norm_gain.reshape(1, width))
    top = jnp.concatenate(upper, axis=0) if len(upper) > 1 else upper[0]
    tops = {0: top} | {r: exchanged_in(top, r, lambda s, seq: s >= QUAD) for r in (3, 1, 2)}

    gain, *outs = pl.pallas_call(
        functools.partial(intra_late_kernel, group),
        out_shape=(sds((width, HEAD_DIM), F32),) + (part_shape,) * QUAD,
        in_specs=[SMEM] + [VMEM] * (5 + QUAD),
        out_specs=(VMEM,) * (1 + QUAD),
        compiler_params=params(),
        cost_estimate=work_cost,
        name="intra_late",
    )(*args, gain, *outs)
    totals = dict(enumerate(outs))

    middle = {0: left_pair} | {r: exchanged(left_pair, "seq", r) for r in (3, 2)}
    middle[1] = exchanged_in(left_pair, 1, lambda s, seq: s >> 1 & 1 == 1)

    def top_reads(ref):
        return tuple((bit, ref, (bit - 2) * group) for bit in range(2, seq_bits))

    def readout(label, work, states, squares, finish=False):
        n, carry = len(work), squares is not None

        def lacks(place):
            return {"far": place & (QUAD - 1) == 0, "mid": place < 2, "last": place < QUAD}[label]

        kernel = functools.partial(readout_kernel, group, 1 + local_bits, work, lacks, len(states), carry, finish)
        ins = [place, queries, level_weights, *states, *(totals[r] for r, _, _ in work)] + [squares] * carry
        shapes = [part_shape] * n + [sds((1 if finish else 8, rows), F32)]
        outs = pl.pallas_call(
            kernel,
            out_shape=tuple(shapes),
            in_specs=[SMEM] + [VMEM] * (len(ins) - 1),
            out_specs=(VMEM,) * len(shapes),
            compiler_params=params(),
            cost_estimate=cost(n * rows * width * HEAD_DIM, 2 * n * rows * width),
        )(*ins)
        totals.update({r: out for (r, _, _), out in zip(work, outs)})
        return outs[n]

    below = {0: ((0, 0, 0), (1, 2, 0)), 1: ((0, 1, 0),)}
    below |= {r: ((0, 1, (r - 1) * group), (1, 1 + r, 0)) for r in (2, 3)}
    work = tuple((r, r == 0, below[r] + (top_reads(5) if r == 0 else ())) for r in (3, 1, 2, 0))
    squares = readout("far", work, (taken1, near, middle[0], middle[2], middle[3], top), None)
    work = (3, True, top_reads(0)), (1, True, ((1, 2, 0), *top_reads(1)))
    squares = readout("mid", work, (tops[3], tops[1], middle[1]), squares)
    squares = readout("last", ((2, True, top_reads(0)),), (tops[2],), squares, finish=True)

    shares = [squares] + [exchanged(squares, "head", mask) for mask in range(1, lax.axis_size("head"))]

    return pl.pallas_call(
        functools.partial(norm_kernel, group, full_width),
        out_shape=sds((rows, width), BF16),
        in_specs=[SMEM] + [VMEM] * (QUAD + len(shares) + 1),
        out_specs=ANY,
        scratch_shapes=[pltpu.VMEM((rows, width), BF16), pltpu.SemaphoreType.DMA((QUAD * group,))],
        compiler_params=params(),
        cost_estimate=cost(2 * rows * width, 2 * rows * width),
        name="norm",
    )(place, *(totals[r] for r in range(QUAD)), *shares, gain)


def solution(mesh):
    return jax.shard_map(
        local,
        mesh=mesh,
        in_specs=(P("seq", "head"), P("seq", "head"), P("seq", "head"), P(None, "head", "seq"), P("head")),
        out_specs=P("seq", "head"),
        check_vma=False,
    )
```

```python
import functools

import jax
import jax.numpy as jnp
from jax import lax
from jax.experimental import pallas as pl
from jax.experimental.pallas import tpu as pltpu
from jax.sharding import PartitionSpec as P


HEAD_DIM = 128
STRETCH = 256
EPSILON = 1e-06
QUAD = 4
F32 = jnp.float32
BF16 = jnp.bfloat16
VMEM = pl.BlockSpec(memory_space=pltpu.VMEM)
SMEM = pl.BlockSpec(memory_space=pltpu.SMEM)
ANY = pl.BlockSpec(memory_space=pl.ANY)
HBM = pl.BlockSpec(memory_space=pltpu.HBM)
GRANT = 24 << 20
TILE = 256
STATES_GRANT = 51968 << 10


def params(grant=GRANT):
    return pltpu.CompilerParams(vmem_limit_bytes=grant)


def cost(flops, moved):
    return pl.CostEstimate(flops=flops, bytes_accessed=moved, transcendentals=0)


def exchanged(block, axis, mask):
    count = lax.axis_size(axis)
    return lax.ppermute(block, axis, [(i, i ^ mask) for i in range(count)])


def exchanged_in(block, mask, real):
    seq, head = lax.axis_size("seq"), lax.axis_size("head")
    route = []
    for s in range(seq):
        for h in range(head):
            to = (s ^ mask, h) if real(s, seq) else (s, h ^ 1)
            route.append((s * head + h, to[0] * head + to[1]))
    return lax.ppermute(block, ("seq", "head"), route)


def nt(a, b):
    return lax.dot_general(a, b, (((1,), (1,)), ((), ())), preferred_element_type=F32)


def tn(a, b):
    return lax.dot_general(a, b, (((0,), (0,)), ((), ())), preferred_element_type=F32)


def column(head):
    return pl.ds(head * HEAD_DIM, HEAD_DIM)


def states_kernel(group, place_ref, k_hbm, v_hbm, k_ref, v_ref, own_ref, one_ref, two_ref, three_ref, rest_ref, sems):
    width = group * HEAD_DIM
    place = place_ref[0] & (QUAD - 1)
    order = (3, 1, 2, 0)
    copies = {}
    for r in order:
        cols = pl.ds(pl.multiple_of((place ^ r) * width, width), width)
        copies[r] = (
            pltpu.make_async_copy(k_hbm.at[:, cols], k_ref.at[r], sems.at[0, r]),
            pltpu.make_async_copy(v_hbm.at[:, cols], v_ref.at[r], sems.at[1, r]),
        )
        for copy in copies[r]:
            copy.start()
    sent = {1: one_ref, 2: two_ref, 3: three_ref}
    spot = {0: 0, 3: 1, 2: 2}
    for r in order:
        for copy in copies[r]:
            copy.wait()
        for j in range(group):
            state = tn(v_ref[r, :, column(j)], k_ref[r, :, column(j)])
            if r == 0:
                own_ref[j] = state
            else:
                sent[r][j] = state.astype(BF16)
            if r in spot:
                rest_ref[spot[r] * group + j] = state.astype(BF16)


def sums_kernel(own_ref, one_ref, two_ref, three_ref, sent_ref, *total_refs):
    total = own_ref[...] + one_ref[...].astype(F32) + two_ref[...].astype(F32) + three_ref[...].astype(F32)
    for total_ref in total_refs:
        total_ref[...] = total
    sent_ref[...] = total.astype(BF16)


def left_kernel(seq, place_ref, own_ref, one_ref, early2_ref, early3_ref, late2_ref, late3_ref, left_ref):
    last_quad = place_ref[0] >= seq - QUAD
    two = jnp.where(last_quad, late2_ref[...], early2_ref[...])
    three = jnp.where(last_quad, late3_ref[...], early3_ref[...])
    pair = own_ref[...] + one_ref[...].astype(F32)
    other = two.astype(F32) + three.astype(F32)
    left_ref[...] = jnp.where(place_ref[0] >> 1 & 1 == 1, other, pair).astype(BF16)


def intra_of(group, groups, place, q_ref, w_ref, k_all, v_all, out_refs):
    count = q_ref.shape[0] // STRETCH
    local_bits = count.bit_length() - 1
    causal = lax.broadcasted_iota(jnp.int32, (STRETCH, STRETCH), 0) <= lax.broadcasted_iota(
        jnp.int32, (STRETCH, STRETCH), 1
    )
    for r, out_ref in zip(groups, out_refs):
        for j in range(group):
            head = (place & (QUAD - 1) ^ r) * group + j
            cols = pl.ds(pl.multiple_of(head * HEAD_DIM, HEAD_DIM), HEAD_DIM)
            states = []
            for c in range(count):
                here = slice(c * STRETCH, (c + 1) * STRETCH)
                q, k, v = q_ref[here, cols], k_all[r, here, column(j)], v_all[r, here, column(j)]
                probs = jnp.where(causal, nt(k, q), 0.0).astype(BF16)
                total = w_ref[0, pl.ds(head, 1), here] * tn(v, probs)
                for bit in range(local_bits):
                    if c >> bit & 1:
                        low = (c >> bit + 1) << bit + 1
                        left = functools.reduce(jnp.add, states[low : low + (1 << bit)])
                        total += w_ref[1 + bit, pl.ds(head, 1), here] * nt(left.astype(BF16), q)
                out_ref[column(j), here] = total
                if c + 1 < count:
                    states.append(tn(v, k))


def lowest(place):
    return place < QUAD


def busy(place):
    return (place >= QUAD) & (place >> 1 & 1 == 1)


def intra_first_kernel(group, place_ref, *refs):
    gain_ref, kept_ref, out_ref = refs[4:]
    kept_ref[...] = gain_ref[...]

    @pl.when(busy(place_ref[0]))
    def _():
        intra_of(group, (3,), place_ref[0], *refs[:4], (out_ref,))


def intra_second_kernel(group, place_ref, *refs):
    args, out_refs = refs[:4], refs[4:]

    @pl.when(lowest(place_ref[0]))
    def _():
        intra_of(group, range(QUAD), place_ref[0], *args, out_refs)

    @pl.when(busy(place_ref[0]))
    def _():
        intra_of(group, (1,), place_ref[0], *args, out_refs[1:2])


def intra_last_kernel(group, place_ref, q_ref, w_ref, k_all, v_all, gain_ref, first_ref, *refs):
    args = (q_ref, w_ref, k_all, v_all)
    done_refs, column_ref, out_refs = refs[:QUAD], refs[QUAD], refs[QUAD + 1 :]
    for head in range(QUAD * group):
        rows = jnp.broadcast_to(gain_ref[:, column(head)], (HEAD_DIM, HEAD_DIM))
        column_ref[column(head), :] = jnp.transpose(rows, (1, 0))

    @pl.when(lowest(place_ref[0]))
    def _():
        for done_ref, out_ref in zip(done_refs, out_refs):
            out_ref[...] = done_ref[...]

    @pl.when(busy(place_ref[0]))
    def _():
        out_refs[3][...] = first_ref[...]
        out_refs[1][...] = done_refs[1][...]
        intra_of(group, (2, 0), place_ref[0], *args, (out_refs[2], out_refs[0]))

    @pl.when(jnp.logical_not(lowest(place_ref[0]) | busy(place_ref[0])))
    def _():
        intra_of(group, range(QUAD), place_ref[0], *args, out_refs)


def readout_of(group, first, work, n_states, carry, finish, place_ref, q_ref, w_ref, *refs):
    n = len(work)
    state_refs, total_refs, refs = refs[:n_states], refs[n_states : n_states + n], refs[n_states + n :]
    carried_ref = refs[0] if carry else None
    out_refs, squares_ref = refs[carry : carry + n], refs[carry + n]
    rows = q_ref.shape[0]
    place = place_ref[0]
    for t in range(0, rows, TILE):
        here = slice(t, t + TILE)
        squares = carried_ref[:, here] if carry else jnp.zeros((8, TILE), F32)
        for (r, complete, reads), total_ref, out_ref in zip(work, total_refs, out_refs):
            for j in range(group):
                head = (place & (QUAD - 1) ^ r) * group + j
                q = q_ref[here, pl.ds(pl.multiple_of(head * HEAD_DIM, HEAD_DIM), HEAD_DIM)]
                total = total_ref[column(j), here]
                for bit, ref, slot in reads:
                    row = w_ref[first + bit, pl.ds(head, 1), here]
                    row = jnp.where(place >> bit & 1 == 1, row, 0.0)
                    total += row * nt(state_refs[ref][slot + j], q)
                out_ref[column(j), here] = total
                if complete:
                    squares += jnp.sum((total * total).reshape(HEAD_DIM // 8, 8, TILE), axis=0)
        squares_ref[:, here] = jnp.sum(squares, axis=0, keepdims=True) if finish else squares


def readout_kernel(group, first, work, lacks, *args):
    low = any(bit == 0 for _, _, reads in work for bit, _, _ in reads)
    fewer = tuple((r, complete, tuple(read for read in reads if low and read[0] >= 2)) for r, complete, reads in work)
    place = args[3][0]
    for present, some in ((True, work), (False, fewer)):
        pl.when(lacks(place) != present)(functools.partial(readout_of, group, first, some, *args))


def norm_kernel(group, full_width, place_ref, *refs):
    total_refs, share_refs, (gain_ref, out_hbm, buf, sems) = refs[:QUAD], refs[QUAD:-4], refs[-4:]
    place = place_ref[0] & (QUAD - 1)
    rows = buf.shape[0]
    scale = lax.rsqrt(functools.reduce(jnp.add, (ref[...] for ref in share_refs)) / full_width + EPSILON)
    copies = []
    for r in range(QUAD):
        for j in range(group):
            start = pl.multiple_of(((place ^ r) * group + j) * HEAD_DIM, HEAD_DIM)
            here = pl.ds(start, HEAD_DIM)
            gain = jnp.concatenate([gain_ref[here, :]] * (rows // HEAD_DIM), axis=1)
            x = (total_refs[r][column(j), :] * scale * gain).astype(BF16)
            spot = column(r * group + j)
            buf[:, spot] = jnp.transpose(x, (1, 0))
            copies.append(pltpu.make_async_copy(buf.at[:, spot], out_hbm.at[:, here], sems.at[r * group + j]))
            copies[-1].start()
    for copy in copies:
        copy.wait()


def local(queries, keys, values, level_weights, norm_gain):
    rows, width = queries.shape
    group = width // HEAD_DIM // QUAD
    local_bits = (rows // STRETCH).bit_length() - 1
    seq_bits = lax.axis_size("seq").bit_length() - 1
    full_width = width * lax.axis_size("head")
    position = lax.axis_index("seq").astype(jnp.int32)
    place = position.reshape(1)
    sds = jax.ShapeDtypeStruct
    block = (group, HEAD_DIM, HEAD_DIM)
    others = (3 * group, HEAD_DIM, HEAD_DIM)
    panel = (rows, group * HEAD_DIM)
    part_shape = sds((group * HEAD_DIM, rows), F32)

    k_all, v_all, own, one, two, three, rest = pl.pallas_call(
        functools.partial(states_kernel, group),
        out_shape=(sds((QUAD,) + panel, BF16),) * 2 + (sds(block, F32),) + (sds(block, BF16),) * 3 + (sds(others, BF16),),
        in_specs=[SMEM, HBM, HBM],
        out_specs=(VMEM,) * 7,
        scratch_shapes=[pltpu.SemaphoreType.DMA((2, QUAD))],
        compiler_params=params(STATES_GRANT),
        cost_estimate=cost(2 * rows * width * HEAD_DIM, 4 * rows * width),
        name="states",
    )(place, keys, values)

    early3 = exchanged_in(three, 3, lambda s, seq: s < seq - QUAD)
    taken1 = exchanged(one, "seq", 1)
    early2 = exchanged_in(two, 2, lambda s, seq: s < seq - QUAD)
    late3 = exchanged_in(three, 3, lambda s, seq: s >= seq - QUAD)
    late2 = exchanged_in(two, 2, lambda s, seq: s >= seq - QUAD)
    near = exchanged(rest, "seq", 1)

    args = (place, queries, level_weights, k_all, v_all)
    work_cost = cost(6 * rows * STRETCH * width, 4 * rows * width)
    gain, first = pl.pallas_call(
        functools.partial(intra_first_kernel, group),
        out_shape=(sds((1, width), F32), part_shape),
        in_specs=[SMEM] + [VMEM] * 5,
        out_specs=(VMEM,) * 2,
        compiler_params=params(),
        cost_estimate=work_cost,
        name="intra_first",
    )(*args, norm_gain.reshape(1, width))
    outs = pl.pallas_call(
        functools.partial(intra_second_kernel, group),
        out_shape=(part_shape,) * QUAD,
        in_specs=[SMEM] + [VMEM] * 4,
        out_specs=(VMEM,) * QUAD,
        compiler_params=params(),
        cost_estimate=work_cost,
        name="intra_second",
    )(*args)

    sums, *running = pl.pallas_call(
        sums_kernel,
        out_shape=(sds(block, BF16),) + (sds(block, F32),) * (seq_bits > 3),
        in_specs=[VMEM] * 4,
        out_specs=(VMEM,) * (1 + (seq_bits > 3)),
        compiler_params=params(),
        cost_estimate=cost(4 * group * HEAD_DIM**2, 16 * group * HEAD_DIM**2),
        name="sums",
    )(own, taken1, early2, early3)
    upper = []
    for bit in range(2, seq_bits):
        if bit > 2:
            running = [running[0] + upper[-1].astype(F32)]
            sums = running[0].astype(BF16)
        upper.append(exchanged(sums, "seq", 1 << bit))
    left_pair = pl.pallas_call(
        functools.partial(left_kernel, lax.axis_size("seq")),
        out_shape=sds(block, BF16),
        in_specs=[SMEM] + [VMEM] * 6,
        out_specs=VMEM,
        compiler_params=params(),
        cost_estimate=cost(4 * group * HEAD_DIM**2, 16 * group * HEAD_DIM**2),
        name="left",
    )(place, own, taken1, early2, early3, late2, late3)
    top = jnp.concatenate(upper, axis=0) if len(upper) > 1 else upper[0]
    tops = {0: top} | {r: exchanged_in(top, r, lambda s, seq: s >= QUAD) for r in (3, 1, 2)}

    gain, *outs = pl.pallas_call(
        functools.partial(intra_last_kernel, group),
        out_shape=(sds((width, HEAD_DIM), F32),) + (part_shape,) * QUAD,
        in_specs=[SMEM] + [VMEM] * (6 + QUAD),
        out_specs=(VMEM,) * (1 + QUAD),
        compiler_params=params(),
        cost_estimate=work_cost,
        name="intra_last",
    )(*args, gain, first, *outs)
    totals = dict(enumerate(outs))

    middle = {0: left_pair} | {r: exchanged(left_pair, "seq", r) for r in (3, 2)}
    middle[1] = exchanged_in(left_pair, 1, lambda s, seq: s >> 1 & 1 == 1)

    def top_reads(ref):
        return tuple((bit, ref, (bit - 2) * group) for bit in range(2, seq_bits))

    def readout(label, work, states, squares, finish=False):
        n, carry = len(work), squares is not None

        def lacks(place):
            return {"far": place & (QUAD - 1) == 0, "mid": place < 2, "last": place < QUAD}[label]

        kernel = functools.partial(readout_kernel, group, 1 + local_bits, work, lacks, len(states), carry, finish)
        ins = [place, queries, level_weights, *states, *(totals[r] for r, _, _ in work)] + [squares] * carry
        shapes = [part_shape] * n + [sds((1 if finish else 8, rows), F32)]
        outs = pl.pallas_call(
            kernel,
            out_shape=tuple(shapes),
            in_specs=[SMEM] + [VMEM] * (len(ins) - 1),
            out_specs=(VMEM,) * len(shapes),
            compiler_params=params(),
            cost_estimate=cost(n * rows * width * HEAD_DIM, 2 * n * rows * width),
        )(*ins)
        totals.update({r: out for (r, _, _), out in zip(work, outs)})
        return outs[n]

    below = {0: ((0, 0, 0), (1, 2, 0)), 1: ((0, 1, 0),)}
    below |= {r: ((0, 1, (r - 1) * group), (1, 1 + r, 0)) for r in (2, 3)}
    work = tuple((r, r == 0, below[r] + (top_reads(5) if r == 0 else ())) for r in (3, 1, 2, 0))
    squares = readout("far", work, (taken1, near, middle[0], middle[2], middle[3], top), None)
    work = (3, True, top_reads(0)), (1, True, ((1, 2, 0), *top_reads(1)))
    squares = readout("mid", work, (tops[3], tops[1], middle[1]), squares)
    squares = readout("last", ((2, True, top_reads(0)),), (tops[2],), squares, finish=True)

    shares = [squares] + [exchanged(squares, "head", mask) for mask in range(1, lax.axis_size("head"))]

    return pl.pallas_call(
        functools.partial(norm_kernel, group, full_width),
        out_shape=sds((rows, width), BF16),
        in_specs=[SMEM] + [VMEM] * (QUAD + len(shares) + 1),
        out_specs=ANY,
        scratch_shapes=[pltpu.VMEM((rows, width), BF16), pltpu.SemaphoreType.DMA((QUAD * group,))],
        compiler_params=params(),
        cost_estimate=cost(2 * rows * width, 2 * rows * width),
        name="norm",
    )(place, *(totals[r] for r in range(QUAD)), *shares, gain)


def solution(mesh):
    return jax.shard_map(
        local,
        mesh=mesh,
        in_specs=(P("seq", "head"), P("seq", "head"), P("seq", "head"), P(None, "head", "seq"), P("head")),
        out_specs=P("seq", "head"),
        check_vma=False,
    )
```

```python
import functools

import jax
import jax.numpy as jnp
from jax import lax
from jax.experimental import pallas as pl
from jax.experimental.pallas import tpu as pltpu
from jax.sharding import PartitionSpec as P


HEAD_DIM = 128
STRETCH = 256
EPSILON = 1e-06
QUAD = 4
F32 = jnp.float32
BF16 = jnp.bfloat16
VMEM = pl.BlockSpec(memory_space=pltpu.VMEM)
SMEM = pl.BlockSpec(memory_space=pltpu.SMEM)
ANY = pl.BlockSpec(memory_space=pl.ANY)
HBM = pl.BlockSpec(memory_space=pltpu.HBM)
GRANT = 24 << 20
TILE = 256
STATES_GRANT = 51968 << 10


def params(grant=GRANT):
    return pltpu.CompilerParams(vmem_limit_bytes=grant)


def cost(flops, moved):
    return pl.CostEstimate(flops=flops, bytes_accessed=moved, transcendentals=0)


def exchanged(block, axis, mask):
    count = lax.axis_size(axis)
    return lax.ppermute(block, axis, [(i, i ^ mask) for i in range(count)])


def exchanged_in(block, mask, real):
    seq, head = lax.axis_size("seq"), lax.axis_size("head")
    route = []
    for s in range(seq):
        for h in range(head):
            to = (s ^ mask, h) if real(s, seq) else (s, h ^ 1)
            route.append((s * head + h, to[0] * head + to[1]))
    return lax.ppermute(block, ("seq", "head"), route)


def nt(a, b):
    return lax.dot_general(a, b, (((1,), (1,)), ((), ())), preferred_element_type=F32)


def tn(a, b):
    return lax.dot_general(a, b, (((0,), (0,)), ((), ())), preferred_element_type=F32)


def column(head):
    return pl.ds(head * HEAD_DIM, HEAD_DIM)


def states_kernel(group, place_ref, k_hbm, v_hbm, k_ref, v_ref, own_ref, one_ref, two_ref, three_ref, rest_ref, sems):
    width = group * HEAD_DIM
    place = place_ref[0] & (QUAD - 1)
    order = (3, 1, 2, 0)
    copies = {}
    for r in order:
        cols = pl.ds(pl.multiple_of((place ^ r) * width, width), width)
        copies[r] = (
            pltpu.make_async_copy(k_hbm.at[:, cols], k_ref.at[r], sems.at[0, r]),
            pltpu.make_async_copy(v_hbm.at[:, cols], v_ref.at[r], sems.at[1, r]),
        )
        for copy in copies[r]:
            copy.start()
    sent = {1: one_ref, 2: two_ref, 3: three_ref}
    spot = {0: 0, 3: 1, 2: 2}
    for r in order:
        for copy in copies[r]:
            copy.wait()
        for j in range(group):
            state = tn(v_ref[r, :, column(j)], k_ref[r, :, column(j)])
            if r == 0:
                own_ref[j] = state
            else:
                sent[r][j] = state.astype(BF16)
            if r in spot:
                rest_ref[spot[r] * group + j] = state.astype(BF16)


def sums_kernel(own_ref, one_ref, two_ref, three_ref, sent_ref, *total_refs):
    total = own_ref[...] + one_ref[...].astype(F32) + two_ref[...].astype(F32) + three_ref[...].astype(F32)
    for total_ref in total_refs:
        total_ref[...] = total
    sent_ref[...] = total.astype(BF16)


def join_kernel(top_ref, left_ref, joined_ref):
    joined_ref[: top_ref.shape[0]] = top_ref[...]
    joined_ref[top_ref.shape[0] :] = left_ref[...]


def left_kernel(seq, place_ref, own_ref, one_ref, early2_ref, early3_ref, late2_ref, late3_ref, left_ref):
    last_quad = place_ref[0] >= seq - QUAD
    two = jnp.where(last_quad, late2_ref[...], early2_ref[...])
    three = jnp.where(last_quad, late3_ref[...], early3_ref[...])
    pair = own_ref[...] + one_ref[...].astype(F32)
    other = two.astype(F32) + three.astype(F32)
    left_ref[...] = jnp.where(place_ref[0] >> 1 & 1 == 1, other, pair).astype(BF16)


def intra_of(group, groups, place, q_ref, w_ref, k_all, v_all, out_refs):
    count = q_ref.shape[0] // STRETCH
    local_bits = count.bit_length() - 1
    causal = lax.broadcasted_iota(jnp.int32, (STRETCH, STRETCH), 0) <= lax.broadcasted_iota(
        jnp.int32, (STRETCH, STRETCH), 1
    )
    for r, out_ref in zip(groups, out_refs):
        for j in range(group):
            head = (place & (QUAD - 1) ^ r) * group + j
            cols = pl.ds(pl.multiple_of(head * HEAD_DIM, HEAD_DIM), HEAD_DIM)
            states = []
            for c in range(count):
                here = slice(c * STRETCH, (c + 1) * STRETCH)
                q, k, v = q_ref[here, cols], k_all[r, here, column(j)], v_all[r, here, column(j)]
                probs = jnp.where(causal, nt(k, q), 0.0).astype(BF16)
                total = w_ref[0, pl.ds(head, 1), here] * tn(v, probs)
                for bit in range(local_bits):
                    if c >> bit & 1:
                        low = (c >> bit + 1) << bit + 1
                        left = functools.reduce(jnp.add, states[low : low + (1 << bit)])
                        total += w_ref[1 + bit, pl.ds(head, 1), here] * nt(left.astype(BF16), q)
                out_ref[column(j), here] = total
                if c + 1 < count:
                    states.append(tn(v, k))


def lowest(place):
    return place < QUAD


def busy(place):
    return (place >= QUAD) & (place >> 1 & 1 == 1)


def intra_first_kernel(group, place_ref, *refs):
    gain_ref, kept_ref, out_ref = refs[4:]
    kept_ref[...] = gain_ref[...]

    @pl.when(busy(place_ref[0]))
    def _():
        intra_of(group, (3,), place_ref[0], *refs[:4], (out_ref,))


def intra_second_kernel(group, place_ref, *refs):
    args, out_refs = refs[:4], refs[4:]

    @pl.when(lowest(place_ref[0]))
    def _():
        intra_of(group, range(QUAD), place_ref[0], *args, out_refs)

    @pl.when(busy(place_ref[0]))
    def _():
        intra_of(group, (1,), place_ref[0], *args, out_refs[1:2])


def intra_last_kernel(group, place_ref, q_ref, w_ref, k_all, v_all, gain_ref, first_ref, *refs):
    args = (q_ref, w_ref, k_all, v_all)
    done_refs, column_ref, out_refs = refs[:QUAD], refs[QUAD], refs[QUAD + 1 :]
    for head in range(QUAD * group):
        rows = jnp.broadcast_to(gain_ref[:, column(head)], (HEAD_DIM, HEAD_DIM))
        column_ref[column(head), :] = jnp.transpose(rows, (1, 0))

    @pl.when(lowest(place_ref[0]))
    def _():
        for done_ref, out_ref in zip(done_refs, out_refs):
            out_ref[...] = done_ref[...]

    @pl.when(busy(place_ref[0]))
    def _():
        out_refs[3][...] = first_ref[...]
        out_refs[1][...] = done_refs[1][...]
        intra_of(group, (2, 0), place_ref[0], *args, (out_refs[2], out_refs[0]))

    @pl.when(jnp.logical_not(lowest(place_ref[0]) | busy(place_ref[0])))
    def _():
        intra_of(group, range(QUAD), place_ref[0], *args, out_refs)


def readout_of(group, first, work, n_states, carry, finish, place_ref, q_ref, w_ref, *refs):
    n = len(work)
    state_refs, total_refs, refs = refs[:n_states], refs[n_states : n_states + n], refs[n_states + n :]
    carried_ref = refs[0] if carry else None
    out_refs, squares_ref = refs[carry : carry + n], refs[carry + n]
    rows = q_ref.shape[0]
    place = place_ref[0]
    for t in range(0, rows, TILE):
        here = slice(t, t + TILE)
        squares = carried_ref[:, here] if carry else jnp.zeros((8, TILE), F32)
        for (r, complete, reads), total_ref, out_ref in zip(work, total_refs, out_refs):
            for j in range(group):
                head = (place & (QUAD - 1) ^ r) * group + j
                q = q_ref[here, pl.ds(pl.multiple_of(head * HEAD_DIM, HEAD_DIM), HEAD_DIM)]
                total = total_ref[column(j), here]
                for bit, ref, slot in reads:
                    row = w_ref[first + bit, pl.ds(head, 1), here]
                    row = jnp.where(place >> bit & 1 == 1, row, 0.0)
                    total += row * nt(state_refs[ref][slot + j], q)
                out_ref[column(j), here] = total
                if complete:
                    squares += jnp.sum((total * total).reshape(HEAD_DIM // 8, 8, TILE), axis=0)
        squares_ref[:, here] = jnp.sum(squares, axis=0, keepdims=True) if finish else squares


def readout_kernel(group, first, work, lacks, *args):
    low = any(bit == 0 for _, _, reads in work for bit, _, _ in reads)
    fewer = tuple((r, complete, tuple(read for read in reads if low and read[0] >= 2)) for r, complete, reads in work)
    place = args[3][0]
    for present, some in ((True, work), (False, fewer)):
        pl.when(lacks(place) != present)(functools.partial(readout_of, group, first, some, *args))


def norm_kernel(group, full_width, place_ref, *refs):
    total_refs, share_refs, (gain_ref, out_hbm, buf, sems) = refs[:QUAD], refs[QUAD:-4], refs[-4:]
    place = place_ref[0] & (QUAD - 1)
    rows = buf.shape[0]
    scale = lax.rsqrt(functools.reduce(jnp.add, (ref[...] for ref in share_refs)) / full_width + EPSILON)
    copies = []
    for r in range(QUAD):
        for j in range(group):
            start = pl.multiple_of(((place ^ r) * group + j) * HEAD_DIM, HEAD_DIM)
            here = pl.ds(start, HEAD_DIM)
            gain = jnp.concatenate([gain_ref[here, :]] * (rows // HEAD_DIM), axis=1)
            x = (total_refs[r][column(j), :] * scale * gain).astype(BF16)
            spot = column(r * group + j)
            buf[:, spot] = jnp.transpose(x, (1, 0))
            copies.append(pltpu.make_async_copy(buf.at[:, spot], out_hbm.at[:, here], sems.at[r * group + j]))
            copies[-1].start()
    for copy in copies:
        copy.wait()


def local(queries, keys, values, level_weights, norm_gain):
    rows, width = queries.shape
    group = width // HEAD_DIM // QUAD
    local_bits = (rows // STRETCH).bit_length() - 1
    seq_bits = lax.axis_size("seq").bit_length() - 1
    full_width = width * lax.axis_size("head")
    position = lax.axis_index("seq").astype(jnp.int32)
    place = position.reshape(1)
    sds = jax.ShapeDtypeStruct
    block = (group, HEAD_DIM, HEAD_DIM)
    others = (3 * group, HEAD_DIM, HEAD_DIM)
    panel = (rows, group * HEAD_DIM)
    part_shape = sds((group * HEAD_DIM, rows), F32)

    k_all, v_all, own, one, two, three, rest = pl.pallas_call(
        functools.partial(states_kernel, group),
        out_shape=(sds((QUAD,) + panel, BF16),) * 2 + (sds(block, F32),) + (sds(block, BF16),) * 3 + (sds(others, BF16),),
        in_specs=[SMEM, HBM, HBM],
        out_specs=(VMEM,) * 7,
        scratch_shapes=[pltpu.SemaphoreType.DMA((2, QUAD))],
        compiler_params=params(STATES_GRANT),
        cost_estimate=cost(2 * rows * width * HEAD_DIM, 4 * rows * width),
        name="states",
    )(place, keys, values)

    early3 = exchanged_in(three, 3, lambda s, seq: s < seq - QUAD)
    taken1 = exchanged(one, "seq", 1)
    early2 = exchanged_in(two, 2, lambda s, seq: s < seq - QUAD)
    late3 = exchanged_in(three, 3, lambda s, seq: s >= seq - QUAD)
    late2 = exchanged_in(two, 2, lambda s, seq: s >= seq - QUAD)
    near = exchanged(rest, "seq", 1)

    args = (place, queries, level_weights, k_all, v_all)
    work_cost = cost(6 * rows * STRETCH * width, 4 * rows * width)
    gain, first = pl.pallas_call(
        functools.partial(intra_first_kernel, group),
        out_shape=(sds((1, width), F32), part_shape),
        in_specs=[SMEM] + [VMEM] * 5,
        out_specs=(VMEM,) * 2,
        compiler_params=params(),
        cost_estimate=work_cost,
        name="intra_first",
    )(*args, norm_gain.reshape(1, width))
    outs = pl.pallas_call(
        functools.partial(intra_second_kernel, group),
        out_shape=(part_shape,) * QUAD,
        in_specs=[SMEM] + [VMEM] * 4,
        out_specs=(VMEM,) * QUAD,
        compiler_params=params(),
        cost_estimate=work_cost,
        name="intra_second",
    )(*args)

    sums, *running = pl.pallas_call(
        sums_kernel,
        out_shape=(sds(block, BF16),) + (sds(block, F32),) * (seq_bits > 3),
        in_specs=[VMEM] * 4,
        out_specs=(VMEM,) * (1 + (seq_bits > 3)),
        compiler_params=params(),
        cost_estimate=cost(4 * group * HEAD_DIM**2, 16 * group * HEAD_DIM**2),
        name="sums",
    )(own, taken1, early2, early3)
    upper = []
    for bit in range(2, seq_bits):
        if bit > 2:
            running = [running[0] + upper[-1].astype(F32)]
            sums = running[0].astype(BF16)
        upper.append(exchanged(sums, "seq", 1 << bit))
    left_pair = pl.pallas_call(
        functools.partial(left_kernel, lax.axis_size("seq")),
        out_shape=sds(block, BF16),
        in_specs=[SMEM] + [VMEM] * 6,
        out_specs=VMEM,
        compiler_params=params(),
        cost_estimate=cost(4 * group * HEAD_DIM**2, 16 * group * HEAD_DIM**2),
        name="left",
    )(place, own, taken1, early2, early3, late2, late3)
    top = jnp.concatenate(upper, axis=0) if len(upper) > 1 else upper[0]
    tops = {r: exchanged_in(top, r, lambda s, seq: s >= QUAD) for r in (3, 2)}
    joined = pl.pallas_call(
        join_kernel,
        out_shape=sds((top.shape[0] + group,) + block[1:], BF16),
        in_specs=[VMEM] * 2,
        out_specs=VMEM,
        compiler_params=params(),
        cost_estimate=cost(0, 16 * group * HEAD_DIM**2),
        name="join",
    )(top, left_pair)
    tops[1] = exchanged_in(joined, 1, lambda s, seq: s >= 2)

    gain, *outs = pl.pallas_call(
        functools.partial(intra_last_kernel, group),
        out_shape=(sds((width, HEAD_DIM), F32),) + (part_shape,) * QUAD,
        in_specs=[SMEM] + [VMEM] * (6 + QUAD),
        out_specs=(VMEM,) * (1 + QUAD),
        compiler_params=params(),
        cost_estimate=work_cost,
        name="intra_last",
    )(*args, gain, first, *outs)
    totals = dict(enumerate(outs))

    middle = {0: left_pair} | {r: exchanged(left_pair, "seq", r) for r in (3, 2)}

    def top_reads(ref):
        return tuple((bit, ref, (bit - 2) * group) for bit in range(2, seq_bits))

    def readout(label, work, states, squares, finish=False):
        n, carry = len(work), squares is not None

        def lacks(place):
            return {"far": place & (QUAD - 1) == 0, "mid": place < 2, "last": place < QUAD}[label]

        kernel = functools.partial(readout_kernel, group, 1 + local_bits, work, lacks, len(states), carry, finish)
        ins = [place, queries, level_weights, *states, *(totals[r] for r, _, _ in work)] + [squares] * carry
        shapes = [part_shape] * n + [sds((1 if finish else 8, rows), F32)]
        outs = pl.pallas_call(
            kernel,
            out_shape=tuple(shapes),
            in_specs=[SMEM] + [VMEM] * (len(ins) - 1),
            out_specs=(VMEM,) * len(shapes),
            compiler_params=params(),
            cost_estimate=cost(n * rows * width * HEAD_DIM, 2 * n * rows * width),
        )(*ins)
        totals.update({r: out for (r, _, _), out in zip(work, outs)})
        return outs[n]

    below = {0: ((0, 0, 0), (1, 2, 0)), 1: ((0, 1, 0),)}
    below |= {r: ((0, 1, (r - 1) * group), (1, 1 + r, 0)) for r in (2, 3)}
    work = tuple((r, r == 0, below[r] + (top_reads(5) if r == 0 else ())) for r in (3, 1, 2, 0))
    squares = readout("far", work, (taken1, near, middle[0], middle[2], middle[3], top), None)
    work = (3, True, top_reads(0)), (1, True, ((1, 1, top.shape[0]), *top_reads(1)))
    squares = readout("mid", work, (tops[3], tops[1]), squares)
    squares = readout("last", ((2, True, top_reads(0)),), (tops[2],), squares, finish=True)

    shares = [squares] + [exchanged(squares, "head", mask) for mask in range(1, lax.axis_size("head"))]

    return pl.pallas_call(
        functools.partial(norm_kernel, group, full_width),
        out_shape=sds((rows, width), BF16),
        in_specs=[SMEM] + [VMEM] * (QUAD + len(shares) + 1),
        out_specs=ANY,
        scratch_shapes=[pltpu.VMEM((rows, width), BF16), pltpu.SemaphoreType.DMA((QUAD * group,))],
        compiler_params=params(),
        cost_estimate=cost(2 * rows * width, 2 * rows * width),
        name="norm",
    )(place, *(totals[r] for r in range(QUAD)), *shares, gain)


def solution(mesh):
    return jax.shard_map(
        local,
        mesh=mesh,
        in_specs=(P("seq", "head"), P("seq", "head"), P("seq", "head"), P(None, "head", "seq"), P("head")),
        out_specs=P("seq", "head"),
        check_vma=False,
    )
```

```python
import functools

import jax
import jax.numpy as jnp
from jax import lax
from jax.experimental import pallas as pl
from jax.experimental.pallas import tpu as pltpu
from jax.sharding import PartitionSpec as P


HEAD_DIM = 128
STRETCH = 256
EPSILON = 1e-06
QUAD = 4
F32 = jnp.float32
BF16 = jnp.bfloat16
VMEM = pl.BlockSpec(memory_space=pltpu.VMEM)
SMEM = pl.BlockSpec(memory_space=pltpu.SMEM)
ANY = pl.BlockSpec(memory_space=pl.ANY)
HBM = pl.BlockSpec(memory_space=pltpu.HBM)
GRANT = 24 << 20
TILE = 256
STATES_GRANT = 51968 << 10


def params(grant=GRANT):
    return pltpu.CompilerParams(vmem_limit_bytes=grant)


def cost(flops, moved):
    return pl.CostEstimate(flops=flops, bytes_accessed=moved, transcendentals=0)


def exchanged(block, axis, mask):
    count = lax.axis_size(axis)
    return lax.ppermute(block, axis, [(i, i ^ mask) for i in range(count)])


def exchanged_in(block, mask, real):
    seq, head = lax.axis_size("seq"), lax.axis_size("head")
    route = []
    for s in range(seq):
        for h in range(head):
            to = (s ^ mask, h) if real(s, seq) else (s, h ^ 1)
            route.append((s * head + h, to[0] * head + to[1]))
    return lax.ppermute(block, ("seq", "head"), route)


def nt(a, b):
    return lax.dot_general(a, b, (((1,), (1,)), ((), ())), preferred_element_type=F32)


def tn(a, b):
    return lax.dot_general(a, b, (((0,), (0,)), ((), ())), preferred_element_type=F32)


def column(head):
    return pl.ds(head * HEAD_DIM, HEAD_DIM)


def states_kernel(group, place_ref, k_hbm, v_hbm, k_ref, v_ref, own_ref, one_ref, two_ref, three_ref, rest_ref, sems):
    width = group * HEAD_DIM
    place = place_ref[0] & (QUAD - 1)
    order = (3, 1, 2, 0)
    copies = {}
    for r in order:
        cols = pl.ds(pl.multiple_of((place ^ r) * width, width), width)
        copies[r] = (
            pltpu.make_async_copy(k_hbm.at[:, cols], k_ref.at[r], sems.at[0, r]),
            pltpu.make_async_copy(v_hbm.at[:, cols], v_ref.at[r], sems.at[1, r]),
        )
        for copy in copies[r]:
            copy.start()
    sent = {1: one_ref, 2: two_ref, 3: three_ref}
    spot = {0: 0, 3: 1, 2: 2}
    for r in order:
        for copy in copies[r]:
            copy.wait()
        for j in range(group):
            state = tn(v_ref[r, :, column(j)], k_ref[r, :, column(j)])
            if r == 0:
                own_ref[j] = state
            else:
                sent[r][j] = state.astype(BF16)
            if r in spot:
                rest_ref[spot[r] * group + j] = state.astype(BF16)


def sums_kernel(own_ref, one_ref, two_ref, three_ref, sent_ref, *total_refs):
    total = own_ref[...] + one_ref[...].astype(F32) + two_ref[...].astype(F32) + three_ref[...].astype(F32)
    for total_ref in total_refs:
        total_ref[...] = total
    sent_ref[...] = total.astype(BF16)


def join_kernel(top_ref, left_ref, joined_ref):
    joined_ref[: top_ref.shape[0]] = top_ref[...]
    joined_ref[top_ref.shape[0] :] = left_ref[...]


def left_kernel(seq, place_ref, own_ref, one_ref, early2_ref, early3_ref, late2_ref, late3_ref, left_ref):
    last_quad = place_ref[0] >= seq - QUAD
    two = jnp.where(last_quad, late2_ref[...], early2_ref[...])
    three = jnp.where(last_quad, late3_ref[...], early3_ref[...])
    pair = own_ref[...] + one_ref[...].astype(F32)
    other = two.astype(F32) + three.astype(F32)
    left_ref[...] = jnp.where(place_ref[0] >> 1 & 1 == 1, other, pair).astype(BF16)


def intra_of(group, groups, place, q_ref, w_ref, k_all, v_all, out_refs):
    count = q_ref.shape[0] // STRETCH
    local_bits = count.bit_length() - 1
    causal = lax.broadcasted_iota(jnp.int32, (STRETCH, STRETCH), 0) <= lax.broadcasted_iota(
        jnp.int32, (STRETCH, STRETCH), 1
    )
    for r, out_ref in zip(groups, out_refs):
        for j in range(group):
            head = (place & (QUAD - 1) ^ r) * group + j
            cols = pl.ds(pl.multiple_of(head * HEAD_DIM, HEAD_DIM), HEAD_DIM)
            states = []
            for c in range(count):
                here = slice(c * STRETCH, (c + 1) * STRETCH)
                q, k, v = q_ref[here, cols], k_all[r, here, column(j)], v_all[r, here, column(j)]
                probs = jnp.where(causal, nt(k, q), 0.0).astype(BF16)
                total = w_ref[0, pl.ds(head, 1), here] * tn(v, probs)
                for bit in range(local_bits):
                    if c >> bit & 1:
                        low = (c >> bit + 1) << bit + 1
                        left = functools.reduce(jnp.add, states[low : low + (1 << bit)])
                        total += w_ref[1 + bit, pl.ds(head, 1), here] * nt(left.astype(BF16), q)
                out_ref[column(j), here] = total
                if c + 1 < count:
                    states.append(tn(v, k))


def lowest(place):
    return place < QUAD


def busy(place):
    return (place >= QUAD) & (place >> 1 & 1 == 1)


def intra_first_kernel(group, place_ref, *refs):
    gain_ref, kept_ref, out_ref = refs[4:]
    kept_ref[...] = gain_ref[...]

    @pl.when(busy(place_ref[0]))
    def _():
        intra_of(group, (3,), place_ref[0], *refs[:4], (out_ref,))


def intra_second_kernel(group, place_ref, *refs):
    @pl.when(lowest(place_ref[0]))
    def _():
        intra_of(group, range(QUAD), place_ref[0], *refs[:4], refs[4:])


def intra_last_kernel(group, place_ref, q_ref, w_ref, k_all, v_all, gain_ref, first_ref, *refs):
    args = (q_ref, w_ref, k_all, v_all)
    done_refs, column_ref, out_refs = refs[:QUAD], refs[QUAD], refs[QUAD + 1 :]
    for head in range(QUAD * group):
        rows = jnp.broadcast_to(gain_ref[:, column(head)], (HEAD_DIM, HEAD_DIM))
        column_ref[column(head), :] = jnp.transpose(rows, (1, 0))

    @pl.when(lowest(place_ref[0]))
    def _():
        for done_ref, out_ref in zip(done_refs, out_refs):
            out_ref[...] = done_ref[...]

    @pl.when(busy(place_ref[0]))
    def _():
        out_refs[3][...] = first_ref[...]
        intra_of(group, range(3), place_ref[0], *args, out_refs[:3])

    @pl.when(jnp.logical_not(lowest(place_ref[0]) | busy(place_ref[0])))
    def _():
        intra_of(group, range(QUAD), place_ref[0], *args, out_refs)


def readout_of(group, first, work, n_states, carry, finish, place_ref, q_ref, w_ref, *refs):
    n = len(work)
    state_refs, total_refs, refs = refs[:n_states], refs[n_states : n_states + n], refs[n_states + n :]
    carried_ref = refs[0] if carry else None
    out_refs, squares_ref = refs[carry : carry + n], refs[carry + n]
    rows = q_ref.shape[0]
    place = place_ref[0]
    for t in range(0, rows, TILE):
        here = slice(t, t + TILE)
        squares = carried_ref[:, here] if carry else jnp.zeros((8, TILE), F32)
        for (r, complete, reads), total_ref, out_ref in zip(work, total_refs, out_refs):
            for j in range(group):
                head = (place & (QUAD - 1) ^ r) * group + j
                q = q_ref[here, pl.ds(pl.multiple_of(head * HEAD_DIM, HEAD_DIM), HEAD_DIM)]
                total = total_ref[column(j), here]
                for bit, ref, slot in reads:
                    row = w_ref[first + bit, pl.ds(head, 1), here]
                    row = jnp.where(place >> bit & 1 == 1, row, 0.0)
                    total += row * nt(state_refs[ref][slot + j], q)
                out_ref[column(j), here] = total
                if complete:
                    squares += jnp.sum((total * total).reshape(HEAD_DIM // 8, 8, TILE), axis=0)
        squares_ref[:, here] = jnp.sum(squares, axis=0, keepdims=True) if finish else squares


def readout_kernel(group, first, work, lacks, *args):
    low = any(bit == 0 for _, _, reads in work for bit, _, _ in reads)
    fewer = tuple((r, complete, tuple(read for read in reads if low and read[0] >= 2)) for r, complete, reads in work)
    place = args[3][0]
    for present, some in ((True, work), (False, fewer)):
        pl.when(lacks(place) != present)(functools.partial(readout_of, group, first, some, *args))


def norm_kernel(group, full_width, place_ref, *refs):
    total_refs, share_refs, (gain_ref, out_hbm, buf, sems) = refs[:QUAD], refs[QUAD:-4], refs[-4:]
    place = place_ref[0] & (QUAD - 1)
    rows = buf.shape[0]
    scale = lax.rsqrt(functools.reduce(jnp.add, (ref[...] for ref in share_refs)) / full_width + EPSILON)
    copies = []
    for r in range(QUAD):
        for j in range(group):
            start = pl.multiple_of(((place ^ r) * group + j) * HEAD_DIM, HEAD_DIM)
            here = pl.ds(start, HEAD_DIM)
            gain = jnp.concatenate([gain_ref[here, :]] * (rows // HEAD_DIM), axis=1)
            x = (total_refs[r][column(j), :] * scale * gain).astype(BF16)
            spot = column(r * group + j)
            buf[:, spot] = jnp.transpose(x, (1, 0))
            copies.append(pltpu.make_async_copy(buf.at[:, spot], out_hbm.at[:, here], sems.at[r * group + j]))
            copies[-1].start()
    for copy in copies:
        copy.wait()


def local(queries, keys, values, level_weights, norm_gain):
    rows, width = queries.shape
    group = width // HEAD_DIM // QUAD
    local_bits = (rows // STRETCH).bit_length() - 1
    seq_bits = lax.axis_size("seq").bit_length() - 1
    full_width = width * lax.axis_size("head")
    position = lax.axis_index("seq").astype(jnp.int32)
    place = position.reshape(1)
    sds = jax.ShapeDtypeStruct
    block = (group, HEAD_DIM, HEAD_DIM)
    others = (3 * group, HEAD_DIM, HEAD_DIM)
    panel = (rows, group * HEAD_DIM)
    part_shape = sds((group * HEAD_DIM, rows), F32)

    k_all, v_all, own, one, two, three, rest = pl.pallas_call(
        functools.partial(states_kernel, group),
        out_shape=(sds((QUAD,) + panel, BF16),) * 2 + (sds(block, F32),) + (sds(block, BF16),) * 3 + (sds(others, BF16),),
        in_specs=[SMEM, HBM, HBM],
        out_specs=(VMEM,) * 7,
        scratch_shapes=[pltpu.SemaphoreType.DMA((2, QUAD))],
        compiler_params=params(STATES_GRANT),
        cost_estimate=cost(2 * rows * width * HEAD_DIM, 4 * rows * width),
        name="states",
    )(place, keys, values)

    early3 = exchanged_in(three, 3, lambda s, seq: s < seq - QUAD)
    taken1 = exchanged(one, "seq", 1)
    early2 = exchanged_in(two, 2, lambda s, seq: s < seq - QUAD)
    late3 = exchanged_in(three, 3, lambda s, seq: s >= seq - QUAD)
    late2 = exchanged_in(two, 2, lambda s, seq: s >= seq - QUAD)
    near = exchanged(rest, "seq", 1)

    args = (place, queries, level_weights, k_all, v_all)
    work_cost = cost(6 * rows * STRETCH * width, 4 * rows * width)
    gain, first = pl.pallas_call(
        functools.partial(intra_first_kernel, group),
        out_shape=(sds((1, width), F32), part_shape),
        in_specs=[SMEM] + [VMEM] * 5,
        out_specs=(VMEM,) * 2,
        compiler_params=params(),
        cost_estimate=work_cost,
        name="intra_first",
    )(*args, norm_gain.reshape(1, width))
    outs = pl.pallas_call(
        functools.partial(intra_second_kernel, group),
        out_shape=(part_shape,) * QUAD,
        in_specs=[SMEM] + [VMEM] * 4,
        out_specs=(VMEM,) * QUAD,
        compiler_params=params(),
        cost_estimate=work_cost,
        name="intra_second",
    )(*args)

    sums, *running = pl.pallas_call(
        sums_kernel,
        out_shape=(sds(block, BF16),) + (sds(block, F32),) * (seq_bits > 3),
        in_specs=[VMEM] * 4,
        out_specs=(VMEM,) * (1 + (seq_bits > 3)),
        compiler_params=params(),
        cost_estimate=cost(4 * group * HEAD_DIM**2, 16 * group * HEAD_DIM**2),
        name="sums",
    )(own, taken1, early2, early3)
    upper = []
    for bit in range(2, seq_bits):
        if bit > 2:
            running = [running[0] + upper[-1].astype(F32)]
            sums = running[0].astype(BF16)
        upper.append(exchanged(sums, "seq", 1 << bit))
    left_pair = pl.pallas_call(
        functools.partial(left_kernel, lax.axis_size("seq")),
        out_shape=sds(block, BF16),
        in_specs=[SMEM] + [VMEM] * 6,
        out_specs=VMEM,
        compiler_params=params(),
        cost_estimate=cost(4 * group * HEAD_DIM**2, 16 * group * HEAD_DIM**2),
        name="left",
    )(place, own, taken1, early2, early3, late2, late3)
    top = jnp.concatenate(upper, axis=0) if len(upper) > 1 else upper[0]
    tops = {r: exchanged_in(top, r, lambda s, seq: s >= QUAD) for r in (3, 2)}
    joined = pl.pallas_call(
        join_kernel,
        out_shape=sds((top.shape[0] + group,) + block[1:], BF16),
        in_specs=[VMEM] * 2,
        out_specs=VMEM,
        compiler_params=params(),
        cost_estimate=cost(0, 16 * group * HEAD_DIM**2),
        name="join",
    )(top, left_pair)
    tops[1] = exchanged_in(joined, 1, lambda s, seq: s >= 2)

    gain, *outs = pl.pallas_call(
        functools.partial(intra_last_kernel, group),
        out_shape=(sds((width, HEAD_DIM), F32),) + (part_shape,) * QUAD,
        in_specs=[SMEM] + [VMEM] * (6 + QUAD),
        out_specs=(VMEM,) * (1 + QUAD),
        compiler_params=params(),
        cost_estimate=work_cost,
        name="intra_last",
    )(*args, gain, first, *outs)
    totals = dict(enumerate(outs))

    middle = {0: left_pair} | {r: exchanged(left_pair, "seq", r) for r in (3, 2)}

    def top_reads(ref):
        return tuple((bit, ref, (bit - 2) * group) for bit in range(2, seq_bits))

    def readout(label, work, states, squares, finish=False):
        n, carry = len(work), squares is not None

        def lacks(place):
            return {"far": place & (QUAD - 1) == 0, "mid": place < 2, "last": place < QUAD}[label]

        kernel = functools.partial(readout_kernel, group, 1 + local_bits, work, lacks, len(states), carry, finish)
        ins = [place, queries, level_weights, *states, *(totals[r] for r, _, _ in work)] + [squares] * carry
        shapes = [part_shape] * n + [sds((1 if finish else 8, rows), F32)]
        outs = pl.pallas_call(
            kernel,
            out_shape=tuple(shapes),
            in_specs=[SMEM] + [VMEM] * (len(ins) - 1),
            out_specs=(VMEM,) * len(shapes),
            compiler_params=params(),
            cost_estimate=cost(n * rows * width * HEAD_DIM, 2 * n * rows * width),
        )(*ins)
        totals.update({r: out for (r, _, _), out in zip(work, outs)})
        return outs[n]

    below = {0: ((0, 0, 0), (1, 2, 0)), 1: ((0, 1, 0),)}
    below |= {r: ((0, 1, (r - 1) * group), (1, 1 + r, 0)) for r in (2, 3)}
    work = tuple((r, r == 0, below[r] + (top_reads(5) if r == 0 else ())) for r in (3, 1, 2, 0))
    squares = readout("far", work, (taken1, near, middle[0], middle[2], middle[3], top), None)
    work = (3, True, top_reads(0)), (1, True, ((1, 1, top.shape[0]), *top_reads(1)))
    squares = readout("mid", work, (tops[3], tops[1]), squares)
    squares = readout("last", ((2, True, top_reads(0)),), (tops[2],), squares, finish=True)

    shares = [squares] + [exchanged(squares, "head", mask) for mask in range(1, lax.axis_size("head"))]

    return pl.pallas_call(
        functools.partial(norm_kernel, group, full_width),
        out_shape=sds((rows, width), BF16),
        in_specs=[SMEM] + [VMEM] * (QUAD + len(shares) + 1),
        out_specs=ANY,
        scratch_shapes=[pltpu.VMEM((rows, width), BF16), pltpu.SemaphoreType.DMA((QUAD * group,))],
        compiler_params=params(),
        cost_estimate=cost(2 * rows * width, 2 * rows * width),
        name="norm",
    )(place, *(totals[r] for r in range(QUAD)), *shares, gain)


def solution(mesh):
    return jax.shard_map(
        local,
        mesh=mesh,
        in_specs=(P("seq", "head"), P("seq", "head"), P("seq", "head"), P(None, "head", "seq"), P("head")),
        out_specs=P("seq", "head"),
        check_vma=False,
    )
```
